256 devices in a mesh: seq: 64 (over x, z, core), head: 4 (over y).
Axes of the slice: x: 4, y: 4, z: 8, core: 2. Of those that a mesh axis runs over, the one named last changes fastest.
Arguments:
- tokens: bfloat16 [65536, 2048], P('seq', 'head'), may hold values from -6 to 6
- w_qkv: bfloat16 [2048, 6144], P(None, 'head'), may hold values from -1 to 1
- item_at: int32 [4, 2048], P('head'), may hold values from 0 to 2047, as said below
- rand_cols: int32 [16, 512, 4], P('head'), may hold values from 0 to 511, as said below
- rand_used: int32 [16, 512], P('head'), may hold values from 0 to 4, as said below
Outputs:
- attended: bfloat16 [4, 2048, 128, 128], P('head', 'seq')
The draws below stay inside these ranges and needn't reach their ends.
Inputs may be any that keep to these rules, and one draw needn't show every extreme that they name: In head group g, item e * 512 + r stands for head g * 4 + e at block row r, and every item appears exactly once in item_at[g]. Positions j * 32 to (j + 1) * 32 - 1 hold the items placed at device j of seq. Of the items whose block rows lie on one device of seq, at most 1 of one group are placed at any one device, and exactly 1 at some. `rand_cols`: take all 128 candidates (used or not) of the items placed at one device in one head group, or of the items of one group whose block rows lie on one device: at most 2 of them lie in the block rows of any one device of seq, and exactly 2 in some. A candidate may equal a window block or block 0. `rand_used`: in each head group the counts of the 32 items placed at one device sum to exactly 64; the sums over the items whose block rows lie on one device vary.
All inputs are finite; a program needn't handle non-finite values.
Results may differ from the reference program's by a relative error of at most 0.019.
Values may be sent and summed in bfloat16 or wider, within the bound.
No kernel may reach another device: no remote copies, remote signals or barrier semaphores. Data moves between devices by JAX's collectives and lax.ppermute only.
A program may use at most 128 MiB of HBM per device.

```python
import math
import jax
import jax.numpy as jnp
from jax import lax

D = 2048
H = 16
HD = 128
BLK = 128
RAND = 4
HPD = 4
TOKENS = 65536
NB = 512
RB = 8
ITEMS = 32


def routing_tables(key):
    groups = H // HPD
    seq_count = NB // RB

    def one_group(group_key):
        key_perm, key_delta, key_order, key_source, key_row, key_base, key_shift = jax.random.split(group_key, 7)
        perm = jax.random.permutation(key_perm, seq_count).astype(jnp.int32)
        inverse = jnp.zeros((seq_count,), jnp.int32).at[perm].set(jnp.arange(seq_count, dtype=jnp.int32))
        delta = (jax.random.permutation(key_delta, ITEMS) % seq_count).astype(jnp.int32)
        homes = perm[(inverse[:, None] - delta[None, :]) % seq_count]
        source_perm = jax.random.permutation(key_source, seq_count).astype(jnp.int32)
        slot_ids = jnp.arange(RAND, dtype=jnp.int32)
        sources = source_perm[(delta[:, None] + slot_ids[None, :] * ITEMS) % seq_count]
        within = jax.random.randint(key_row, (seq_count, ITEMS, RAND), 0, RB).astype(jnp.int32)
        columns = sources[None, :, :] * RB + within
        base = jax.random.randint(key_base, (ITEMS // 2,), 0, RAND + 1).astype(jnp.int32)
        pattern = jnp.concatenate([base, RAND - base])
        shifts = jax.random.randint(key_shift, (seq_count,), 0, ITEMS).astype(jnp.int32)
        local_ids = jnp.arange(ITEMS, dtype=jnp.int32)
        counts = pattern[(local_ids[None, :] + shifts[:, None]) % ITEMS]
        heads_full = jnp.broadcast_to((local_ids // RB)[None, :], (seq_count, ITEMS))
        rows_full = homes * RB + (local_ids % RB)[None, :]
        order = jax.vmap(lambda one_key: jax.random.permutation(one_key, ITEMS))(jax.random.split(key_order, seq_count)).astype(jnp.int32)
        item_ids = jnp.take_along_axis(heads_full * NB + rows_full, order, axis=1)
        rand_table = jnp.zeros((HPD, NB, RAND), jnp.int32)
        rand_table = rand_table.at[heads_full.reshape(-1), rows_full.reshape(-1)].set(columns.reshape(-1, RAND))
        used_table = jnp.zeros((HPD, NB), jnp.int32)
        used_table = used_table.at[heads_full.reshape(-1), rows_full.reshape(-1)].set(counts.reshape(-1))
        return (item_ids.reshape(-1), rand_table, used_table)
    item_table, rand_table, used_table = jax.vmap(one_group)(jax.random.split(jax.random.fold_in(key, 7), groups))
    return (item_table, rand_table.reshape(H, NB, RAND), used_table.reshape(H, NB))


def draw_item_at(key, part):
    return routing_tables(key)[0]


def draw_rand_cols(key, part):
    return routing_tables(key)[1]


def draw_rand_used(key, part):
    return routing_tables(key)[2]


def draw_tokens(key, part):
    drawn_key = jax.random.fold_in(key, 0)
    result = jnp.clip(jax.random.normal(drawn_key, (TOKENS, D), jnp.float32), -6.0, 6.0)
    return result.astype(jnp.bfloat16)


def draw_w_qkv(key, part):
    first_key = jax.random.fold_in(key, 0)
    shaped = jnp.clip(jax.random.normal(first_key, (D, H // HPD, 3, HPD, HD), jnp.float32), -6.0, 6.0) / math.sqrt(D)
    return shaped.reshape(D, 3 * H * HD).astype(jnp.bfloat16)


def setup_inputs(seed: int = 0) -> dict:
    streams_of = jax.random.split(jax.random.key(seed), 6)
    tokens = draw_tokens(jax.random.fold_in(streams_of[5], 71), 0)
    w_qkv = draw_w_qkv(jax.random.fold_in(streams_of[5], 71), 0)
    item_at = draw_item_at(jax.random.fold_in(streams_of[5], 71), 0)
    rand_cols = draw_rand_cols(jax.random.fold_in(streams_of[5], 71), 0)
    rand_used = draw_rand_used(jax.random.fold_in(streams_of[5], 71), 0)
    return {"tokens": tokens, "w_qkv": w_qkv, "item_at": item_at, "rand_cols": rand_cols, "rand_used": rand_used}


neg_large = -1.0e30


def attend(queries, key_tiles, value_tiles, usable, factor):
    scores = jnp.einsum("ibe,ijke->ibjk", queries.astype(jnp.float32), key_tiles.astype(jnp.float32)) * factor
    scores = jnp.where(usable[:, None, :, None], scores, neg_large)
    row_max = jnp.max(scores, axis=(2, 3))
    expo = jnp.exp(scores - row_max[:, :, None, None])
    row_sum = jnp.sum(expo, axis=(2, 3))
    weights = expo.astype(jnp.bfloat16)
    summed = jnp.einsum("ibjk,ijke->ibe", weights.astype(jnp.float32), value_tiles.astype(jnp.float32))
    return summed, row_max, row_sum


def reference(tokens, w_qkv, item_at, rand_cols, rand_used):
    groups = H // HPD
    group_weights = w_qkv.reshape(D, groups, 3 * HPD * HD).transpose(1, 0, 2)

    def project(weight_part):
        return jnp.dot(tokens, weight_part, preferred_element_type=jnp.float32).astype(jnp.bfloat16)

    projected = lax.map(project, group_weights)
    projected = projected.reshape(groups, NB, BLK, 3, HPD, HD).transpose(0, 4, 3, 1, 2, 5)
    projected = projected.reshape(H, 3, NB, BLK, HD)
    block_ids = jnp.arange(NB, dtype=jnp.int32)
    slot_ids = jnp.arange(RAND, dtype=jnp.int32)
    factor = HD ** -0.5

    def one_head(inputs):
        head_tiles, randoms, counts = inputs
        columns = jnp.concatenate([(block_ids - 1)[:, None], block_ids[:, None], (block_ids + 1)[:, None],
                                   jnp.zeros((NB, 1), jnp.int32), randoms], axis=1)
        usable = jnp.concatenate([(block_ids >= 1)[:, None], jnp.ones((NB, 1), bool),
                                  (block_ids + 1 < NB)[:, None], jnp.ones((NB, 1), bool),
                                  slot_ids[None, :] < counts[:, None]], axis=1)
        clipped = jnp.clip(columns, 0, NB - 1)
        key_tiles = head_tiles[1][clipped]
        value_tiles = head_tiles[2][clipped]
        summed, row_max, row_sum = attend(head_tiles[0], key_tiles, value_tiles, usable, factor)
        return (summed / row_sum[:, :, None]).astype(jnp.bfloat16)

    heads_out = lax.map(one_head, (projected, rand_cols, rand_used))
    grouped = heads_out.reshape(groups, HPD * NB, BLK, HD)
    return jax.vmap(lambda table, picks: table[picks])(grouped, item_at)
```

```python
import math

import jax
import jax.numpy as jnp
from jax import lax
from jax.experimental import pallas as pl
from jax.experimental.pallas import tpu as pltpu
from jax.sharding import PartitionSpec as P

NEG = -1e30
BF = jnp.bfloat16
F32 = jnp.float32
VMEM_BYTES = 48 << 20


def dot_t(a, b):
    return lax.dot_general(a, b, (((1,), (1,)), ((), ())), preferred_element_type=F32)


def pack_tiles(index, proj, slots, rows, heads, blk, hd):
    step = 8

    def kernel(index_ref, k_ref, v_ref, out_ref):
        first = pl.program_id(0) * step
        for j in range(step):
            tile = index_ref[first + j]
            row = pl.ds(pl.multiple_of((tile % rows) * blk, blk), blk)
            col = pl.ds(pl.multiple_of((tile // rows) * hd, hd), hd)
            out_ref[j, 0] = k_ref[row, col]
            out_ref[j, 1] = v_ref[row, col]

    tokens, width = proj.shape[0], heads * hd
    return pl.pallas_call(
        kernel,
        out_shape=jax.ShapeDtypeStruct((slots, 2, blk, hd), BF),
        grid_spec=pltpu.PrefetchScalarGridSpec(
            num_scalar_prefetch=1,
            grid=(slots // step,),
            in_specs=[
                pl.BlockSpec((tokens, width), lambda i, s: (0, 1)),
                pl.BlockSpec((tokens, width), lambda i, s: (0, 2)),
            ],
            out_specs=pl.BlockSpec((step, 2, blk, hd), lambda i, s: (i, 0, 0, 0)),
        ),
        compiler_params=pltpu.CompilerParams(vmem_limit_bytes=VMEM_BYTES),
        name="pack_tiles",
    )(index, proj, proj)


def near_attend(edges, proj, around, first, rows, heads, blk, hd, factor):
    width = heads * hd

    def kernel(edge_ref, q_ref, kv_ref, first_ref, acc_ref, stat_ref):
        r = pl.program_id(0)
        window = pl.ds(pl.multiple_of(r * blk, blk), 3 * blk)
        lane = lax.broadcasted_iota(jnp.int32, (blk, 3 * blk), 1)
        low = jnp.where((r == 0) & (edge_ref[0] == 1), blk, 0)
        high = jnp.where((r == rows - 1) & (edge_ref[1] == 1), 2 * blk, 3 * blk)
        usable = (lane >= low) & (lane < high)
        half = lax.broadcasted_iota(jnp.int32, (blk, hd), 1) < hd // 2
        for e in range(heads):
            cols = slice(e * hd, (e + 1) * hd)
            vcols = slice(width + e * hd, width + (e + 1) * hd)
            q = q_ref[:, cols]
            near = jnp.where(usable, dot_t(q, kv_ref[window, cols]) * factor, NEG)
            glob = dot_t(q, first_ref[:, cols]) * factor
            top = jnp.maximum(
                jnp.max(near, axis=1, keepdims=True), jnp.max(glob, axis=1, keepdims=True)
            )
            near = jnp.exp(near - top)
            glob = jnp.exp(glob - top)
            total = jnp.sum(near, axis=1, keepdims=True) + jnp.sum(glob, axis=1, keepdims=True)
            acc_ref[e] = jnp.dot(
                near.astype(BF), kv_ref[window, vcols], preferred_element_type=F32
            ) + jnp.dot(glob.astype(BF), first_ref[:, vcols], preferred_element_type=F32)
            stat_ref[e] = jnp.where(half, top, total)

    out = jax.ShapeDtypeStruct((rows * heads, blk, hd), F32)
    return pl.pallas_call(
        kernel,
        out_shape=(out, out),
        grid_spec=pltpu.PrefetchScalarGridSpec(
            num_scalar_prefetch=1,
            grid=(rows,),
            in_specs=[
                pl.BlockSpec((blk, width), lambda r, s: (r, 0)),
                pl.BlockSpec(around.shape, lambda r, s: (0, 0)),
                pl.BlockSpec(first.shape, lambda r, s: (0, 0)),
            ],
            out_specs=(
                pl.BlockSpec((heads, blk, hd), lambda r, s: (r, 0, 0)),
                pl.BlockSpec((heads, blk, hd), lambda r, s: (r, 0, 0)),
            ),
        ),
        compiler_params=pltpu.CompilerParams(vmem_limit_bytes=VMEM_BYTES),
        name="near_attend",
    )(edges, proj, around, first)


def rand_attend(slot, count, target, proj, tiles, acc, stat, rows, heads, blk, hd, rand, peers, factor):
    items = rows * heads

    def kernel(slot_ref, count_ref, target_ref, q_ref, *refs):
        kv = refs[:rand]
        acc_ref, stat_ref, out_ref = refs[rand:]
        used = count_ref[pl.program_id(0)]
        q = q_ref[...]
        stats = stat_ref[0]
        top0, total0 = stats[:, 0:1], stats[:, hd // 2 : hd // 2 + 1]
        scores = [
            jnp.where(j < used, dot_t(q, kv[j][0, 0]) * factor, NEG) for j in range(rand)
        ]
        best = scores[0]
        for s in scores[1:]:
            best = jnp.maximum(best, s)
        top = jnp.maximum(jnp.max(best, axis=1, keepdims=True), top0)
        keep = jnp.exp(top0 - top)
        summed = acc_ref[0] * keep
        sums = None
        for j in range(rand):
            w = jnp.exp(scores[j] - top)
            sums = w if sums is None else sums + w
            summed += jnp.dot(w.astype(BF), kv[j][0, 1], preferred_element_type=F32)
        total = total0 * keep + jnp.sum(sums, axis=1, keepdims=True)
        out_ref[0] = (summed / total).astype(BF)

    def tile_spec(j):
        return pl.BlockSpec((1, 2, blk, hd), lambda i, s, c, t: (s[i * rand + j], 0, 0, 0))

    return pl.pallas_call(
        kernel,
        out_shape=jax.ShapeDtypeStruct((peers, blk, hd), BF),
        grid_spec=pltpu.PrefetchScalarGridSpec(
            num_scalar_prefetch=3,
            grid=(items,),
            in_specs=[
                pl.BlockSpec((blk, hd), lambda i, s, c, t: (i // heads, i % heads)),
                *[tile_spec(j) for j in range(rand)],
                pl.BlockSpec((1, blk, hd), lambda i, s, c, t: (i, 0, 0)),
                pl.BlockSpec((1, blk, hd), lambda i, s, c, t: (i, 0, 0)),
            ],
            out_specs=pl.BlockSpec((1, blk, hd), lambda i, s, c, t: (t[i], 0, 0)),
        ),
        compiler_params=pltpu.CompilerParams(vmem_limit_bytes=VMEM_BYTES),
        name="rand_attend",
    )(slot, count, target, proj, *[tiles] * rand, acc, stat)


def take_tiles(index, tiles):
    count = index.shape[0]

    def kernel(index_ref, in_ref, out_ref, sems):
        copies = [
            pltpu.make_async_copy(in_ref.at[index_ref[i]], out_ref.at[i], sems.at[i])
            for i in range(count)
        ]
        for copy in copies:
            copy.start()
        for copy in copies:
            copy.wait()

    return pl.pallas_call(
        kernel,
        out_shape=jax.ShapeDtypeStruct((count, *tiles.shape[1:]), tiles.dtype),
        grid_spec=pltpu.PrefetchScalarGridSpec(
            num_scalar_prefetch=1,
            grid=(1,),
            in_specs=[pl.BlockSpec(memory_space=pl.ANY)],
            out_specs=pl.BlockSpec(memory_space=pl.ANY),
            scratch_shapes=[pltpu.SemaphoreType.DMA((count,))],
        ),
        name="take_tiles",
    )(index, tiles)


def local(tokens, w_qkv, item_at, rand_cols, rand_used):
    peers = lax.axis_size("seq")
    me = lax.axis_index("seq")
    heads, nblocks, rand = rand_cols.shape
    rows = nblocks // peers
    blk = tokens.shape[0] // rows
    hd = w_qkv.shape[1] // (3 * heads)
    width = heads * hd
    items = heads * rows
    factor = 1.0 / math.sqrt(hd)

    asked = rand_cols.reshape(heads, peers, rows, rand).transpose(1, 2, 0, 3)
    asked = asked.reshape(peers, items * rand)
    head_of = (jnp.arange(items * rand, dtype=jnp.int32) // rand) % heads
    order = jnp.arange(items * rand, dtype=jnp.int32)
    code = order * items + head_of * rows + asked % rows
    mine = asked // rows == me
    low = jnp.min(jnp.where(mine, code, jnp.int32(1 << 30)), axis=1) % items
    high = jnp.max(jnp.where(mine, code, 0), axis=1) % items
    send_tile = jnp.stack([low, high], axis=1).reshape(-1)
    wanted = lax.dynamic_index_in_dim(asked, me, 0, keepdims=False)
    source = wanted // rows
    again = jnp.sum(
        ((source[:, None] == source[None, :]) & (order[None, :] < order[:, None])).astype(jnp.int32),
        axis=1,
    )
    slot = source * 2 + again
    my_used = lax.dynamic_slice_in_dim(rand_used, me * rows, rows, axis=1).T.reshape(-1)
    number = jnp.arange(items, dtype=jnp.int32)
    my_item = (number % heads) * nblocks + me * rows + number // heads
    place = jnp.arange(peers * items, dtype=jnp.int32)
    target = jnp.sum(
        jnp.where(item_at[0][None, :] == my_item[:, None], place[None, :] // items, 0), axis=1
    )
    home = (lax.dynamic_slice_in_dim(item_at[0], me * items, items) % nblocks) // rows
    edges = jnp.stack([me == 0, me == peers - 1]).astype(jnp.int32)

    proj = jnp.dot(
        lax.all_gather(tokens, "head", axis=1, tiled=True), w_qkv, preferred_element_type=F32
    ).astype(BF)
    sent = pack_tiles(send_tile, proj, 2 * peers, rows, heads, blk, hd)
    up = [(i, i + 1) for i in range(peers - 1)]
    down = [(b, a) for a, b in up]
    pair = proj[:, width:]
    before = lax.ppermute(pair[-blk:], "seq", up)
    after = lax.ppermute(pair[:blk], "seq", down)
    first = pair[:blk]
    first = lax.psum(jnp.where(me == 0, first, jnp.zeros_like(first)), "seq")
    around = jnp.concatenate([before, pair, after], axis=0)

    tiles = lax.all_to_all(sent, "seq", split_axis=0, concat_axis=0, tiled=True)
    acc, stat = near_attend(edges, proj, around, first, rows, heads, blk, hd, factor)
    done = rand_attend(
        slot, my_used, target, proj, tiles, acc, stat, rows, heads, blk, hd, rand, peers, factor
    )
    back = lax.all_to_all(done, "seq", split_axis=0, concat_axis=0, tiled=True)
    return take_tiles(home, back)[None]


def solution(mesh):
    return jax.shard_map(
        local,
        mesh=mesh,
        in_specs=(
            P("seq", "head"),
            P(None, "head"),
            P("head", None),
            P("head", None, None),
            P("head", None),
        ),
        out_specs=P("head", "seq", None, None),
        check_vma=False,
    )
```

```python
import math

import jax
import jax.numpy as jnp
from jax import lax
from jax.experimental import pallas as pl
from jax.experimental.pallas import tpu as pltpu
from jax.sharding import PartitionSpec as P

NEG = -1e30
BF = jnp.bfloat16
F32 = jnp.float32
VMEM_BYTES = 48 << 20


def dot(a, b):
    return jnp.dot(a, b, preferred_element_type=F32)


def dot_t(a, b):
    return lax.dot_general(a, b, (((1,), (1,)), ((), ())), preferred_element_type=F32)


def params():
    return pltpu.CompilerParams(vmem_limit_bytes=VMEM_BYTES)


def pack_tiles(index, pair, slots, rows, blk, wide):
    def kernel(index_ref, pair_ref, out_ref, sems):
        def copy(s):
            tile = index_ref[s]
            row = pl.ds(pl.multiple_of((tile % rows) * blk, blk), blk)
            col = pl.ds(pl.multiple_of((tile // rows) * wide, wide), wide)
            return pltpu.make_async_copy(pair_ref.at[row, col], out_ref.at[s], sems.at[s])

        for s in range(slots):
            copy(s).start()
        for s in range(slots):
            copy(s).wait()

    return pl.pallas_call(
        kernel,
        out_shape=jax.ShapeDtypeStruct((slots, blk, wide), BF),
        grid_spec=pltpu.PrefetchScalarGridSpec(
            num_scalar_prefetch=1,
            grid=(1,),
            in_specs=[pl.BlockSpec(memory_space=pltpu.VMEM)],
            out_specs=pl.BlockSpec(memory_space=pl.ANY),
            scratch_shapes=[pltpu.SemaphoreType.DMA((slots,))],
        ),
        compiler_params=params(),
        name="pack_tiles",
    )(index, pair)


def take_tiles(index, tiles):
    count = index.shape[0]

    def kernel(index_ref, in_ref, out_ref, sems):
        def copy(i):
            return pltpu.make_async_copy(in_ref.at[index_ref[i]], out_ref.at[i], sems.at[i])

        for i in range(count):
            copy(i).start()
        for i in range(count):
            copy(i).wait()

    return pl.pallas_call(
        kernel,
        out_shape=jax.ShapeDtypeStruct((count, *tiles.shape[1:]), tiles.dtype),
        grid_spec=pltpu.PrefetchScalarGridSpec(
            num_scalar_prefetch=1,
            grid=(1,),
            in_specs=[pl.BlockSpec(memory_space=pltpu.VMEM)],
            out_specs=pl.BlockSpec(memory_space=pl.ANY),
            scratch_shapes=[pltpu.SemaphoreType.DMA((count,))],
        ),
        compiler_params=params(),
        name="take_tiles",
    )(index, tiles)


def near_attend(edges, query, around, first, rows, heads, blk, hd, factor):
    def kernel(edge_ref, q_ref, kv_ref, first_ref, acc_ref, stat_ref):
        r = pl.program_id(0)
        window = pl.ds(pl.multiple_of(r * blk, blk), 3 * blk)
        lane = lax.broadcasted_iota(jnp.int32, (blk, 3 * blk), 1)
        low = jnp.where((r == 0) & (edge_ref[0] == 1), blk, 0)
        high = jnp.where((r == rows - 1) & (edge_ref[1] == 1), 2 * blk, 3 * blk)
        usable = (lane >= low) & (lane < high)
        half = lax.broadcasted_iota(jnp.int32, (blk, hd), 1) < hd // 2
        for e in range(heads):
            keys = slice(2 * e * hd, (2 * e + 1) * hd)
            values = slice((2 * e + 1) * hd, (2 * e + 2) * hd)
            q = q_ref[:, e * hd : (e + 1) * hd]
            near = jnp.where(usable, dot_t(q, kv_ref[window, keys]) * factor, NEG)
            glob = dot_t(q, first_ref[:, keys]) * factor
            top = jnp.maximum(
                jnp.max(near, axis=1, keepdims=True), jnp.max(glob, axis=1, keepdims=True)
            )
            near = jnp.exp2(near - top)
            glob = jnp.exp2(glob - top)
            total = jnp.sum(near, axis=1, keepdims=True) + jnp.sum(glob, axis=1, keepdims=True)
            acc_ref[e] = dot(near.astype(BF), kv_ref[window, values]) + dot(
                glob.astype(BF), first_ref[:, values]
            )
            stat_ref[e] = jnp.where(half, top, total)

    out = jax.ShapeDtypeStruct((rows * heads, blk, hd), F32)
    return pl.pallas_call(
        kernel,
        out_shape=(out, out),
        grid_spec=pltpu.PrefetchScalarGridSpec(
            num_scalar_prefetch=1,
            grid=(rows,),
            in_specs=[
                pl.BlockSpec((blk, heads * hd), lambda r, s: (r, 0)),
                pl.BlockSpec(around.shape, lambda r, s: (0, 0)),
                pl.BlockSpec(first.shape, lambda r, s: (0, 0)),
            ],
            out_specs=(
                pl.BlockSpec((heads, blk, hd), lambda r, s: (r, 0, 0)),
                pl.BlockSpec((heads, blk, hd), lambda r, s: (r, 0, 0)),
            ),
        ),
        compiler_params=params(),
        name="near_attend",
    )(edges, query, around, first)


def rand_attend(slot, count, target, query, tiles, acc, stat, rows, heads, blk, hd, rand, peers, factor):
    items = rows * heads
    parts = heads * rand

    def kernel(slot_ref, count_ref, target_ref, q_ref, *refs):
        kv = refs[:parts]
        acc_ref, stat_ref, out_ref, done_ref, sems = refs[parts:]
        r = pl.program_id(0)
        for e in range(heads):
            used = count_ref[r * heads + e]
            q = q_ref[:, e * hd : (e + 1) * hd]
            top0 = stat_ref[e, :, 0:1]
            total0 = stat_ref[e, :, hd // 2 : hd // 2 + 1]
            scores = [
                jnp.where(j < used, dot_t(q, kv[e * rand + j][0, :, :hd]) * factor, NEG)
                for j in range(rand)
            ]
            best = scores[0]
            for s in scores[1:]:
                best = jnp.maximum(best, s)
            top = jnp.maximum(jnp.max(best, axis=1, keepdims=True), top0)
            keep = jnp.exp2(top0 - top)
            summed = acc_ref[e] * keep
            sums = None
            for j in range(rand):
                w = jnp.exp2(scores[j] - top)
                sums = w if sums is None else sums + w
                summed += dot(w.astype(BF), kv[e * rand + j][0, :, hd:])
            total = total0 * keep + jnp.sum(sums, axis=1, keepdims=True)
            i = r * heads + e
            done_ref[i] = (summed / total).astype(BF)
            pltpu.make_async_copy(
                done_ref.at[i], out_ref.at[target_ref[i]], sems.at[i]
            ).start()

        @pl.when(r == rows - 1)
        def _():
            for i in range(items):
                pltpu.make_async_copy(
                    done_ref.at[i], out_ref.at[target_ref[i]], sems.at[i]
                ).wait()

    def tile_spec(n):
        return pl.BlockSpec((1, blk, 2 * hd), lambda r, s, c, t: (s[r * parts + n], 0, 0))

    return pl.pallas_call(
        kernel,
        out_shape=jax.ShapeDtypeStruct((peers, blk, hd), BF),
        grid_spec=pltpu.PrefetchScalarGridSpec(
            num_scalar_prefetch=3,
            grid=(rows,),
            in_specs=[
                pl.BlockSpec((blk, heads * hd), lambda r, s, c, t: (r, 0)),
                *[tile_spec(n) for n in range(parts)],
                pl.BlockSpec((heads, blk, hd), lambda r, s, c, t: (r, 0, 0)),
                pl.BlockSpec((heads, blk, hd), lambda r, s, c, t: (r, 0, 0)),
            ],
            out_specs=pl.BlockSpec(memory_space=pl.ANY),
            scratch_shapes=[pltpu.VMEM((items, blk, hd), BF), pltpu.SemaphoreType.DMA((items,))],
        ),
        compiler_params=params(),
        name="rand_attend",
    )(slot, count, target, query, *[tiles] * parts, acc, stat)


def local(tokens, w_qkv, item_at, rand_cols, rand_used):
    peers = lax.axis_size("seq")
    me = lax.axis_index("seq")
    groups = lax.axis_size("head")
    mine_y = lax.axis_index("head")
    heads, nblocks, rand = rand_cols.shape
    rows = nblocks // peers
    count, depth = tokens.shape
    blk = count // rows
    hd = w_qkv.shape[1] // (3 * heads)
    width = heads * hd
    items = heads * rows
    factor = math.log2(math.e) / math.sqrt(hd)

    first_part = tokens[:blk]
    first_part = lax.psum(jnp.where(me == 0, first_part, jnp.zeros_like(first_part)), "seq")
    first_all = lax.all_gather(first_part, "head", axis=1, tiled=True)

    asked = rand_cols.reshape(heads, peers, rows, rand).transpose(1, 2, 0, 3)
    asked = asked.reshape(peers, items * rand)
    order = jnp.arange(items * rand, dtype=jnp.int32)
    head_of = (order // rand) % heads
    code = order * items + head_of * rows + asked % rows
    mine = asked // rows == me
    low = jnp.min(jnp.where(mine, code, jnp.int32(1 << 30)), axis=1) % items
    high = jnp.max(jnp.where(mine, code, 0), axis=1) % items
    send_tile = jnp.stack([low, high], axis=1).reshape(-1)
    wanted = lax.dynamic_index_in_dim(asked, me, 0, keepdims=False)
    source = wanted // rows
    again = jnp.sum(
        ((source[:, None] == source[None, :]) & (order[None, :] < order[:, None])).astype(jnp.int32),
        axis=1,
    )
    slot = source * 2 + again
    my_used = lax.dynamic_slice_in_dim(rand_used, me * rows, rows, axis=1).T.reshape(-1)
    number = jnp.arange(items, dtype=jnp.int32)
    my_item = (number % heads) * nblocks + me * rows + number // heads
    place = jnp.arange(peers * items, dtype=jnp.int32)
    target = jnp.sum(
        jnp.where(item_at[0][None, :] == my_item[:, None], place[None, :] // items, 0), axis=1
    )
    home = (lax.dynamic_slice_in_dim(item_at[0], me * items, items) % nblocks) // rows
    edges = jnp.stack([me == 0, me == peers - 1]).astype(jnp.int32)

    w_query = w_qkv[:, :width]
    w_pair = w_qkv[:, width:].reshape(-1, 2, heads, hd).transpose(0, 2, 1, 3).reshape(-1, 2 * width)

    def weight(table, shift):
        return lax.dynamic_slice_in_dim(table, (mine_y + shift) % groups * depth, depth, axis=0)

    onward = [(i, (i + 1) % groups) for i in range(groups)]
    backward = [(b, a) for a, b in onward]
    middle = count // 2
    from_low = lax.ppermute(tokens, "head", onward)
    from_high = lax.ppermute(tokens, "head", backward)
    far_top = lax.ppermute(from_low[:middle], "head", onward)
    far_bottom = lax.ppermute(from_high[middle:], "head", backward)

    total = dot(tokens, weight(w_pair, 0))
    total += dot(from_low, weight(w_pair, 3))
    total += dot(from_high, weight(w_pair, 1))
    w_far = weight(w_pair, 2)
    pair = jnp.concatenate(
        [
            (total[:middle] + dot(far_top, w_far)).astype(BF),
            (total[middle:] + dot(far_bottom, w_far)).astype(BF),
        ],
        axis=0,
    )
    sent = pack_tiles(send_tile, pair, 2 * peers, rows, blk, 2 * hd)
    up = [(i, i + 1) for i in range(peers - 1)]
    down = [(b, a) for a, b in up]
    before = lax.ppermute(pair[-blk:], "seq", up)
    after = lax.ppermute(pair[:blk], "seq", down)
    sent, before, after, first_all, far_top, far_bottom = lax.optimization_barrier(
        (sent, before, after, first_all, far_top, far_bottom)
    )
    tiles = lax.all_to_all(sent, "seq", split_axis=0, concat_axis=0, tiled=True)

    around = jnp.concatenate([before, pair, after], axis=0)
    first = dot(first_all, w_pair).astype(BF)
    far = jnp.concatenate([far_top, far_bottom], axis=0)
    query = dot(tokens, weight(w_query, 0)) + dot(from_low, weight(w_query, 3))
    query = query + dot(from_high, weight(w_query, 1)) + dot(far, weight(w_query, 2))
    query = query.astype(BF)
    acc, stat = near_attend(edges, query, around, first, rows, heads, blk, hd, factor)
    done = rand_attend(
        slot, my_used, target, query, tiles, acc, stat, rows, heads, blk, hd, rand, peers, factor
    )
    back = lax.all_to_all(done, "seq", split_axis=0, concat_axis=0, tiled=True)
    return take_tiles(home, back)[None]


def solution(mesh):
    return jax.shard_map(
        local,
        mesh=mesh,
        in_specs=(
            P("seq", "head"),
            P(None, "head"),
            P("head", None),
            P("head", None, None),
            P("head", None),
        ),
        out_specs=P("head", "seq", None, None),
        check_vma=False,
    )
```

```python
import math

import jax
import jax.numpy as jnp
from jax import lax
from jax.experimental import pallas as pl
from jax.experimental.pallas import tpu as pltpu
from jax.sharding import PartitionSpec as P

NEG = -1e30
BF = jnp.bfloat16
F32 = jnp.float32
VMEM_BYTES = 48 << 20


def dot(a, b):
    return jnp.dot(a, b, preferred_element_type=F32)


def dot_t(a, b):
    return lax.dot_general(a, b, (((1,), (1,)), ((), ())), preferred_element_type=F32)


def params():
    return pltpu.CompilerParams(vmem_limit_bytes=VMEM_BYTES)


def finish_pack(index, total, far_top, far_bottom, weight, slots, rows, heads, blk, hd):
    width, wide = heads * hd, 2 * hd
    half = far_top.shape[0] // blk

    def kernel(index_ref, total_ref, top_ref, bottom_ref, w_ref, out_ref, pair_ref, query_ref, sems):
        def far(r):
            ref, at = (top_ref, r) if r < half else (bottom_ref, r - half)
            return ref[at * blk : (at + 1) * blk]

        def copy(s):
            tile = index_ref[s]
            row = pl.ds(pl.multiple_of((tile % rows) * blk, blk), blk)
            col = pl.ds(pl.multiple_of((tile // rows) * wide, wide), wide)
            return pltpu.make_async_copy(pair_ref.at[row, col], out_ref.at[s], sems.at[s])

        for r in range(rows):
            at = slice(r * blk, (r + 1) * blk)
            both = (dot(far(r), w_ref[:, width:]) + total_ref[at, width:]).astype(BF)
            for e in range(heads):
                for c in range(2):
                    pair_ref[at, e * wide + c * hd : e * wide + (c + 1) * hd] = both[
                        :, c * width + e * hd : c * width + (e + 1) * hd
                    ]
        for s in range(slots):
            copy(s).start()
        for r in range(rows):
            at = slice(r * blk, (r + 1) * blk)
            query_ref[at] = (dot(far(r), w_ref[:, :width]) + total_ref[at, :width]).astype(BF)
        for s in range(slots):
            copy(s).wait()

    vmem = pl.BlockSpec(memory_space=pltpu.VMEM)
    return pl.pallas_call(
        kernel,
        out_shape=(
            jax.ShapeDtypeStruct((slots, blk, wide), BF),
            jax.ShapeDtypeStruct((rows * blk, 2 * width), BF),
            jax.ShapeDtypeStruct((rows * blk, width), BF),
        ),
        grid_spec=pltpu.PrefetchScalarGridSpec(
            num_scalar_prefetch=1,
            grid=(1,),
            in_specs=[vmem] * 4,
            out_specs=(pl.BlockSpec(memory_space=pl.ANY), vmem, vmem),
            scratch_shapes=[pltpu.SemaphoreType.DMA((slots,))],
        ),
        compiler_params=params(),
        name="finish_pack",
    )(index, total, far_top, far_bottom, weight)


def take_tiles(index, tiles):
    count = index.shape[0]

    def kernel(index_ref, in_ref, out_ref, sems):
        def copy(i):
            return pltpu.make_async_copy(in_ref.at[index_ref[i]], out_ref.at[i], sems.at[i])

        for i in range(count):
            copy(i).start()
        for i in range(count):
            copy(i).wait()

    return pl.pallas_call(
        kernel,
        out_shape=jax.ShapeDtypeStruct((count, *tiles.shape[1:]), tiles.dtype),
        grid_spec=pltpu.PrefetchScalarGridSpec(
            num_scalar_prefetch=1,
            grid=(1,),
            in_specs=[pl.BlockSpec(memory_space=pltpu.VMEM)],
            out_specs=pl.BlockSpec(memory_space=pl.ANY),
            scratch_shapes=[pltpu.SemaphoreType.DMA((count,))],
        ),
        compiler_params=params(),
        name="take_tiles",
    )(index, tiles)


def near_attend(edges, query, around, first, rows, heads, blk, hd, factor):
    def kernel(edge_ref, q_ref, kv_ref, first_ref, acc_ref, stat_ref):
        r = pl.program_id(0)
        window = pl.ds(pl.multiple_of(r * blk, blk), 3 * blk)
        lane = lax.broadcasted_iota(jnp.int32, (blk, 3 * blk), 1)
        low = jnp.where((r == 0) & (edge_ref[0] == 1), blk, 0)
        high = jnp.where((r == rows - 1) & (edge_ref[1] == 1), 2 * blk, 3 * blk)
        usable = (lane >= low) & (lane < high)
        half = lax.broadcasted_iota(jnp.int32, (blk, hd), 1) < hd // 2
        for e in range(heads):
            keys = slice(2 * e * hd, (2 * e + 1) * hd)
            values = slice((2 * e + 1) * hd, (2 * e + 2) * hd)
            q = q_ref[:, e * hd : (e + 1) * hd]
            near = jnp.where(usable, dot_t(q, kv_ref[window, keys]) * factor, NEG)
            glob = dot_t(q, first_ref[:, e * hd : (e + 1) * hd]) * factor
            top = jnp.maximum(
                jnp.max(near, axis=1, keepdims=True), jnp.max(glob, axis=1, keepdims=True)
            )
            near = jnp.exp2(near - top)
            glob = jnp.exp2(glob - top)
            total = jnp.sum(near, axis=1, keepdims=True) + jnp.sum(glob, axis=1, keepdims=True)
            acc_ref[e] = dot(near.astype(BF), kv_ref[window, values]) + dot(
                glob.astype(BF), first_ref[:, (heads + e) * hd : (heads + e + 1) * hd]
            )
            stat_ref[e] = jnp.where(half, top, total)

    out = jax.ShapeDtypeStruct((rows * heads, blk, hd), F32)
    return pl.pallas_call(
        kernel,
        out_shape=(out, out),
        grid_spec=pltpu.PrefetchScalarGridSpec(
            num_scalar_prefetch=1,
            grid=(rows,),
            in_specs=[
                pl.BlockSpec((blk, heads * hd), lambda r, s: (r, 0)),
                pl.BlockSpec(around.shape, lambda r, s: (0, 0)),
                pl.BlockSpec(first.shape, lambda r, s: (0, 0)),
            ],
            out_specs=(
                pl.BlockSpec((heads, blk, hd), lambda r, s: (r, 0, 0)),
                pl.BlockSpec((heads, blk, hd), lambda r, s: (r, 0, 0)),
            ),
        ),
        compiler_params=params(),
        name="near_attend",
    )(edges, query, around, first)


def rand_attend(slot, count, target, query, tiles, acc, stat, rows, heads, blk, hd, rand, peers, factor):
    items = rows * heads
    slots = items * rand

    def kernel(
        slot_ref, count_ref, target_ref, q_ref, acc_ref, stat_ref, tiles_ref, out_ref,
        buffer, done, in_sems, out_sems,
    ):
        def fetch(n):
            return pltpu.make_async_copy(tiles_ref.at[slot_ref[n]], buffer.at[n], in_sems.at[n])

        def deliver(i):
            return pltpu.make_async_copy(done.at[i], out_ref.at[target_ref[i]], out_sems.at[i])

        for n in range(slots):
            fetch(n).start()
        lane = lax.broadcasted_iota(jnp.int32, (blk, rand * blk), 1)

        def step(r, carry):
            first = r * heads
            for n in range(heads * rand):
                fetch(first * rand + n).wait()
            at = pl.ds(pl.multiple_of(r * blk, blk), blk)
            each = range(heads)
            tile_ids = [pl.ds((first + e) * rand, rand) for e in each]
            keys = [buffer[tile_ids[e], :, :hd].reshape(rand * blk, hd) for e in each]
            scores = [dot_t(q_ref[at, e * hd : (e + 1) * hd], keys[e]) for e in each]
            scores = [
                jnp.where(lane < count_ref[first + e] * blk, scores[e] * factor, NEG) for e in each
            ]
            top0 = [stat_ref[first + e, :, 0:1] for e in each]
            total0 = [stat_ref[first + e, :, hd // 2 : hd // 2 + 1] for e in each]
            top = [jnp.maximum(jnp.max(scores[e], axis=1, keepdims=True), top0[e]) for e in each]
            keep = [jnp.exp2(top0[e] - top[e]) for e in each]
            expo = [jnp.exp2(scores[e] - top[e]) for e in each]
            total = [total0[e] * keep[e] + jnp.sum(expo[e], axis=1, keepdims=True) for e in each]
            values = [buffer[tile_ids[e], :, hd:].reshape(rand * blk, hd) for e in each]
            summed = [acc_ref[first + e] * keep[e] + dot(expo[e].astype(BF), values[e]) for e in each]
            for e in each:
                done[first + e] = (summed[e] / total[e]).astype(BF)
            for e in each:
                deliver(first + e).start()
            return carry

        lax.fori_loop(0, rows, step, 0)
        for i in range(items):
            deliver(i).wait()

    vmem = pl.BlockSpec(memory_space=pltpu.VMEM)
    anywhere = pl.BlockSpec(memory_space=pl.ANY)
    return pl.pallas_call(
        kernel,
        out_shape=jax.ShapeDtypeStruct((peers, blk, hd), BF),
        grid_spec=pltpu.PrefetchScalarGridSpec(
            num_scalar_prefetch=3,
            grid=(1,),
            in_specs=[vmem, vmem, vmem, anywhere],
            out_specs=anywhere,
            scratch_shapes=[
                pltpu.VMEM((slots, blk, 2 * hd), BF),
                pltpu.VMEM((items, blk, hd), BF),
                pltpu.SemaphoreType.DMA((slots,)),
                pltpu.SemaphoreType.DMA((items,)),
            ],
        ),
        compiler_params=params(),
        name="rand_attend",
    )(slot, count, target, query, acc, stat, tiles)


def local(tokens, w_qkv, item_at, rand_cols, rand_used):
    peers = lax.axis_size("seq")
    me = lax.axis_index("seq")
    groups = lax.axis_size("head")
    mine_y = lax.axis_index("head")
    heads, nblocks, rand = rand_cols.shape
    rows = nblocks // peers
    count, depth = tokens.shape
    blk = count // rows
    hd = w_qkv.shape[1] // (3 * heads)
    width = heads * hd
    items = heads * rows
    factor = math.log2(math.e) / math.sqrt(hd)

    first_part = tokens[:blk]
    first_part = jnp.where(me == 0, first_part, jnp.zeros_like(first_part))
    stride = peers
    while stride > 1:
        fan = min(4, stride)
        stride //= fan
        holders = range(0, peers, stride * fan)
        got = [
            lax.ppermute(first_part, "seq", [(h, h + k * stride) for h in holders])
            for k in range(1, fan)
        ]
        for other in got:
            first_part = first_part + other

    asked = rand_cols.reshape(heads, peers, rows, rand).transpose(1, 2, 0, 3)
    asked = asked.reshape(peers, items * rand)
    order = jnp.arange(items * rand, dtype=jnp.int32)
    head_of = (order // rand) % heads
    code = order * items + head_of * rows + asked % rows
    mine = asked // rows == me
    low = jnp.min(jnp.where(mine, code, jnp.int32(1 << 30)), axis=1) % items
    high = jnp.max(jnp.where(mine, code, 0), axis=1) % items
    send_tile = jnp.stack([low, high], axis=1).reshape(-1)
    wanted = lax.dynamic_index_in_dim(asked, me, 0, keepdims=False)
    source = wanted // rows
    again = jnp.sum(
        ((source[:, None] == source[None, :]) & (order[None, :] < order[:, None])).astype(jnp.int32),
        axis=1,
    )
    slot = source * 2 + again
    my_used = lax.dynamic_slice_in_dim(rand_used, me * rows, rows, axis=1).T.reshape(-1)
    number = jnp.arange(items, dtype=jnp.int32)
    my_item = (number % heads) * nblocks + me * rows + number // heads
    place = jnp.arange(peers * items, dtype=jnp.int32)
    target = jnp.sum(
        jnp.where(item_at[0][None, :] == my_item[:, None], place[None, :] // items, 0), axis=1
    )
    home = (lax.dynamic_slice_in_dim(item_at[0], me * items, items) % nblocks) // rows
    edges = jnp.stack([me == 0, me == peers - 1]).astype(jnp.int32)

    def weight(shift):
        return lax.dynamic_slice_in_dim(w_qkv, (mine_y + shift) % groups * depth, depth, axis=0)

    onward = [(i, (i + 1) % groups) for i in range(groups)]
    backward = [(b, a) for a, b in onward]
    across = [(i, (i + 2) % groups) for i in range(groups)]
    middle = count // 2
    from_low = lax.ppermute(tokens, "head", onward)
    from_high = lax.ppermute(tokens, "head", backward)
    far_top = lax.ppermute(from_low[:middle], "head", onward)
    far_bottom = lax.ppermute(from_high[middle:], "head", backward)
    first_low = lax.ppermute(first_part, "head", onward)
    first_high = lax.ppermute(first_part, "head", backward)
    first_far = lax.ppermute(first_part, "head", across)

    total = dot(tokens, weight(0)) + dot(from_low, weight(3)) + dot(from_high, weight(1))
    sent, pair, query = finish_pack(
        send_tile, total, far_top, far_bottom, weight(2), 2 * peers, rows, heads, blk, hd
    )
    up = [(i, i + 1) for i in range(peers - 1)]
    down = [(b, a) for a, b in up]
    before = lax.ppermute(pair[-blk:], "seq", up)
    after = lax.ppermute(pair[:blk], "seq", down)
    sent, before, after, first_low, first_high, first_far = lax.optimization_barrier(
        (sent, before, after, first_low, first_high, first_far)
    )
    tiles = lax.all_to_all(sent, "seq", split_axis=0, concat_axis=0, tiled=True)

    around = jnp.concatenate([before, pair, after], axis=0)
    first = dot(first_part, weight(0)[:, width:]) + dot(first_low, weight(3)[:, width:])
    first += dot(first_high, weight(1)[:, width:]) + dot(first_far, weight(2)[:, width:])
    first = first.astype(BF)
    acc, stat = near_attend(edges, query, around, first, rows, heads, blk, hd, factor)
    done = rand_attend(
        slot, my_used, target, query, tiles, acc, stat, rows, heads, blk, hd, rand, peers, factor
    )
    back = lax.all_to_all(done, "seq", split_axis=0, concat_axis=0, tiled=True)
    return take_tiles(home, back)[None]


def solution(mesh):
    return jax.shard_map(
        local,
        mesh=mesh,
        in_specs=(
            P("seq", "head"),
            P(None, "head"),
            P("head", None),
            P("head", None, None),
            P("head", None),
        ),
        out_specs=P("head", "seq", None, None),
        check_vma=False,
    )
```

```python
import math

import jax
import jax.numpy as jnp
from jax import lax
from jax.experimental import pallas as pl
from jax.experimental.pallas import tpu as pltpu
from jax.sharding import PartitionSpec as P

NEG = -1e30
BF = jnp.bfloat16
F32 = jnp.float32
VMEM_BYTES = 48 << 20


def dot(a, b):
    return jnp.dot(a, b, preferred_element_type=F32)


def dot_t(a, b):
    return lax.dot_general(a, b, (((1,), (1,)), ((), ())), preferred_element_type=F32)


def params():
    return pltpu.CompilerParams(vmem_limit_bytes=VMEM_BYTES)


def pack_tiles(index, pair, slots, rows, heads, blk, hd):
    width = heads * hd

    def kernel(index_ref, pair_ref, out_ref, tiles, sems):
        def copy(s):
            return pltpu.make_async_copy(tiles.at[index_ref[s]], out_ref.at[s], sems.at[s])

        for e in range(heads):
            for r in range(rows):
                at = slice(r * blk, (r + 1) * blk)
                tiles[e * rows + r, :, :hd] = pair_ref[at, e * hd : (e + 1) * hd]
                tiles[e * rows + r, :, hd:] = pair_ref[at, width + e * hd : width + (e + 1) * hd].T
        for s in range(slots):
            copy(s).start()
        for s in range(slots):
            copy(s).wait()

    return pl.pallas_call(
        kernel,
        out_shape=jax.ShapeDtypeStruct((slots, blk, 2 * hd), BF),
        grid_spec=pltpu.PrefetchScalarGridSpec(
            num_scalar_prefetch=1,
            grid=(1,),
            in_specs=[pl.BlockSpec(memory_space=pltpu.VMEM)],
            out_specs=pl.BlockSpec(memory_space=pl.ANY),
            scratch_shapes=[
                pltpu.VMEM((rows * heads, blk, 2 * hd), BF),
                pltpu.SemaphoreType.DMA((slots,)),
            ],
        ),
        compiler_params=params(),
        name="pack_tiles",
    )(index, pair)


def take_tiles(index, tiles):
    count = index.shape[0]

    def kernel(index_ref, in_ref, out_ref, sems):
        def copy(i):
            return pltpu.make_async_copy(in_ref.at[index_ref[i]], out_ref.at[i], sems.at[i])

        for i in range(count):
            copy(i).start()
        for i in range(count):
            copy(i).wait()

    return pl.pallas_call(
        kernel,
        out_shape=jax.ShapeDtypeStruct((count, *tiles.shape[1:]), tiles.dtype),
        grid_spec=pltpu.PrefetchScalarGridSpec(
            num_scalar_prefetch=1,
            grid=(1,),
            in_specs=[pl.BlockSpec(memory_space=pltpu.VMEM)],
            out_specs=pl.BlockSpec(memory_space=pl.ANY),
            scratch_shapes=[pltpu.SemaphoreType.DMA((count,))],
        ),
        compiler_params=params(),
        name="take_tiles",
    )(index, tiles)


def near_attend(edges, query, around, first, rows, heads, blk, hd, factor):
    width = heads * hd

    def kernel(edge_ref, q_ref, kv_ref, first_ref, acc_ref, stat_ref):
        r = pl.program_id(0)
        window = pl.ds(pl.multiple_of(r * blk, blk), 3 * blk)
        key = lax.broadcasted_iota(jnp.int32, (3 * blk, blk), 0)
        low = jnp.where((r == 0) & (edge_ref[0] == 1), blk, 0)
        high = jnp.where((r == rows - 1) & (edge_ref[1] == 1), 2 * blk, 3 * blk)
        usable = (key >= low) & (key < high)
        row = lax.broadcasted_iota(jnp.int32, (8, blk), 0)
        for e in range(heads):
            keys = slice(e * hd, (e + 1) * hd)
            values = slice(width + e * hd, width + (e + 1) * hd)
            q = q_ref[:, keys]
            near = jnp.where(usable, dot_t(kv_ref[window, keys], q) * factor, NEG)
            glob = dot_t(first_ref[:, keys], q) * factor
            top = jnp.maximum(
                jnp.max(near, axis=0, keepdims=True), jnp.max(glob, axis=0, keepdims=True)
            )
            near = jnp.exp2(near - top)
            glob = jnp.exp2(glob - top)
            total = jnp.sum(near, axis=0, keepdims=True) + jnp.sum(glob, axis=0, keepdims=True)
            acc_ref[e] = dot(kv_ref[window, values].T, near.astype(BF)) + dot(
                first_ref[:, values].T, glob.astype(BF)
            )
            stat_ref[e] = jnp.where(row == 0, top, total)

    return pl.pallas_call(
        kernel,
        out_shape=(
            jax.ShapeDtypeStruct((rows * heads, hd, blk), F32),
            jax.ShapeDtypeStruct((rows * heads, 8, blk), F32),
        ),
        grid_spec=pltpu.PrefetchScalarGridSpec(
            num_scalar_prefetch=1,
            grid=(rows,),
            in_specs=[
                pl.BlockSpec((blk, width), lambda r, s: (r, 0)),
                pl.BlockSpec(around.shape, lambda r, s: (0, 0)),
                pl.BlockSpec(first.shape, lambda r, s: (0, 0)),
            ],
            out_specs=(
                pl.BlockSpec((heads, hd, blk), lambda r, s: (r, 0, 0)),
                pl.BlockSpec((heads, 8, blk), lambda r, s: (r, 0, 0)),
            ),
        ),
        compiler_params=params(),
        name="near_attend",
    )(edges, query, around, first)


def rand_attend(slot, count, target, query, tiles, acc, stat, rows, heads, blk, hd, rand, peers, factor):
    items = rows * heads
    slots = items * rand

    def kernel(
        slot_ref, count_ref, target_ref, q_ref, acc_ref, stat_ref, tiles_ref, out_ref,
        buffer, done, in_sems, out_sems,
    ):
        def fetch(n):
            return pltpu.make_async_copy(tiles_ref.at[slot_ref[n]], buffer.at[n], in_sems.at[n])

        def deliver(i):
            return pltpu.make_async_copy(done.at[i], out_ref.at[target_ref[i]], out_sems.at[i])

        for n in range(slots):
            fetch(n).start()
        key = lax.broadcasted_iota(jnp.int32, (rand * blk, blk), 0)

        def step(r, carry):
            first = r * heads
            for n in range(heads * rand):
                fetch(first * rand + n).wait()
            at = pl.ds(pl.multiple_of(r * blk, blk), blk)
            each = range(heads)
            keys = [
                buffer[pl.ds((first + e) * rand, rand), :, :hd].reshape(rand * blk, hd) for e in each
            ]
            scores = [dot_t(keys[e], q_ref[at, e * hd : (e + 1) * hd]) for e in each]
            scores = [
                jnp.where(key < count_ref[first + e] * blk, scores[e] * factor, NEG) for e in each
            ]
            top0 = [stat_ref[first + e, 0:1] for e in each]
            total0 = [stat_ref[first + e, 1:2] for e in each]
            top = [jnp.maximum(jnp.max(scores[e], axis=0, keepdims=True), top0[e]) for e in each]
            keep = [jnp.exp2(top0[e] - top[e]) for e in each]
            expo = [jnp.exp2(scores[e] - top[e]) for e in each]
            total = [total0[e] * keep[e] + jnp.sum(expo[e], axis=0, keepdims=True) for e in each]
            values = [
                jnp.concatenate([buffer[(first + e) * rand + j, :, hd:] for j in range(rand)], axis=1)
                for e in each
            ]
            summed = [acc_ref[first + e] * keep[e] + dot(values[e], expo[e].astype(BF)) for e in each]
            for e in each:
                done[first + e] = (summed[e] / total[e]).T.astype(BF)
            for e in each:
                deliver(first + e).start()
            return carry

        lax.fori_loop(0, rows, step, 0)
        for i in range(items):
            deliver(i).wait()

    vmem = pl.BlockSpec(memory_space=pltpu.VMEM)
    anywhere = pl.BlockSpec(memory_space=pl.ANY)
    return pl.pallas_call(
        kernel,
        out_shape=jax.ShapeDtypeStruct((peers, blk, hd), BF),
        grid_spec=pltpu.PrefetchScalarGridSpec(
            num_scalar_prefetch=3,
            grid=(1,),
            in_specs=[vmem, vmem, vmem, anywhere],
            out_specs=anywhere,
            scratch_shapes=[
                pltpu.VMEM((slots, blk, 2 * hd), BF),
                pltpu.VMEM((items, blk, hd), BF),
                pltpu.SemaphoreType.DMA((slots,)),
                pltpu.SemaphoreType.DMA((items,)),
            ],
        ),
        compiler_params=params(),
        name="rand_attend",
    )(slot, count, target, query, acc, stat, tiles)


def local(tokens, w_qkv, item_at, rand_cols, rand_used):
    peers = lax.axis_size("seq")
    me = lax.axis_index("seq")
    groups = lax.axis_size("head")
    mine_y = lax.axis_index("head")
    heads, nblocks, rand = rand_cols.shape
    rows = nblocks // peers
    count, depth = tokens.shape
    blk = count // rows
    hd = w_qkv.shape[1] // (3 * heads)
    width = heads * hd
    items = heads * rows
    factor = math.log2(math.e) / math.sqrt(hd)

    asked = rand_cols.reshape(heads, peers, rows, rand).transpose(1, 2, 0, 3)
    asked = asked.reshape(peers, items * rand)
    order = jnp.arange(items * rand, dtype=jnp.int32)
    head_of = (order // rand) % heads
    code = order * items + head_of * rows + asked % rows
    mine = asked // rows == me
    low = jnp.min(jnp.where(mine, code, jnp.int32(1 << 30)), axis=1) % items
    high = jnp.max(jnp.where(mine, code, 0), axis=1) % items
    send_tile = jnp.stack([low, high], axis=1).reshape(-1)
    wanted = lax.dynamic_index_in_dim(asked, me, 0, keepdims=False)
    source = wanted // rows
    again = jnp.sum(
        ((source[:, None] == source[None, :]) & (order[None, :] < order[:, None])).astype(jnp.int32),
        axis=1,
    )
    slot = source * 2 + again
    my_used = lax.dynamic_slice_in_dim(rand_used, me * rows, rows, axis=1).T.reshape(-1)
    number = jnp.arange(items, dtype=jnp.int32)
    my_item = (number % heads) * nblocks + me * rows + number // heads
    place = jnp.arange(peers * items, dtype=jnp.int32)
    target = jnp.sum(
        jnp.where(item_at[0][None, :] == my_item[:, None], place[None, :] // items, 0), axis=1
    )
    home = (lax.dynamic_slice_in_dim(item_at[0], me * items, items) % nblocks) // rows
    edges = jnp.stack([me == 0, me == peers - 1]).astype(jnp.int32)

    def weight(shift, first, size):
        row = (mine_y + shift) % groups * depth
        return lax.dynamic_slice(w_qkv, (row, jnp.int32(first)), (depth, size))

    def w_pair(shift):
        return weight(shift, width, 2 * width)

    def w_query(shift):
        return weight(shift, 0, width)

    def spread(block, stride):
        holders = range(0, peers, 4 * stride)
        got = [
            lax.ppermute(block, "seq", [(h, h + k * stride) for h in holders]) for k in (1, 2, 3)
        ]
        return block + got[0] + got[1] + got[2]

    onward = [(i, (i + 1) % groups) for i in range(groups)]
    backward = [(b, a) for a, b in onward]
    across = [(i, (i + 2) % groups) for i in range(groups)]
    middle = count // 2
    from_low = lax.ppermute(tokens, "head", onward)
    from_high = lax.ppermute(tokens, "head", backward)
    zero = tokens[:blk]
    zero = jnp.where(me == 0, zero, jnp.zeros_like(zero))
    zero = spread(spread(spread(zero, peers // 4), peers // 16), peers // 64)
    far_top = lax.ppermute(from_low[:middle], "head", onward)
    far_bottom = lax.ppermute(from_high[middle:], "head", backward)
    total = dot(tokens, w_pair(0)) + dot(from_low, w_pair(3))
    total, zero = lax.optimization_barrier((total, zero))
    zero_low = lax.ppermute(zero, "head", onward)
    zero_high = lax.ppermute(zero, "head", backward)
    zero_far = lax.ppermute(zero, "head", across)
    total += dot(from_high, w_pair(1))
    far_top, far_bottom, zero_low, zero_high, zero_far = lax.optimization_barrier(
        (far_top, far_bottom, zero_low, zero_high, zero_far)
    )
    pair = jnp.concatenate(
        [
            (total[:middle] + dot(far_top, w_pair(2))).astype(BF),
            (total[middle:] + dot(far_bottom, w_pair(2))).astype(BF),
        ],
        axis=0,
    )
    up = [(i, i + 1) for i in range(peers - 1)]
    down = [(b, a) for a, b in up]
    before = lax.ppermute(pair[-blk:], "seq", up)
    after = lax.ppermute(pair[:blk], "seq", down)
    sent = pack_tiles(send_tile, pair, 2 * peers, rows, heads, blk, hd)
    sent, before, after, far_top, far_bottom = lax.optimization_barrier(
        (sent, before, after, far_top, far_bottom)
    )
    tiles = lax.all_to_all(sent, "seq", split_axis=0, concat_axis=0, tiled=True)

    around = jnp.concatenate([before, pair, after], axis=0)
    far = jnp.concatenate([far_top, far_bottom], axis=0)
    query = dot(far, w_query(2)) + dot(tokens, w_query(0))
    query = (query + dot(from_low, w_query(3)) + dot(from_high, w_query(1))).astype(BF)
    first = dot(zero, w_pair(0)) + dot(zero_low, w_pair(3))
    first = (first + dot(zero_high, w_pair(1)) + dot(zero_far, w_pair(2))).astype(BF)
    acc, stat = near_attend(edges, query, around, first, rows, heads, blk, hd, factor)
    done = rand_attend(
        slot, my_used, target, query, tiles, acc, stat, rows, heads, blk, hd, rand, peers, factor
    )
    back = lax.all_to_all(done, "seq", split_axis=0, concat_axis=0, tiled=True)
    return take_tiles(home, back)[None]


def solution(mesh):
    return jax.shard_map(
        local,
        mesh=mesh,
        in_specs=(
            P("seq", "head"),
            P(None, "head"),
            P("head", None),
            P("head", None, None),
            P("head", None),
        ),
        out_specs=P("head", "seq", None, None),
        check_vma=False,
    )
```

```python
import math

import jax
import jax.numpy as jnp
from jax import lax
from jax.experimental import pallas as pl
from jax.experimental.pallas import tpu as pltpu
from jax.sharding import PartitionSpec as P

NEG = -1e30
BF = jnp.bfloat16
F32 = jnp.float32
VMEM_BYTES = 48 << 20


def dot(a, b):
    return jnp.dot(a, b, preferred_element_type=F32)


def dot_t(a, b):
    return lax.dot_general(a, b, (((1,), (1,)), ((), ())), preferred_element_type=F32)


def params():
    return pltpu.CompilerParams(vmem_limit_bytes=VMEM_BYTES)


def pack_tiles(table, dests, pair, routes, rows, heads, blk, hd, name):
    width = heads * hd
    count = 4 * routes

    def kernel(table_ref, dest_ref, pair_ref, *refs):
        outs = refs[:routes]
        tiles, sems = refs[routes:]

        def copy(s):
            k, j, t = s // 4, s // 2 % 2, s % 2
            tile = table_ref[2 * dest_ref[2 * k + j] + t]
            return pltpu.make_async_copy(tiles.at[tile], outs[k].at[j, t], sems.at[s])

        for e in range(heads):
            for r in range(rows):
                at = slice(r * blk, (r + 1) * blk)
                tiles[e * rows + r, :, :hd] = pair_ref[at, e * hd : (e + 1) * hd]
                tiles[e * rows + r, :, hd:] = pair_ref[at, width + e * hd : width + (e + 1) * hd].T
        for s in range(count):
            copy(s).start()
        for s in range(count):
            copy(s).wait()

    return pl.pallas_call(
        kernel,
        out_shape=[jax.ShapeDtypeStruct((2, 2, blk, 2 * hd), BF)] * routes,
        grid_spec=pltpu.PrefetchScalarGridSpec(
            num_scalar_prefetch=2,
            grid=(1,),
            in_specs=[pl.BlockSpec(memory_space=pltpu.VMEM)],
            out_specs=[pl.BlockSpec(memory_space=pltpu.HBM)] * routes,
            scratch_shapes=[
                pltpu.VMEM((rows * heads, blk, 2 * hd), BF),
                pltpu.SemaphoreType.DMA((count,)),
            ],
        ),
        compiler_params=params(),
        name=name,
    )(table, dests, pair)


def take_tiles(index, tiles):
    count = index.shape[0]

    def kernel(index_ref, in_ref, out_ref, sems):
        def copy(i):
            return pltpu.make_async_copy(in_ref.at[index_ref[i]], out_ref.at[i], sems.at[i])

        for i in range(count):
            copy(i).start()
        for i in range(count):
            copy(i).wait()

    return pl.pallas_call(
        kernel,
        out_shape=jax.ShapeDtypeStruct((count, *tiles.shape[1:]), tiles.dtype),
        grid_spec=pltpu.PrefetchScalarGridSpec(
            num_scalar_prefetch=1,
            grid=(1,),
            in_specs=[pl.BlockSpec(memory_space=pltpu.VMEM)],
            out_specs=pl.BlockSpec(memory_space=pl.ANY),
            scratch_shapes=[pltpu.SemaphoreType.DMA((count,))],
        ),
        compiler_params=params(),
        name="take_tiles",
    )(index, tiles)


def near_attend(edges, query, around, first, rows, heads, blk, hd, factor):
    width = heads * hd

    def kernel(edge_ref, q_ref, kv_ref, first_ref, acc_ref, stat_ref):
        r = pl.program_id(0)
        window = pl.ds(pl.multiple_of(r * blk, blk), 3 * blk)
        key = lax.broadcasted_iota(jnp.int32, (3 * blk, blk), 0)
        low = jnp.where((r == 0) & (edge_ref[0] == 1), blk, 0)
        high = jnp.where((r == rows - 1) & (edge_ref[1] == 1), 2 * blk, 3 * blk)
        usable = (key >= low) & (key < high)
        row = lax.broadcasted_iota(jnp.int32, (8, blk), 0)
        for e in range(heads):
            keys = slice(e * hd, (e + 1) * hd)
            values = slice(width + e * hd, width + (e + 1) * hd)
            q = q_ref[:, keys]
            near = jnp.where(usable, dot_t(kv_ref[window, keys], q) * factor, NEG)
            glob = dot_t(first_ref[:, keys], q) * factor
            top = jnp.maximum(
                jnp.max(near, axis=0, keepdims=True), jnp.max(glob, axis=0, keepdims=True)
            )
            near = jnp.exp2(near - top)
            glob = jnp.exp2(glob - top)
            total = jnp.sum(near, axis=0, keepdims=True) + jnp.sum(glob, axis=0, keepdims=True)
            acc_ref[e] = dot(kv_ref[window, values].T, near.astype(BF)) + dot(
                first_ref[:, values].T, glob.astype(BF)
            )
            stat_ref[e] = jnp.where(row == 0, top, total)

    return pl.pallas_call(
        kernel,
        out_shape=(
            jax.ShapeDtypeStruct((rows * heads, hd, blk), F32),
            jax.ShapeDtypeStruct((rows * heads, 8, blk), F32),
        ),
        grid_spec=pltpu.PrefetchScalarGridSpec(
            num_scalar_prefetch=1,
            grid=(rows,),
            in_specs=[
                pl.BlockSpec((blk, width), lambda r, s: (r, 0)),
                pl.BlockSpec(around.shape, lambda r, s: (0, 0)),
                pl.BlockSpec(first.shape, lambda r, s: (0, 0)),
            ],
            out_specs=(
                pl.BlockSpec((heads, hd, blk), lambda r, s: (r, 0, 0)),
                pl.BlockSpec((heads, 8, blk), lambda r, s: (r, 0, 0)),
            ),
        ),
        compiler_params=params(),
        name="near_attend",
    )(edges, query, around, first)


def rand_attend(slot, count, target, query, direct, swapped, acc, stat, rows, heads, blk, hd, rand, peers, factor):
    items = rows * heads
    slots = items * rand
    routes = len(direct[0])

    def kernel(slot_ref, count_ref, target_ref, q_ref, acc_ref, stat_ref, *refs):
        arrived = refs[: 2 * routes]
        crossed = refs[2 * routes : 2 * routes + 2]
        out_ref, buffer, done, in_sems, out_sems = refs[2 * routes + 2 :]
        copies = []
        for half in range(2):
            for k in range(routes):
                place = buffer.at[pl.ds((2 * half * routes + k) * 2, 2)]
                copies.append((arrived[half * routes + k].at[0], place))
            for k in range(routes):
                place = buffer.at[pl.ds(((2 * half + 1) * routes + k) * 2, 2)]
                copies.append((crossed[half].at[k], place))
        copies = [
            pltpu.make_async_copy(source, place, in_sems.at[n])
            for n, (source, place) in enumerate(copies)
        ]

        def deliver(i):
            return pltpu.make_async_copy(done.at[i], out_ref.at[target_ref[i]], out_sems.at[i])

        for copy in copies:
            copy.start()
        key = lax.broadcasted_iota(jnp.int32, (rand * blk, blk), 0)

        def step(r, carry):
            first = r * heads
            at = pl.ds(pl.multiple_of(r * blk, blk), blk)
            each = range(heads)
            places = [[slot_ref[(first + e) * rand + j] for j in range(rand)] for e in each]
            keys = [jnp.concatenate([buffer[p, :, :hd] for p in places[e]], axis=0) for e in each]
            scores = [dot_t(keys[e], q_ref[at, e * hd : (e + 1) * hd]) for e in each]
            scores = [
                jnp.where(key < count_ref[first + e] * blk, scores[e] * factor, NEG) for e in each
            ]
            top0 = [stat_ref[first + e, 0:1] for e in each]
            total0 = [stat_ref[first + e, 1:2] for e in each]
            top = [jnp.maximum(jnp.max(scores[e], axis=0, keepdims=True), top0[e]) for e in each]
            keep = [jnp.exp2(top0[e] - top[e]) for e in each]
            expo = [jnp.exp2(scores[e] - top[e]) for e in each]
            total = [total0[e] * keep[e] + jnp.sum(expo[e], axis=0, keepdims=True) for e in each]
            values = [jnp.concatenate([buffer[p, :, hd:] for p in places[e]], axis=1) for e in each]
            summed = [acc_ref[first + e] * keep[e] + dot(values[e], expo[e].astype(BF)) for e in each]
            for e in each:
                done[first + e] = (summed[e] / total[e]).T.astype(BF)
            for e in each:
                deliver(first + e).start()
            return carry

        for copy in copies:
            copy.wait()
        lax.fori_loop(0, rows, step, 0)
        for i in range(items):
            deliver(i).wait()

    vmem = pl.BlockSpec(memory_space=pltpu.VMEM)
    anywhere = pl.BlockSpec(memory_space=pl.ANY)
    return pl.pallas_call(
        kernel,
        out_shape=jax.ShapeDtypeStruct((peers, blk, hd), BF),
        grid_spec=pltpu.PrefetchScalarGridSpec(
            num_scalar_prefetch=3,
            grid=(1,),
            in_specs=[vmem, vmem, vmem, *[anywhere] * (2 * routes + 2)],
            out_specs=pl.BlockSpec(memory_space=pltpu.HBM),
            scratch_shapes=[
                pltpu.VMEM((slots, blk, 2 * hd), BF),
                pltpu.VMEM((items, blk, hd), BF),
                pltpu.SemaphoreType.DMA((4 * routes,)),
                pltpu.SemaphoreType.DMA((items,)),
            ],
        ),
        compiler_params=params(),
        name="rand_attend",
    )(slot, count, target, query, acc, stat, *direct[0], *direct[1], *swapped)


NX, NZ, NC = 4, 8, 2
ROUTES = [(a, b) for a in range(4) for b in range(NX)]


def z_step(a, to_x):
    return [0, 1, -1, 2 - 4 * (to_x % 2)][a]


def device(x, z, core):
    return (x % NX * NZ + z % NZ) * NC + core


def seq_pairs(goal):
    return [
        (device(x, z, c), device(*goal(x, z, c)))
        for x in range(NX)
        for z in range(NZ)
        for c in range(NC)
    ]


def route_goal(a, b):
    return lambda x, z, c: (x + b, z + z_step(a, (x + b) % NX), c)


def local(tokens, w_qkv, item_at, rand_cols, rand_used):
    peers = lax.axis_size("seq")
    assert peers == NX * NZ * NC
    me = lax.axis_index("seq")
    my_x, my_z, my_core = me // (NZ * NC), me // NC % NZ, me % NC
    groups = lax.axis_size("head")
    mine_y = lax.axis_index("head")
    heads, nblocks, rand = rand_cols.shape
    rows = nblocks // peers
    count, depth = tokens.shape
    blk = count // rows
    hd = w_qkv.shape[1] // (3 * heads)
    width = heads * hd
    items = heads * rows
    factor = math.log2(math.e) / math.sqrt(hd)

    asked = rand_cols.reshape(heads, peers, rows, rand).transpose(1, 2, 0, 3)
    asked = asked.reshape(peers, items * rand)
    order = jnp.arange(items * rand, dtype=jnp.int32)
    code = order * items + (order // rand) % heads * rows + asked % rows

    def held_for(holder):
        held = asked // rows == holder
        low = jnp.min(jnp.where(held, code, jnp.int32(1 << 30)), axis=1) % items
        high = jnp.max(jnp.where(held, code, 0), axis=1) % items
        return jnp.stack([low, high], axis=1).reshape(-1)

    far_z = device(my_x, my_z + NZ // 2, my_core)
    tables = (held_for(me), held_for(far_z))
    route = jnp.arange(2 * len(ROUTES), dtype=jnp.int32)
    kind, to_x = route // (2 * NX), (my_x + route // 2 % NX) % NX
    two = 2 - 4 * (to_x % 2)
    to_z = my_z + jnp.where(kind == 3, two, jnp.where(kind == 2, -1, kind))
    dests = device(to_x, to_z, (my_core + route) % NC)

    wanted = lax.dynamic_index_in_dim(asked, me, 0, keepdims=False)
    source = wanted // rows
    rank = jnp.sum(
        ((source[:, None] == source[None, :]) & (order[None, :] < order[:, None])).astype(jnp.int32),
        axis=1,
    )
    turn = (my_x - source // (NZ * NC)) % NX
    step = (my_z - source // NC) % NZ
    cross = (source % NC != my_core).astype(jnp.int32)
    my_two = (2 - 4 * (my_x % 2)) % NZ

    def route_kind(step):
        return jnp.where(
            step == 0, 0, jnp.where(step == 1, 1, jnp.where(step == NZ - 1, 2, jnp.where(step == my_two, 3, -1)))
        )

    near_kind = route_kind(step)
    other_kind = route_kind((step + NZ // 2) % NZ)
    half = (near_kind < 0).astype(jnp.int32)
    slot = ((2 * half + cross) * 4 + jnp.where(half == 1, other_kind, near_kind)) * NX + turn
    slot = slot * 2 + rank

    my_used = lax.dynamic_slice_in_dim(rand_used, me * rows, rows, axis=1).T.reshape(-1)
    number = jnp.arange(items, dtype=jnp.int32)
    my_item = (number % heads) * nblocks + me * rows + number // heads
    place = jnp.arange(peers * items, dtype=jnp.int32)
    target = jnp.sum(
        jnp.where(item_at[0][None, :] == my_item[:, None], place[None, :] // items, 0), axis=1
    )
    home = (lax.dynamic_slice_in_dim(item_at[0], me * items, items) % nblocks) // rows
    edges = jnp.stack([me == 0, me == peers - 1]).astype(jnp.int32)

    def weight(shift, first, size):
        row = (mine_y + shift) % groups * depth
        return lax.dynamic_slice(w_qkv, (row, jnp.int32(first)), (depth, size))

    def w_pair(shift):
        return weight(shift, width, 2 * width)

    def w_query(shift):
        return weight(shift, 0, width)

    def spread(block, stride):
        holders = range(0, peers, 4 * stride)
        got = [
            lax.ppermute(block, "seq", [(h, h + k * stride) for h in holders]) for k in (1, 2, 3)
        ]
        return block + got[0] + got[1] + got[2]

    onward = [(i, (i + 1) % groups) for i in range(groups)]
    backward = [(b, a) for a, b in onward]

    def ring(part):
        middle = part.shape[0] // 2
        low = lax.ppermute(part, "head", onward)
        high = lax.ppermute(part, "head", backward)
        top = lax.ppermute(low[:middle], "head", onward)
        bottom = lax.ppermute(high[middle:], "head", backward)
        return low, high, top, bottom

    def keys_values(part, low, high, top, bottom):
        middle = part.shape[0] // 2
        total = dot(part, w_pair(0)) + dot(low, w_pair(3)) + dot(high, w_pair(1))
        return jnp.concatenate(
            [
                (total[:middle] + dot(top, w_pair(2))).astype(BF),
                (total[middle:] + dot(bottom, w_pair(2))).astype(BF),
            ],
            axis=0,
        )

    from_low, from_high, far_top, far_bottom = ring(tokens)
    copied = lax.ppermute(tokens, "seq", seq_pairs(lambda x, z, c: (x, z + NZ // 2, c)))
    zero = tokens[:blk]
    zero = jnp.where(me == 0, zero, jnp.zeros_like(zero))
    zero = spread(spread(spread(zero, peers // 4), peers // 16), peers // 64)
    copied = jnp.concatenate([copied, zero], axis=0)
    copied_ring = ring(copied)

    pair = keys_values(tokens, from_low, from_high, far_top, far_bottom)
    up = [(i, i + 1) for i in range(peers - 1)]
    down = [(b, a) for a, b in up]
    before = lax.ppermute(pair[-blk:], "seq", up)
    after = lax.ppermute(pair[:blk], "seq", down)

    def exchange(table, pair, name):
        parts = pack_tiles(table, dests, pair, len(ROUTES), rows, heads, blk, hd, name)
        got = [
            lax.ppermute(part, "seq", seq_pairs(route_goal(a, b))) if a or b else part
            for part, (a, b) in zip(parts, ROUTES)
        ]
        crossing = jnp.stack([part[1] for part in got])
        swapped = lax.ppermute(crossing, "seq", seq_pairs(lambda x, z, c: (x, z, 1 - c)))
        return got, swapped

    direct, swapped = exchange(tables[0], pair, "pack_own")
    copied_pair = keys_values(copied, *copied_ring)
    direct2, swapped2 = exchange(tables[1], copied_pair, "pack_copied")

    around = jnp.concatenate([before, pair, after], axis=0)
    far = jnp.concatenate([far_top, far_bottom], axis=0)
    query = dot(far, w_query(2)) + dot(tokens, w_query(0))
    query = (query + dot(from_low, w_query(3)) + dot(from_high, w_query(1))).astype(BF)
    first = copied_pair[count:]
    acc, stat = near_attend(edges, query, around, first, rows, heads, blk, hd, factor)
    done = rand_attend(
        slot, my_used, target, query, (direct, direct2), (swapped, swapped2), acc, stat,
        rows, heads, blk, hd, rand, peers, factor,
    )
    back = lax.all_to_all(done, "seq", split_axis=0, concat_axis=0, tiled=True)
    return take_tiles(home, back)[None]


def solution(mesh):
    return jax.shard_map(
        local,
        mesh=mesh,
        in_specs=(
            P("seq", "head"),
            P(None, "head"),
            P("head", None),
            P("head", None, None),
            P("head", None),
        ),
        out_specs=P("head", "seq", None, None),
        check_vma=False,
    )
```

```python
import math

import jax
import jax.numpy as jnp
from jax import lax
from jax.experimental import pallas as pl
from jax.experimental.pallas import tpu as pltpu
from jax.sharding import PartitionSpec as P

NEG = -1e30
BF = jnp.bfloat16
F32 = jnp.float32
VMEM_BYTES = 48 << 20


def dot(a, b):
    return jnp.dot(a, b, preferred_element_type=F32)


def dot_t(a, b):
    return lax.dot_general(a, b, (((1,), (1,)), ((), ())), preferred_element_type=F32)


def params():
    return pltpu.CompilerParams(vmem_limit_bytes=VMEM_BYTES)


def pack_tiles(table, dests, pair, shares, rows, heads, blk, hd, name):
    width = heads * hd
    ends = [(k, i) for k, share in enumerate(shares) for i in range(share)]

    def kernel(table_ref, dest_ref, pair_ref, *refs):
        outs = refs[: len(shares)]
        tiles, sems = refs[len(shares) :]

        def copy(n, t):
            k, i = ends[n]
            tile = table_ref[2 * dest_ref[n] + t]
            return pltpu.make_async_copy(tiles.at[tile], outs[k].at[i, t], sems.at[2 * n + t])

        for e in range(heads):
            for r in range(rows):
                at = slice(r * blk, (r + 1) * blk)
                tiles[e * rows + r, :, :hd] = pair_ref[at, e * hd : (e + 1) * hd]
                tiles[e * rows + r, :, hd:] = pair_ref[at, width + e * hd : width + (e + 1) * hd].T
        for n in range(len(ends)):
            for t in range(2):
                copy(n, t).start()
        for n in range(len(ends)):
            for t in range(2):
                copy(n, t).wait()

    anywhere = pl.BlockSpec(memory_space=pl.ANY)
    return pl.pallas_call(
        kernel,
        out_shape=[jax.ShapeDtypeStruct((share, 2, blk, 2 * hd), BF) for share in shares],
        grid_spec=pltpu.PrefetchScalarGridSpec(
            num_scalar_prefetch=2,
            grid=(1,),
            in_specs=[pl.BlockSpec(memory_space=pltpu.VMEM)],
            out_specs=[anywhere] * len(shares),
            scratch_shapes=[
                pltpu.VMEM((rows * heads, blk, 2 * hd), BF),
                pltpu.SemaphoreType.DMA((2 * len(ends),)),
            ],
        ),
        compiler_params=params(),
        name=name,
    )(table, dests, pair)


def merge_parts(parts, places, name):
    count = sum(len(at) for at in places)
    rest = parts[0].shape[1:]

    def kernel(*refs):
        out_ref, sems = refs[len(parts) :]
        copies = []
        for ref, at in zip(refs, places):
            for i, (g, a) in enumerate(at):
                copies.append(
                    pltpu.make_async_copy(ref.at[i], out_ref.at[g, a], sems.at[len(copies)])
                )
        for copy in copies:
            copy.start()
        for copy in copies:
            copy.wait()

    return pl.pallas_call(
        kernel,
        out_shape=jax.ShapeDtypeStruct((count // 4, 4, *rest), parts[0].dtype),
        in_specs=[pl.BlockSpec(memory_space=pltpu.VMEM)] * len(parts),
        out_specs=pl.BlockSpec(memory_space=pltpu.HBM),
        scratch_shapes=[pltpu.SemaphoreType.DMA((count,))],
        compiler_params=params(),
        name=name,
    )(*parts)


def take_tiles(index, tiles):
    count = index.shape[0]

    def kernel(index_ref, in_ref, out_ref, sems):
        def copy(i):
            return pltpu.make_async_copy(in_ref.at[index_ref[i]], out_ref.at[i], sems.at[i])

        for i in range(count):
            copy(i).start()
        for i in range(count):
            copy(i).wait()

    return pl.pallas_call(
        kernel,
        out_shape=jax.ShapeDtypeStruct((count, *tiles.shape[1:]), tiles.dtype),
        grid_spec=pltpu.PrefetchScalarGridSpec(
            num_scalar_prefetch=1,
            grid=(1,),
            in_specs=[pl.BlockSpec(memory_space=pltpu.VMEM)],
            out_specs=pl.BlockSpec(memory_space=pl.ANY),
            scratch_shapes=[pltpu.SemaphoreType.DMA((count,))],
        ),
        compiler_params=params(),
        name="take_tiles",
    )(index, tiles)


def near_attend(edges, query, around, first, rows, heads, blk, hd, factor):
    width = heads * hd

    def kernel(edge_ref, q_ref, kv_ref, first_ref, acc_ref, stat_ref):
        r = pl.program_id(0)
        window = pl.ds(pl.multiple_of(r * blk, blk), 3 * blk)
        key = lax.broadcasted_iota(jnp.int32, (3 * blk, blk), 0)
        low = jnp.where((r == 0) & (edge_ref[0] == 1), blk, 0)
        high = jnp.where((r == rows - 1) & (edge_ref[1] == 1), 2 * blk, 3 * blk)
        usable = (key >= low) & (key < high)
        row = lax.broadcasted_iota(jnp.int32, (8, blk), 0)
        for e in range(heads):
            keys = slice(e * hd, (e + 1) * hd)
            values = slice(width + e * hd, width + (e + 1) * hd)
            q = q_ref[:, keys]
            near = jnp.where(usable, dot_t(kv_ref[window, keys], q) * factor, NEG)
            glob = dot_t(first_ref[:, keys], q) * factor
            top = jnp.maximum(
                jnp.max(near, axis=0, keepdims=True), jnp.max(glob, axis=0, keepdims=True)
            )
            near = jnp.exp2(near - top)
            glob = jnp.exp2(glob - top)
            total = jnp.sum(near, axis=0, keepdims=True) + jnp.sum(glob, axis=0, keepdims=True)
            acc_ref[e] = dot(kv_ref[window, values].T, near.astype(BF)) + dot(
                first_ref[:, values].T, glob.astype(BF)
            )
            stat_ref[e] = jnp.where(row == 0, top, total)

    return pl.pallas_call(
        kernel,
        out_shape=(
            jax.ShapeDtypeStruct((rows * heads, hd, blk), F32),
            jax.ShapeDtypeStruct((rows * heads, 8, blk), F32),
        ),
        grid_spec=pltpu.PrefetchScalarGridSpec(
            num_scalar_prefetch=1,
            grid=(rows,),
            in_specs=[
                pl.BlockSpec((blk, width), lambda r, s: (r, 0)),
                pl.BlockSpec(around.shape, lambda r, s: (0, 0)),
                pl.BlockSpec(first.shape, lambda r, s: (0, 0)),
            ],
            out_specs=(
                pl.BlockSpec((heads, hd, blk), lambda r, s: (r, 0, 0)),
                pl.BlockSpec((heads, 8, blk), lambda r, s: (r, 0, 0)),
            ),
        ),
        compiler_params=params(),
        name="near_attend",
    )(edges, query, around, first)


def rand_attend(slot, count, target, query, tiles, acc, stat, rows, heads, blk, hd, rand, peers, factor):
    items = rows * heads
    slots = items * rand
    share = slots // len(tiles)

    def kernel(slot_ref, count_ref, target_ref, q_ref, acc_ref, stat_ref, *refs):
        out_ref, buffer, done, in_sems, out_sems = refs[len(tiles) :]
        copies = [
            pltpu.make_async_copy(refs[n], buffer.at[pl.ds(n * share, share)], in_sems.at[n])
            for n in range(len(tiles))
        ]

        def deliver(i):
            return pltpu.make_async_copy(done.at[i], out_ref.at[target_ref[i]], out_sems.at[i])

        for copy in copies:
            copy.start()
        key = lax.broadcasted_iota(jnp.int32, (rand * blk, blk), 0)

        def step(r, carry):
            first = r * heads
            at = pl.ds(pl.multiple_of(r * blk, blk), blk)
            each = range(heads)
            places = [[slot_ref[(first + e) * rand + j] for j in range(rand)] for e in each]
            keys = [jnp.concatenate([buffer[p, :, :hd] for p in places[e]], axis=0) for e in each]
            scores = [dot_t(keys[e], q_ref[at, e * hd : (e + 1) * hd]) for e in each]
            scores = [
                jnp.where(key < count_ref[first + e] * blk, scores[e] * factor, NEG) for e in each
            ]
            top0 = [stat_ref[first + e, 0:1] for e in each]
            total0 = [stat_ref[first + e, 1:2] for e in each]
            top = [jnp.maximum(jnp.max(scores[e], axis=0, keepdims=True), top0[e]) for e in each]
            keep = [jnp.exp2(top0[e] - top[e]) for e in each]
            expo = [jnp.exp2(scores[e] - top[e]) for e in each]
            total = [total0[e] * keep[e] + jnp.sum(expo[e], axis=0, keepdims=True) for e in each]
            values = [jnp.concatenate([buffer[p, :, hd:] for p in places[e]], axis=1) for e in each]
            summed = [acc_ref[first + e] * keep[e] + dot(values[e], expo[e].astype(BF)) for e in each]
            for e in each:
                done[first + e] = (summed[e] / total[e]).T.astype(BF)
            for e in each:
                deliver(first + e).start()
            return carry

        for copy in copies:
            copy.wait()
        lax.fori_loop(0, rows, step, 0)
        for i in range(items):
            deliver(i).wait()

    vmem = pl.BlockSpec(memory_space=pltpu.VMEM)
    anywhere = pl.BlockSpec(memory_space=pl.ANY)
    return pl.pallas_call(
        kernel,
        out_shape=jax.ShapeDtypeStruct((peers, blk, hd), BF),
        grid_spec=pltpu.PrefetchScalarGridSpec(
            num_scalar_prefetch=3,
            grid=(1,),
            in_specs=[vmem, vmem, vmem, *[anywhere] * len(tiles)],
            out_specs=pl.BlockSpec(memory_space=pltpu.HBM),
            scratch_shapes=[
                pltpu.VMEM((slots, blk, 2 * hd), BF),
                pltpu.VMEM((items, blk, hd), BF),
                pltpu.SemaphoreType.DMA((len(tiles),)),
                pltpu.SemaphoreType.DMA((items,)),
            ],
        ),
        compiler_params=params(),
        name="rand_attend",
    )(slot, count, target, query, acc, stat, *tiles)


NX, NZ, NC = 4, 8, 2
def device(x, z, core):
    return (x % NX * NZ + z % NZ) * NC + core


def seq_pairs(goal):
    return [
        (device(x, z, c), device(*goal(x, z, c)))
        for x in range(NX)
        for z in range(NZ)
        for c in range(NC)
    ]


def local(tokens, w_qkv, item_at, rand_cols, rand_used):
    peers = lax.axis_size("seq")
    assert peers == NX * NZ * NC
    me = lax.axis_index("seq")
    my_x, my_z, my_core = me // (NZ * NC), me // NC % NZ, me % NC
    groups = lax.axis_size("head")
    mine_y = lax.axis_index("head")
    heads, nblocks, rand = rand_cols.shape
    rows = nblocks // peers
    count, depth = tokens.shape
    blk = count // rows
    hd = w_qkv.shape[1] // (3 * heads)
    width = heads * hd
    items = heads * rows
    factor = math.log2(math.e) / math.sqrt(hd)

    asked = rand_cols.reshape(heads, peers, rows, rand).transpose(1, 2, 0, 3)
    asked = asked.reshape(peers, items * rand)
    order = jnp.arange(items * rand, dtype=jnp.int32)
    code = order * items + (order // rand) % heads * rows + asked % rows

    def held_for(holder):
        held = asked // rows == holder
        low = jnp.min(jnp.where(held, code, jnp.int32(1 << 30)), axis=1) % items
        high = jnp.max(jnp.where(held, code, 0), axis=1) % items
        return jnp.stack([low, high], axis=1).reshape(-1)

    far_z = device(my_x, my_z + NZ // 2, my_core)
    tables = (held_for(me), held_for(far_z))
    plane = NX * NC
    spot = jnp.arange(plane, dtype=jnp.int32)
    even = jnp.concatenate([spot[0:2], spot[4:6]])
    odd = jnp.concatenate([spot[2:4], spot[6:8]])
    moves = [(0, spot), (1, spot), (-1, spot), (2, even), (-2, odd)]
    dests = jnp.concatenate(
        [device(at // NC, my_z + move, at % NC) for move, at in moves]
    ).astype(jnp.int32)

    wanted = lax.dynamic_index_in_dim(asked, me, 0, keepdims=False)
    source = wanted // rows
    rank = jnp.sum(
        ((source[:, None] == source[None, :]) & (order[None, :] < order[:, None])).astype(jnp.int32),
        axis=1,
    )
    step = (my_z - source // NC) % NZ
    source_spot = source // (NZ * NC) * NC + source % NC
    my_two = (2 - 4 * (my_x % 2)) % NZ

    def route_kind(step):
        return jnp.where(
            step == 0, 0, jnp.where(step == 1, 1, jnp.where(step == NZ - 1, 2, jnp.where(step == my_two, 3, -1)))
        )

    near_kind = route_kind(step)
    other_kind = route_kind((step + NZ // 2) % NZ)
    half = (near_kind < 0).astype(jnp.int32)
    slot = source_spot * 4 + jnp.where(half == 1, other_kind, near_kind)
    slot = half * (items * rand // 2) + slot * 2 + rank

    my_used = lax.dynamic_slice_in_dim(rand_used, me * rows, rows, axis=1).T.reshape(-1)
    number = jnp.arange(items, dtype=jnp.int32)
    my_item = (number % heads) * nblocks + me * rows + number // heads
    place = jnp.arange(peers * items, dtype=jnp.int32)
    target = jnp.sum(
        jnp.where(item_at[0][None, :] == my_item[:, None], place[None, :] // items, 0), axis=1
    )
    home = (lax.dynamic_slice_in_dim(item_at[0], me * items, items) % nblocks) // rows
    edges = jnp.stack([me == 0, me == peers - 1]).astype(jnp.int32)

    def weight(shift, first, size):
        row = (mine_y + shift) % groups * depth
        return lax.dynamic_slice(w_qkv, (row, jnp.int32(first)), (depth, size))

    def w_pair(shift):
        return weight(shift, width, 2 * width)

    def w_query(shift):
        return weight(shift, 0, width)

    def spread(block, stride):
        holders = range(0, peers, 4 * stride)
        got = [
            lax.ppermute(block, "seq", [(h, h + k * stride) for h in holders]) for k in (1, 2, 3)
        ]
        return block + got[0] + got[1] + got[2]

    onward = [(i, (i + 1) % groups) for i in range(groups)]
    backward = [(b, a) for a, b in onward]

    def ring(part):
        middle = part.shape[0] // 2
        low = lax.ppermute(part, "head", onward)
        high = lax.ppermute(part, "head", backward)
        top = lax.ppermute(low[:middle], "head", onward)
        bottom = lax.ppermute(high[middle:], "head", backward)
        return low, high, top, bottom

    def keys_values(part, low, high, top, bottom):
        middle = part.shape[0] // 2
        total = dot(part, w_pair(0)) + dot(low, w_pair(3)) + dot(high, w_pair(1))
        return jnp.concatenate(
            [
                (total[:middle] + dot(top, w_pair(2))).astype(BF),
                (total[middle:] + dot(bottom, w_pair(2))).astype(BF),
            ],
            axis=0,
        )

    copied = lax.ppermute(tokens, "seq", seq_pairs(lambda x, z, c: (x, z + NZ // 2, c)))
    from_low, from_high, far_top, far_bottom = ring(tokens)
    zero = tokens[:blk]
    zero = jnp.where(me == 0, zero, jnp.zeros_like(zero))
    zero, own_table = lax.optimization_barrier((zero, tables[0]))
    zero = spread(spread(zero, peers // 4), peers // 16)
    zero, _ = lax.optimization_barrier((zero, (from_low, from_high)))
    zero = spread(zero, peers // 64)
    copied = jnp.concatenate([copied, zero], axis=0)
    copied_ring = ring(copied)

    pair = keys_values(tokens, from_low, from_high, far_top, far_bottom)
    up = [(i, i + 1) for i in range(peers - 1)]
    down = [(b, a) for a, b in up]
    before = lax.ppermute(pair[-blk:], "seq", up)
    after = lax.ppermute(pair[:blk], "seq", down)

    planes = [[device(x, z, c) for x in range(NX) for c in range(NC)] for z in range(NZ)]

    def along_z(part, move):
        return lax.ppermute(part, "seq", seq_pairs(lambda x, z, c: (x, z + move, c))) if move else part

    shares = [at.shape[0] for _, at in moves]
    steps = [move for move, _ in moves]
    whole = list(range(NX * NC))
    spots = [whole, whole, whole, [0, 1, 4, 5], [2, 3, 6, 7]]
    places = [[(g, min(k, 3)) for g in at] for k, at in enumerate(spots)]

    def pack(table, pair, name):
        return pack_tiles(table, dests, pair, shares, rows, heads, blk, hd, name)

    def shifted(parts):
        return [along_z(part, move) for part, move in zip(parts, steps)]

    def in_plane(block):
        got = lax.all_to_all(
            block, "seq", split_axis=0, concat_axis=0, axis_index_groups=planes, tiled=True
        )
        return got.reshape(-1, blk, 2 * hd)

    own_parts = shifted(pack(own_table, pair, "pack_own"))
    copied_pair = keys_values(copied, *copied_ring)
    copied_parts = pack(tables[1], copied_pair, "pack_copied")
    own_parts, copied_parts = lax.optimization_barrier((own_parts, copied_parts))
    copied_parts = shifted(copied_parts)
    own_tiles = in_plane(merge_parts(own_parts, places, "merge_own"))

    around = jnp.concatenate([before, pair, after], axis=0)
    far = jnp.concatenate([far_top, far_bottom], axis=0)
    query = dot(far, w_query(2)) + dot(tokens, w_query(0))
    query = (query + dot(from_low, w_query(3)) + dot(from_high, w_query(1))).astype(BF)
    first = copied_pair[count:]
    acc, stat = near_attend(edges, query, around, first, rows, heads, blk, hd, factor)
    copied_parts, acc, stat = lax.optimization_barrier((copied_parts, acc, stat))
    copied_tiles = in_plane(merge_parts(copied_parts, places, "merge_copied"))
    done = rand_attend(
        slot, my_used, target, query, (own_tiles, copied_tiles), acc, stat,
        rows, heads, blk, hd, rand, peers, factor,
    )
    back = lax.all_to_all(done, "seq", split_axis=0, concat_axis=0, tiled=True)
    return take_tiles(home, back)[None]


def solution(mesh):
    return jax.shard_map(
        local,
        mesh=mesh,
        in_specs=(
            P("seq", "head"),
            P(None, "head"),
            P("head", None),
            P("head", None, None),
            P("head", None),
        ),
        out_specs=P("head", "seq", None, None),
        check_vma=False,
    )
```

```python
import math

import jax
import jax.numpy as jnp
from jax import lax
from jax.experimental import pallas as pl
from jax.experimental.pallas import tpu as pltpu
from jax.sharding import PartitionSpec as P

NEG = -1e30
BF = jnp.bfloat16
F32 = jnp.float32
VMEM_BYTES = 48 << 20


def dot(a, b):
    return jnp.dot(a, b, preferred_element_type=F32)


def dot_t(a, b):
    return lax.dot_general(a, b, (((1,), (1,)), ((), ())), preferred_element_type=F32)


def params():
    return pltpu.CompilerParams(vmem_limit_bytes=VMEM_BYTES)


def pack_tiles(table, dests, pair, shares, rows, heads, blk, hd, name):
    width = heads * hd
    ends = [(k, i) for k, share in enumerate(shares) for i in range(share)]

    def kernel(table_ref, dest_ref, pair_ref, *refs):
        outs = refs[: len(shares)]
        tiles, sems = refs[len(shares) :]

        def copy(n, t):
            k, i = ends[n]
            tile = table_ref[2 * dest_ref[n] + t]
            return pltpu.make_async_copy(tiles.at[tile], outs[k].at[i, t], sems.at[2 * n + t])

        for e in range(heads):
            for r in range(rows):
                at = slice(r * blk, (r + 1) * blk)
                tiles[e * rows + r, :, :hd] = pair_ref[at, e * hd : (e + 1) * hd]
                tiles[e * rows + r, :, hd:] = pair_ref[at, width + e * hd : width + (e + 1) * hd].T
        for n in range(len(ends)):
            for t in range(2):
                copy(n, t).start()
        for n in range(len(ends)):
            for t in range(2):
                copy(n, t).wait()

    anywhere = pl.BlockSpec(memory_space=pl.ANY)
    return pl.pallas_call(
        kernel,
        out_shape=[jax.ShapeDtypeStruct((share, 2, blk, 2 * hd), BF) for share in shares],
        grid_spec=pltpu.PrefetchScalarGridSpec(
            num_scalar_prefetch=2,
            grid=(1,),
            in_specs=[pl.BlockSpec(memory_space=pltpu.VMEM)],
            out_specs=[anywhere] * len(shares),
            scratch_shapes=[
                pltpu.VMEM((rows * heads, blk, 2 * hd), BF),
                pltpu.SemaphoreType.DMA((2 * len(ends),)),
            ],
        ),
        compiler_params=params(),
        name=name,
    )(table, dests, pair)


def merge_parts(parts, places, name):
    count = sum(len(at) for at in places)
    rest = parts[0].shape[1:]

    def kernel(*refs):
        out_ref, sems = refs[len(parts) :]
        copies = []
        for ref, at in zip(refs, places):
            for i, (g, a) in enumerate(at):
                copies.append(
                    pltpu.make_async_copy(ref.at[i], out_ref.at[g, a], sems.at[len(copies)])
                )
        for copy in copies:
            copy.start()
        for copy in copies:
            copy.wait()

    return pl.pallas_call(
        kernel,
        out_shape=jax.ShapeDtypeStruct((count // 4, 4, *rest), parts[0].dtype),
        in_specs=[pl.BlockSpec(memory_space=pltpu.VMEM)] * len(parts),
        out_specs=pl.BlockSpec(memory_space=pltpu.HBM),
        scratch_shapes=[pltpu.SemaphoreType.DMA((count,))],
        compiler_params=params(),
        name=name,
    )(*parts)


def take_tiles(index, tiles):
    count = index.shape[0]

    def kernel(index_ref, in_ref, out_ref, sems):
        def copy(i):
            return pltpu.make_async_copy(in_ref.at[index_ref[i]], out_ref.at[i], sems.at[i])

        for i in range(count):
            copy(i).start()
        for i in range(count):
            copy(i).wait()

    return pl.pallas_call(
        kernel,
        out_shape=jax.ShapeDtypeStruct((count, *tiles.shape[1:]), tiles.dtype),
        grid_spec=pltpu.PrefetchScalarGridSpec(
            num_scalar_prefetch=1,
            grid=(1,),
            in_specs=[pl.BlockSpec(memory_space=pltpu.VMEM)],
            out_specs=pl.BlockSpec(memory_space=pl.ANY),
            scratch_shapes=[pltpu.SemaphoreType.DMA((count,))],
        ),
        compiler_params=params(),
        name="take_tiles",
    )(index, tiles)


def near_attend(edges, query, around, first, rows, heads, blk, hd, factor):
    width = heads * hd

    def kernel(edge_ref, q_ref, kv_ref, first_ref, acc_ref, stat_ref):
        r = pl.program_id(0)
        window = pl.ds(pl.multiple_of(r * blk, blk), 3 * blk)
        key = lax.broadcasted_iota(jnp.int32, (3 * blk, blk), 0)
        low = jnp.where((r == 0) & (edge_ref[0] == 1), blk, 0)
        high = jnp.where((r == rows - 1) & (edge_ref[1] == 1), 2 * blk, 3 * blk)
        usable = (key >= low) & (key < high)
        row = lax.broadcasted_iota(jnp.int32, (8, blk), 0)
        for e in range(heads):
            keys = slice(e * hd, (e + 1) * hd)
            values = slice(width + e * hd, width + (e + 1) * hd)
            q = q_ref[:, keys]
            near = jnp.where(usable, dot_t(kv_ref[window, keys], q) * factor, NEG)
            glob = dot_t(first_ref[:, keys], q) * factor
            top = jnp.maximum(
                jnp.max(near, axis=0, keepdims=True), jnp.max(glob, axis=0, keepdims=True)
            )
            near = jnp.exp2(near - top)
            glob = jnp.exp2(glob - top)
            total = jnp.sum(near, axis=0, keepdims=True) + jnp.sum(glob, axis=0, keepdims=True)
            acc_ref[e] = dot(kv_ref[window, values].T, near.astype(BF)) + dot(
                first_ref[:, values].T, glob.astype(BF)
            )
            stat_ref[e] = jnp.where(row == 0, top, total)

    return pl.pallas_call(
        kernel,
        out_shape=(
            jax.ShapeDtypeStruct((rows * heads, hd, blk), F32),
            jax.ShapeDtypeStruct((rows * heads, 8, blk), F32),
        ),
        grid_spec=pltpu.PrefetchScalarGridSpec(
            num_scalar_prefetch=1,
            grid=(rows,),
            in_specs=[
                pl.BlockSpec((blk, width), lambda r, s: (r, 0)),
                pl.BlockSpec(around.shape, lambda r, s: (0, 0)),
                pl.BlockSpec(first.shape, lambda r, s: (0, 0)),
            ],
            out_specs=(
                pl.BlockSpec((heads, hd, blk), lambda r, s: (r, 0, 0)),
                pl.BlockSpec((heads, 8, blk), lambda r, s: (r, 0, 0)),
            ),
        ),
        compiler_params=params(),
        name="near_attend",
    )(edges, query, around, first)


def rand_attend(slot, count, target, query, tiles, acc, stat, rows, heads, blk, hd, rand, peers, factor):
    items = rows * heads
    slots = items * rand
    share = slots // len(tiles)

    def kernel(slot_ref, count_ref, target_ref, q_ref, acc_ref, stat_ref, *refs):
        out_ref, buffer, done, in_sems, out_sems = refs[len(tiles) :]
        copies = [
            pltpu.make_async_copy(refs[n], buffer.at[pl.ds(n * share, share)], in_sems.at[n])
            for n in range(len(tiles))
        ]

        def deliver(i):
            return pltpu.make_async_copy(done.at[i], out_ref.at[target_ref[i]], out_sems.at[i])

        for copy in copies:
            copy.start()
        key = lax.broadcasted_iota(jnp.int32, (rand * blk, blk), 0)

        def step(r, carry):
            first = r * heads
            at = pl.ds(pl.multiple_of(r * blk, blk), blk)
            each = range(heads)
            places = [[slot_ref[(first + e) * rand + j] for j in range(rand)] for e in each]
            keys = [jnp.concatenate([buffer[p, :, :hd] for p in places[e]], axis=0) for e in each]
            scores = [dot_t(keys[e], q_ref[at, e * hd : (e + 1) * hd]) for e in each]
            scores = [
                jnp.where(key < count_ref[first + e] * blk, scores[e] * factor, NEG) for e in each
            ]
            top0 = [stat_ref[first + e, 0:1] for e in each]
            total0 = [stat_ref[first + e, 1:2] for e in each]
            top = [jnp.maximum(jnp.max(scores[e], axis=0, keepdims=True), top0[e]) for e in each]
            keep = [jnp.exp2(top0[e] - top[e]) for e in each]
            expo = [jnp.exp2(scores[e] - top[e]) for e in each]
            total = [total0[e] * keep[e] + jnp.sum(expo[e], axis=0, keepdims=True) for e in each]
            values = [jnp.concatenate([buffer[p, :, hd:] for p in places[e]], axis=1) for e in each]
            summed = [acc_ref[first + e] * keep[e] + dot(values[e], expo[e].astype(BF)) for e in each]
            for e in each:
                done[first + e] = (summed[e] / total[e]).T.astype(BF)
            for e in each:
                deliver(first + e).start()
            return carry

        for copy in copies:
            copy.wait()
        lax.fori_loop(0, rows, step, 0)
        for i in range(items):
            deliver(i).wait()

    vmem = pl.BlockSpec(memory_space=pltpu.VMEM)
    anywhere = pl.BlockSpec(memory_space=pl.ANY)
    return pl.pallas_call(
        kernel,
        out_shape=jax.ShapeDtypeStruct((peers, blk, hd), BF),
        grid_spec=pltpu.PrefetchScalarGridSpec(
            num_scalar_prefetch=3,
            grid=(1,),
            in_specs=[vmem, vmem, vmem, *[anywhere] * len(tiles)],
            out_specs=pl.BlockSpec(memory_space=pltpu.HBM),
            scratch_shapes=[
                pltpu.VMEM((slots, blk, 2 * hd), BF),
                pltpu.VMEM((items, blk, hd), BF),
                pltpu.SemaphoreType.DMA((len(tiles),)),
                pltpu.SemaphoreType.DMA((items,)),
            ],
        ),
        compiler_params=params(),
        name="rand_attend",
    )(slot, count, target, query, acc, stat, *tiles)


NX, NZ, NC = 4, 8, 2
def device(x, z, core):
    return (x % NX * NZ + z % NZ) * NC + core


def seq_pairs(goal):
    return [
        (device(x, z, c), device(*goal(x, z, c)))
        for x in range(NX)
        for z in range(NZ)
        for c in range(NC)
    ]


def local(tokens, w_qkv, item_at, rand_cols, rand_used):
    peers = lax.axis_size("seq")
    assert peers == NX * NZ * NC
    me = lax.axis_index("seq")
    my_x, my_z, my_core = me // (NZ * NC), me // NC % NZ, me % NC
    groups = lax.axis_size("head")
    mine_y = lax.axis_index("head")
    heads, nblocks, rand = rand_cols.shape
    rows = nblocks // peers
    count, depth = tokens.shape
    blk = count // rows
    hd = w_qkv.shape[1] // (3 * heads)
    width = heads * hd
    items = heads * rows
    factor = math.log2(math.e) / math.sqrt(hd)

    asked = rand_cols.reshape(heads, peers, rows, rand).transpose(1, 2, 0, 3)
    asked = asked.reshape(peers, items * rand)
    order = jnp.arange(items * rand, dtype=jnp.int32)
    code = order * items + (order // rand) % heads * rows + asked % rows

    def held_for(holder):
        held = asked // rows == holder
        low = jnp.min(jnp.where(held, code, jnp.int32(1 << 30)), axis=1) % items
        high = jnp.max(jnp.where(held, code, 0), axis=1) % items
        return jnp.stack([low, high], axis=1).reshape(-1)

    far_z = device(my_x, my_z + NZ // 2, my_core)
    tables = (held_for(me), held_for(far_z))
    plane = NX * NC
    spot = jnp.arange(plane, dtype=jnp.int32)
    even = jnp.concatenate([spot[0:2], spot[4:6]])
    odd = jnp.concatenate([spot[2:4], spot[6:8]])
    moves = [(0, spot), (1, spot), (-1, spot), (2, even), (-2, odd)]
    dests = jnp.concatenate(
        [device(at // NC, my_z + move, at % NC) for move, at in moves]
    ).astype(jnp.int32)

    wanted = lax.dynamic_index_in_dim(asked, me, 0, keepdims=False)
    source = wanted // rows
    rank = jnp.sum(
        ((source[:, None] == source[None, :]) & (order[None, :] < order[:, None])).astype(jnp.int32),
        axis=1,
    )
    step = (my_z - source // NC) % NZ
    source_spot = source // (NZ * NC) * NC + source % NC
    my_two = (2 - 4 * (my_x % 2)) % NZ

    def route_kind(step):
        return jnp.where(
            step == 0, 0, jnp.where(step == 1, 1, jnp.where(step == NZ - 1, 2, jnp.where(step == my_two, 3, -1)))
        )

    near_kind = route_kind(step)
    other_kind = route_kind((step + NZ // 2) % NZ)
    half = (near_kind < 0).astype(jnp.int32)
    slot = source_spot * 4 + jnp.where(half == 1, other_kind, near_kind)
    slot = half * (items * rand // 2) + slot * 2 + rank

    my_used = lax.dynamic_slice_in_dim(rand_used, me * rows, rows, axis=1).T.reshape(-1)
    number = jnp.arange(items, dtype=jnp.int32)
    my_item = (number % heads) * nblocks + me * rows + number // heads
    place = jnp.arange(peers * items, dtype=jnp.int32)
    target = jnp.sum(
        jnp.where(item_at[0][None, :] == my_item[:, None], place[None, :] // items, 0), axis=1
    )
    home = (lax.dynamic_slice_in_dim(item_at[0], me * items, items) % nblocks) // rows
    edges = jnp.stack([me == 0, me == peers - 1]).astype(jnp.int32)

    def weight(shift, first, size):
        row = (mine_y + shift) % groups * depth
        return lax.dynamic_slice(w_qkv, (row, jnp.int32(first)), (depth, size))

    def w_pair(shift):
        return weight(shift, width, 2 * width)

    def w_query(shift):
        return weight(shift, 0, width)

    def spread(block, stride):
        holders = range(0, peers, 4 * stride)
        got = [
            lax.ppermute(block, "seq", [(h, h + k * stride) for h in holders]) for k in (1, 2, 3)
        ]
        return block + got[0] + got[1] + got[2]

    onward = [(i, (i + 1) % groups) for i in range(groups)]
    backward = [(b, a) for a, b in onward]

    def ring(part):
        middle = part.shape[0] // 2
        low = lax.ppermute(part, "head", onward)
        high = lax.ppermute(part, "head", backward)
        top = lax.ppermute(low[:middle], "head", onward)
        bottom = lax.ppermute(high[middle:], "head", backward)
        return low, high, top, bottom

    def keys_values(part, low, high, top, bottom):
        middle = part.shape[0] // 2
        total = dot(part, w_pair(0)) + dot(low, w_pair(3)) + dot(high, w_pair(1))
        return jnp.concatenate(
            [
                (total[:middle] + dot(top, w_pair(2))).astype(BF),
                (total[middle:] + dot(bottom, w_pair(2))).astype(BF),
            ],
            axis=0,
        )

    from_low, from_high, far_top, far_bottom = ring(tokens)
    zero = tokens[:blk]
    zero = jnp.where(me == 0, zero, jnp.zeros_like(zero))
    zero = spread(spread(spread(zero, peers // 4), peers // 16), peers // 64)
    copied, zero = lax.optimization_barrier((tokens, zero))
    copied = lax.ppermute(copied, "seq", seq_pairs(lambda x, z, c: (x, z + NZ // 2, c)))
    copied = jnp.concatenate([copied, zero], axis=0)
    copied_ring = ring(copied)

    pair = keys_values(tokens, from_low, from_high, far_top, far_bottom)
    up = [(i, i + 1) for i in range(peers - 1)]
    down = [(b, a) for a, b in up]
    before = lax.ppermute(pair[-blk:], "seq", up)
    after = lax.ppermute(pair[:blk], "seq", down)

    planes = [[device(x, z, c) for x in range(NX) for c in range(NC)] for z in range(NZ)]

    def along_z(part, move):
        return lax.ppermute(part, "seq", seq_pairs(lambda x, z, c: (x, z + move, c))) if move else part

    shares = [at.shape[0] for _, at in moves]
    steps = [move for move, _ in moves]
    whole = list(range(NX * NC))
    spots = [whole, whole, whole, [0, 1, 4, 5], [2, 3, 6, 7]]
    places = [[(g, min(k, 3)) for g in at] for k, at in enumerate(spots)]

    def pack(table, pair, name):
        return pack_tiles(table, dests, pair, shares, rows, heads, blk, hd, name)

    def shifted(parts):
        return [along_z(part, move) for part, move in zip(parts, steps)]

    def in_plane(block):
        got = lax.all_to_all(
            block, "seq", split_axis=0, concat_axis=0, axis_index_groups=planes, tiled=True
        )
        return got.reshape(-1, blk, 2 * hd)

    own_parts = shifted(pack(tables[0], pair, "pack_own"))
    copied_pair = keys_values(copied, *copied_ring)
    copied_parts = pack(tables[1], copied_pair, "pack_copied")
    own_parts, _ = lax.optimization_barrier((own_parts, copied_parts))
    copied_parts = shifted(copied_parts)
    own_tiles = in_plane(merge_parts(own_parts, places, "merge_own"))

    around = jnp.concatenate([before, pair, after], axis=0)
    far = jnp.concatenate([far_top, far_bottom], axis=0)
    query = dot(far, w_query(2)) + dot(tokens, w_query(0))
    query = (query + dot(from_low, w_query(3)) + dot(from_high, w_query(1))).astype(BF)
    first = copied_pair[count:]
    acc, stat = near_attend(edges, query, around, first, rows, heads, blk, hd, factor)
    copied_parts, acc, stat = lax.optimization_barrier((copied_parts, acc, stat))
    copied_tiles = in_plane(merge_parts(copied_parts, places, "merge_copied"))
    done = rand_attend(
        slot, my_used, target, query, (own_tiles, copied_tiles), acc, stat,
        rows, heads, blk, hd, rand, peers, factor,
    )
    back = lax.all_to_all(done, "seq", split_axis=0, concat_axis=0, tiled=True)
    return take_tiles(home, back)[None]


def solution(mesh):
    return jax.shard_map(
        local,
        mesh=mesh,
        in_specs=(
            P("seq", "head"),
            P(None, "head"),
            P("head", None),
            P("head", None, None),
            P("head", None),
        ),
        out_specs=P("head", "seq", None, None),
        check_vma=False,
    )
```

```python
import math

import jax
import jax.numpy as jnp
from jax import lax
from jax.experimental import pallas as pl
from jax.experimental.pallas import tpu as pltpu
from jax.sharding import PartitionSpec as P

NEG = -1e30
BF = jnp.bfloat16
F32 = jnp.float32
VMEM_BYTES = 48 << 20


def dot(a, b):
    return jnp.dot(a, b, preferred_element_type=F32)


def dot_t(a, b):
    return lax.dot_general(a, b, (((1,), (1,)), ((), ())), preferred_element_type=F32)


def params():
    return pltpu.CompilerParams(vmem_limit_bytes=VMEM_BYTES)


def pack_tiles(table, dests, pair, shares, rows, heads, blk, hd, name):
    width = heads * hd
    ends = [(k, i) for k, share in enumerate(shares) for i in range(share)]

    def kernel(table_ref, dest_ref, pair_ref, *refs):
        outs = refs[: len(shares)]
        tiles, sems = refs[len(shares) :]

        def copy(n, t):
            k, i = ends[n]
            tile = table_ref[2 * dest_ref[n] + t]
            return pltpu.make_async_copy(tiles.at[tile], outs[k].at[i, t], sems.at[2 * n + t])

        for e in range(heads):
            for r in range(rows):
                at = slice(r * blk, (r + 1) * blk)
                tiles[e * rows + r, :, :hd] = pair_ref[at, e * hd : (e + 1) * hd]
                tiles[e * rows + r, :, hd:] = pair_ref[at, width + e * hd : width + (e + 1) * hd].T
        for n in range(len(ends)):
            for t in range(2):
                copy(n, t).start()
        for n in range(len(ends)):
            for t in range(2):
                copy(n, t).wait()

    anywhere = pl.BlockSpec(memory_space=pl.ANY)
    return pl.pallas_call(
        kernel,
        out_shape=[jax.ShapeDtypeStruct((share, 2, blk, 2 * hd), BF) for share in shares],
        grid_spec=pltpu.PrefetchScalarGridSpec(
            num_scalar_prefetch=2,
            grid=(1,),
            in_specs=[pl.BlockSpec(memory_space=pltpu.VMEM)],
            out_specs=[anywhere] * len(shares),
            scratch_shapes=[
                pltpu.VMEM((rows * heads, blk, 2 * hd), BF),
                pltpu.SemaphoreType.DMA((2 * len(ends),)),
            ],
        ),
        compiler_params=params(),
        name=name,
    )(table, dests, pair)


def merge_parts(parts, places, name):
    count = sum(len(at) for at in places)
    rest = parts[0].shape[1:]

    def kernel(*refs):
        out_ref, sems = refs[len(parts) :]
        copies = []
        for ref, at in zip(refs, places):
            for i, (g, a) in enumerate(at):
                copies.append(
                    pltpu.make_async_copy(ref.at[i], out_ref.at[g, a], sems.at[len(copies)])
                )
        for copy in copies:
            copy.start()
        for copy in copies:
            copy.wait()

    return pl.pallas_call(
        kernel,
        out_shape=jax.ShapeDtypeStruct((count // 4, 4, *rest), parts[0].dtype),
        in_specs=[pl.BlockSpec(memory_space=pltpu.VMEM)] * len(parts),
        out_specs=pl.BlockSpec(memory_space=pltpu.HBM),
        scratch_shapes=[pltpu.SemaphoreType.DMA((count,))],
        compiler_params=params(),
        name=name,
    )(*parts)


def take_tiles(index, tiles):
    count = index.shape[0]

    def kernel(index_ref, in_ref, out_ref, sems):
        def copy(i):
            return pltpu.make_async_copy(in_ref.at[index_ref[i]], out_ref.at[i], sems.at[i])

        for i in range(count):
            copy(i).start()
        for i in range(count):
            copy(i).wait()

    return pl.pallas_call(
        kernel,
        out_shape=jax.ShapeDtypeStruct((count, *tiles.shape[1:]), tiles.dtype),
        grid_spec=pltpu.PrefetchScalarGridSpec(
            num_scalar_prefetch=1,
            grid=(1,),
            in_specs=[pl.BlockSpec(memory_space=pltpu.VMEM)],
            out_specs=pl.BlockSpec(memory_space=pl.ANY),
            scratch_shapes=[pltpu.SemaphoreType.DMA((count,))],
        ),
        compiler_params=params(),
        name="take_tiles",
    )(index, tiles)


def near_attend(edges, query, around, first, rows, heads, blk, hd, factor):
    width = heads * hd

    def kernel(edge_ref, q_ref, kv_ref, first_ref, acc_ref, stat_ref):
        r = pl.program_id(0)
        window = pl.ds(pl.multiple_of(r * blk, blk), 3 * blk)
        key = lax.broadcasted_iota(jnp.int32, (3 * blk, blk), 0)
        low = jnp.where((r == 0) & (edge_ref[0] == 1), blk, 0)
        high = jnp.where((r == rows - 1) & (edge_ref[1] == 1), 2 * blk, 3 * blk)
        usable = (key >= low) & (key < high)
        row = lax.broadcasted_iota(jnp.int32, (8, blk), 0)
        for e in range(heads):
            keys = slice(e * hd, (e + 1) * hd)
            values = slice(width + e * hd, width + (e + 1) * hd)
            q = q_ref[:, keys]
            near = jnp.where(usable, dot_t(kv_ref[window, keys], q) * factor, NEG)
            glob = dot_t(first_ref[:, keys], q) * factor
            top = jnp.maximum(
                jnp.max(near, axis=0, keepdims=True), jnp.max(glob, axis=0, keepdims=True)
            )
            near = jnp.exp2(near - top)
            glob = jnp.exp2(glob - top)
            total = jnp.sum(near, axis=0, keepdims=True) + jnp.sum(glob, axis=0, keepdims=True)
            acc_ref[e] = dot(kv_ref[window, values].T, near.astype(BF)) + dot(
                first_ref[:, values].T, glob.astype(BF)
            )
            stat_ref[e] = jnp.where(row == 0, top, total)

    return pl.pallas_call(
        kernel,
        out_shape=(
            jax.ShapeDtypeStruct((rows * heads, hd, blk), F32),
            jax.ShapeDtypeStruct((rows * heads, 8, blk), F32),
        ),
        grid_spec=pltpu.PrefetchScalarGridSpec(
            num_scalar_prefetch=1,
            grid=(rows,),
            in_specs=[
                pl.BlockSpec((blk, width), lambda r, s: (r, 0)),
                pl.BlockSpec(around.shape, lambda r, s: (0, 0)),
                pl.BlockSpec(first.shape, lambda r, s: (0, 0)),
            ],
            out_specs=(
                pl.BlockSpec((heads, hd, blk), lambda r, s: (r, 0, 0)),
                pl.BlockSpec((heads, 8, blk), lambda r, s: (r, 0, 0)),
            ),
        ),
        compiler_params=params(),
        name="near_attend",
    )(edges, query, around, first)


def rand_attend(slot, count, target, query, tiles, acc, stat, rows, heads, blk, hd, rand, peers, factor):
    items = rows * heads
    slots = items * rand
    share = slots // len(tiles)

    def kernel(slot_ref, count_ref, target_ref, q_ref, acc_ref, stat_ref, *refs):
        out_ref, buffer, done, in_sems, out_sems = refs[len(tiles) :]
        copies = [
            pltpu.make_async_copy(refs[n], buffer.at[pl.ds(n * share, share)], in_sems.at[n])
            for n in range(len(tiles))
        ]

        def deliver(i):
            return pltpu.make_async_copy(done.at[i], out_ref.at[target_ref[i]], out_sems.at[i])

        for copy in copies:
            copy.start()
        key = lax.broadcasted_iota(jnp.int32, (rand * blk, blk), 0)

        def step(r, carry):
            first = r * heads
            at = pl.ds(pl.multiple_of(r * blk, blk), blk)
            each = range(heads)
            places = [[slot_ref[(first + e) * rand + j] for j in range(rand)] for e in each]
            keys = [jnp.concatenate([buffer[p, :, :hd] for p in places[e]], axis=0) for e in each]
            scores = [dot_t(keys[e], q_ref[at, e * hd : (e + 1) * hd]) for e in each]
            scores = [
                jnp.where(key < count_ref[first + e] * blk, scores[e] * factor, NEG) for e in each
            ]
            top0 = [stat_ref[first + e, 0:1] for e in each]
            total0 = [stat_ref[first + e, 1:2] for e in each]
            top = [jnp.maximum(jnp.max(scores[e], axis=0, keepdims=True), top0[e]) for e in each]
            keep = [jnp.exp2(top0[e] - top[e]) for e in each]
            expo = [jnp.exp2(scores[e] - top[e]) for e in each]
            total = [total0[e] * keep[e] + jnp.sum(expo[e], axis=0, keepdims=True) for e in each]
            values = [jnp.concatenate([buffer[p, :, hd:] for p in places[e]], axis=1) for e in each]
            summed = [acc_ref[first + e] * keep[e] + dot(values[e], expo[e].astype(BF)) for e in each]
            for e in each:
                done[first + e] = (summed[e] / total[e]).T.astype(BF)
            for e in each:
                deliver(first + e).start()
            return carry

        for copy in copies:
            copy.wait()
        lax.fori_loop(0, rows, step, 0)
        for i in range(items):
            deliver(i).wait()

    vmem = pl.BlockSpec(memory_space=pltpu.VMEM)
    anywhere = pl.BlockSpec(memory_space=pl.ANY)
    return pl.pallas_call(
        kernel,
        out_shape=jax.ShapeDtypeStruct((peers, blk, hd), BF),
        grid_spec=pltpu.PrefetchScalarGridSpec(
            num_scalar_prefetch=3,
            grid=(1,),
            in_specs=[vmem, vmem, vmem, *[anywhere] * len(tiles)],
            out_specs=pl.BlockSpec(memory_space=pltpu.HBM),
            scratch_shapes=[
                pltpu.VMEM((slots, blk, 2 * hd), BF),
                pltpu.VMEM((items, blk, hd), BF),
                pltpu.SemaphoreType.DMA((len(tiles),)),
                pltpu.SemaphoreType.DMA((items,)),
            ],
        ),
        compiler_params=params(),
        name="rand_attend",
    )(slot, count, target, query, acc, stat, *tiles)


NX, NZ, NC = 4, 8, 2
def device(x, z, core):
    return (x % NX * NZ + z % NZ) * NC + core


def seq_pairs(goal):
    return [
        (device(x, z, c), device(*goal(x, z, c)))
        for x in range(NX)
        for z in range(NZ)
        for c in range(NC)
    ]


def local(tokens, w_qkv, item_at, rand_cols, rand_used):
    peers = lax.axis_size("seq")
    assert peers == NX * NZ * NC
    me = lax.axis_index("seq")
    my_x, my_z, my_core = me // (NZ * NC), me // NC % NZ, me % NC
    groups = lax.axis_size("head")
    mine_y = lax.axis_index("head")
    heads, nblocks, rand = rand_cols.shape
    rows = nblocks // peers
    count, depth = tokens.shape
    blk = count // rows
    hd = w_qkv.shape[1] // (3 * heads)
    width = heads * hd
    items = heads * rows
    factor = math.log2(math.e) / math.sqrt(hd)

    asked = rand_cols.reshape(heads, peers, rows, rand).transpose(1, 2, 0, 3)
    asked = asked.reshape(peers, items * rand)
    order = jnp.arange(items * rand, dtype=jnp.int32)
    code = order * items + (order // rand) % heads * rows + asked % rows

    def held_for(holder):
        held = asked // rows == holder
        low = jnp.min(jnp.where(held, code, jnp.int32(1 << 30)), axis=1) % items
        high = jnp.max(jnp.where(held, code, 0), axis=1) % items
        return jnp.stack([low, high], axis=1).reshape(-1)

    far_z = device(my_x, my_z + NZ // 2, my_core)
    tables = (held_for(me), held_for(far_z))
    plane = NX * NC
    spot = jnp.arange(plane, dtype=jnp.int32)
    even = jnp.concatenate([spot[0:2], spot[4:6]])
    odd = jnp.concatenate([spot[2:4], spot[6:8]])
    moves = [(0, spot), (1, spot), (-1, spot), (2, even), (-2, odd)]
    dests = jnp.concatenate(
        [device(at // NC, my_z + move, at % NC) for move, at in moves]
    ).astype(jnp.int32)

    wanted = lax.dynamic_index_in_dim(asked, me, 0, keepdims=False)
    source = wanted // rows
    rank = jnp.sum(
        ((source[:, None] == source[None, :]) & (order[None, :] < order[:, None])).astype(jnp.int32),
        axis=1,
    )
    step = (my_z - source // NC) % NZ
    source_spot = source // (NZ * NC) * NC + source % NC
    my_two = (2 - 4 * (my_x % 2)) % NZ

    def route_kind(step):
        return jnp.where(
            step == 0, 0, jnp.where(step == 1, 1, jnp.where(step == NZ - 1, 2, jnp.where(step == my_two, 3, -1)))
        )

    near_kind = route_kind(step)
    other_kind = route_kind((step + NZ // 2) % NZ)
    half = (near_kind < 0).astype(jnp.int32)
    slot = source_spot * 4 + jnp.where(half == 1, other_kind, near_kind)
    slot = half * (items * rand // 2) + slot * 2 + rank

    my_used = lax.dynamic_slice_in_dim(rand_used, me * rows, rows, axis=1).T.reshape(-1)
    number = jnp.arange(items, dtype=jnp.int32)
    my_item = (number % heads) * nblocks + me * rows + number // heads
    place = jnp.arange(peers * items, dtype=jnp.int32)
    target = jnp.sum(
        jnp.where(item_at[0][None, :] == my_item[:, None], place[None, :] // items, 0), axis=1
    )
    home = (lax.dynamic_slice_in_dim(item_at[0], me * items, items) % nblocks) // rows
    edges = jnp.stack([me == 0, me == peers - 1]).astype(jnp.int32)

    def weight(shift, first, size):
        row = (mine_y + shift) % groups * depth
        return lax.dynamic_slice(w_qkv, (row, jnp.int32(first)), (depth, size))

    def w_pair(shift):
        return weight(shift, width, 2 * width)

    def w_query(shift):
        return weight(shift, 0, width)

    def spread(block, holders, stride):
        got = [lax.ppermute(block, "seq", [(h, h + k * stride) for h in holders]) for k in (1, 2, 3)]
        return block + got[0] + got[1] + got[2]

    onward = [(i, (i + 1) % groups) for i in range(groups)]
    backward = [(b, a) for a, b in onward]

    def ring(part):
        middle = part.shape[0] // 2
        low = lax.ppermute(part, "head", onward)
        high = lax.ppermute(part, "head", backward)
        top = lax.ppermute(low[:middle], "head", onward)
        bottom = lax.ppermute(high[middle:], "head", backward)
        return low, high, top, bottom

    def keys_values(part, low, high, top, bottom):
        middle = part.shape[0] // 2
        total = dot(part, w_pair(0)) + dot(low, w_pair(3)) + dot(high, w_pair(1))
        return jnp.concatenate(
            [
                (total[:middle] + dot(top, w_pair(2))).astype(BF),
                (total[middle:] + dot(bottom, w_pair(2))).astype(BF),
            ],
            axis=0,
        )

    from_low, from_high, far_top, far_bottom = ring(tokens)
    zero = tokens[:blk]
    zero = jnp.where(me == 0, zero, jnp.zeros_like(zero))
    zero = spread(spread(zero, [0], 4), range(0, 16, 4), 1)
    copied, zero = lax.optimization_barrier((tokens, zero))
    copied = lax.ppermute(copied, "seq", seq_pairs(lambda x, z, c: (x, z + NZ // 2, c)))
    zero = spread(zero, range(16), 16)

    pair = keys_values(tokens, from_low, from_high, far_top, far_bottom)
    up = [(i, i + 1) for i in range(peers - 1)]
    down = [(b, a) for a, b in up]
    before = lax.ppermute(pair[-blk:], "seq", up)
    after = lax.ppermute(pair[:blk], "seq", down)

    planes = [[device(x, z, c) for x in range(NX) for c in range(NC)] for z in range(NZ)]

    def along_z(part, move):
        return lax.ppermute(part, "seq", seq_pairs(lambda x, z, c: (x, z + move, c))) if move else part

    shares = [at.shape[0] for _, at in moves]
    steps = [move for move, _ in moves]
    whole = list(range(NX * NC))
    spots = [whole, whole, whole, [0, 1, 4, 5], [2, 3, 6, 7]]
    places = [[(g, min(k, 3)) for g in at] for k, at in enumerate(spots)]

    def pack(table, pair, name):
        return pack_tiles(table, dests, pair, shares, rows, heads, blk, hd, name)

    def shifted(parts):
        return [along_z(part, move) for part, move in zip(parts, steps)]

    def in_plane(block):
        got = lax.all_to_all(
            block, "seq", split_axis=0, concat_axis=0, axis_index_groups=planes, tiled=True
        )
        return got.reshape(-1, blk, 2 * hd)

    own_parts = pack(tables[0], pair, "pack_own")
    copied, zero, _ = lax.optimization_barrier((copied, zero, own_parts))
    own_parts = shifted(own_parts)
    copied = jnp.concatenate([copied, zero], axis=0)
    copied_ring = ring(copied)
    copied_pair = keys_values(copied, *copied_ring)
    copied_parts = pack(tables[1], copied_pair, "pack_copied")
    own_parts, _ = lax.optimization_barrier((own_parts, copied_parts))
    copied_parts = shifted(copied_parts)
    own_tiles = in_plane(merge_parts(own_parts, places, "merge_own"))

    around = jnp.concatenate([before, pair, after], axis=0)
    far = jnp.concatenate([far_top, far_bottom], axis=0)
    query = dot(far, w_query(2)) + dot(tokens, w_query(0))
    query = (query + dot(from_low, w_query(3)) + dot(from_high, w_query(1))).astype(BF)
    first = copied_pair[count:]
    acc, stat = near_attend(edges, query, around, first, rows, heads, blk, hd, factor)
    copied_parts, acc, stat = lax.optimization_barrier((copied_parts, acc, stat))
    copied_tiles = in_plane(merge_parts(copied_parts, places, "merge_copied"))
    done = rand_attend(
        slot, my_used, target, query, (own_tiles, copied_tiles), acc, stat,
        rows, heads, blk, hd, rand, peers, factor,
    )
    back = lax.all_to_all(done, "seq", split_axis=0, concat_axis=0, tiled=True)
    return take_tiles(home, back)[None]


def solution(mesh):
    return jax.shard_map(
        local,
        mesh=mesh,
        in_specs=(
            P("seq", "head"),
            P(None, "head"),
            P("head", None),
            P("head", None, None),
            P("head", None),
        ),
        out_specs=P("head", "seq", None, None),
        check_vma=False,
    )
```

```python
import math

import jax
import jax.numpy as jnp
from jax import lax
from jax.experimental import pallas as pl
from jax.experimental.pallas import tpu as pltpu
from jax.sharding import PartitionSpec as P

NEG = -1e30
BF = jnp.bfloat16
F32 = jnp.float32
VMEM_BYTES = 48 << 20


def dot(a, b):
    return jnp.dot(a, b, preferred_element_type=F32)


def dot_t(a, b):
    return lax.dot_general(a, b, (((1,), (1,)), ((), ())), preferred_element_type=F32)


def params():
    return pltpu.CompilerParams(vmem_limit_bytes=VMEM_BYTES)


def pack_tiles(table, dests, pair, shares, rows, heads, blk, hd, name):
    width = heads * hd
    ends = [(k, i) for k, share in enumerate(shares) for i in range(share)]

    def kernel(table_ref, dest_ref, pair_ref, *refs):
        outs = refs[: len(shares)]
        tiles, sems = refs[len(shares) :]

        def copy(n, t):
            k, i = ends[n]
            tile = table_ref[2 * dest_ref[n] + t]
            return pltpu.make_async_copy(tiles.at[tile], outs[k].at[i, t], sems.at[2 * n + t])

        for e in range(heads):
            for r in range(rows):
                at = slice(r * blk, (r + 1) * blk)
                tiles[e * rows + r, :, :hd] = pair_ref[at, e * hd : (e + 1) * hd]
                tiles[e * rows + r, :, hd:] = pair_ref[at, width + e * hd : width + (e + 1) * hd].T
        for n in range(len(ends)):
            for t in range(2):
                copy(n, t).start()
        for n in range(len(ends)):
            for t in range(2):
                copy(n, t).wait()

    anywhere = pl.BlockSpec(memory_space=pl.ANY)
    return pl.pallas_call(
        kernel,
        out_shape=[jax.ShapeDtypeStruct((share, 2, blk, 2 * hd), BF) for share in shares],
        grid_spec=pltpu.PrefetchScalarGridSpec(
            num_scalar_prefetch=2,
            grid=(1,),
            in_specs=[pl.BlockSpec(memory_space=pltpu.VMEM)],
            out_specs=[anywhere] * len(shares),
            scratch_shapes=[
                pltpu.VMEM((rows * heads, blk, 2 * hd), BF),
                pltpu.SemaphoreType.DMA((2 * len(ends),)),
            ],
        ),
        compiler_params=params(),
        name=name,
    )(table, dests, pair)


def merge_parts(parts, places, name):
    count = sum(len(at) for at in places)
    rest = parts[0].shape[1:]

    def kernel(*refs):
        out_ref, sems = refs[len(parts) :]
        copies = []
        for ref, at in zip(refs, places):
            for i, (g, a) in enumerate(at):
                copies.append(
                    pltpu.make_async_copy(ref.at[i], out_ref.at[g, a], sems.at[len(copies)])
                )
        for copy in copies:
            copy.start()
        for copy in copies:
            copy.wait()

    return pl.pallas_call(
        kernel,
        out_shape=jax.ShapeDtypeStruct((count // 4, 4, *rest), parts[0].dtype),
        in_specs=[pl.BlockSpec(memory_space=pltpu.VMEM)] * len(parts),
        out_specs=pl.BlockSpec(memory_space=pltpu.HBM),
        scratch_shapes=[pltpu.SemaphoreType.DMA((count,))],
        compiler_params=params(),
        name=name,
    )(*parts)


def take_tiles(index, tiles):
    count = index.shape[0]

    def kernel(index_ref, in_ref, out_ref, sems):
        def copy(i):
            return pltpu.make_async_copy(in_ref.at[index_ref[i]], out_ref.at[i], sems.at[i])

        for i in range(count):
            copy(i).start()
        for i in range(count):
            copy(i).wait()

    return pl.pallas_call(
        kernel,
        out_shape=jax.ShapeDtypeStruct((count, *tiles.shape[1:]), tiles.dtype),
        grid_spec=pltpu.PrefetchScalarGridSpec(
            num_scalar_prefetch=1,
            grid=(1,),
            in_specs=[pl.BlockSpec(memory_space=pltpu.VMEM)],
            out_specs=pl.BlockSpec(memory_space=pl.ANY),
            scratch_shapes=[pltpu.SemaphoreType.DMA((count,))],
        ),
        compiler_params=params(),
        name="take_tiles",
    )(index, tiles)


def near_attend(edges, query, around, first, rows, heads, blk, hd, factor):
    width = heads * hd

    def kernel(edge_ref, q_ref, kv_ref, first_ref, acc_ref, stat_ref):
        r = pl.program_id(0)
        window = pl.ds(pl.multiple_of(r * blk, blk), 3 * blk)
        key = lax.broadcasted_iota(jnp.int32, (3 * blk, blk), 0)
        low = jnp.where((r == 0) & (edge_ref[0] == 1), blk, 0)
        high = jnp.where((r == rows - 1) & (edge_ref[1] == 1), 2 * blk, 3 * blk)
        usable = (key >= low) & (key < high)
        row = lax.broadcasted_iota(jnp.int32, (8, blk), 0)
        for e in range(heads):
            keys = slice(e * hd, (e + 1) * hd)
            values = slice(width + e * hd, width + (e + 1) * hd)
            q = q_ref[:, keys]
            near = jnp.where(usable, dot_t(kv_ref[window, keys], q) * factor, NEG)
            glob = dot_t(first_ref[:, keys], q) * factor
            top = jnp.maximum(
                jnp.max(near, axis=0, keepdims=True), jnp.max(glob, axis=0, keepdims=True)
            )
            near = jnp.exp2(near - top)
            glob = jnp.exp2(glob - top)
            total = jnp.sum(near, axis=0, keepdims=True) + jnp.sum(glob, axis=0, keepdims=True)
            acc_ref[e] = dot(kv_ref[window, values].T, near.astype(BF)) + dot(
                first_ref[:, values].T, glob.astype(BF)
            )
            stat_ref[e] = jnp.where(row == 0, top, total)

    return pl.pallas_call(
        kernel,
        out_shape=(
            jax.ShapeDtypeStruct((rows * heads, hd, blk), F32),
            jax.ShapeDtypeStruct((rows * heads, 8, blk), F32),
        ),
        grid_spec=pltpu.PrefetchScalarGridSpec(
            num_scalar_prefetch=1,
            grid=(rows,),
            in_specs=[
                pl.BlockSpec((blk, width), lambda r, s: (r, 0)),
                pl.BlockSpec(around.shape, lambda r, s: (0, 0)),
                pl.BlockSpec(first.shape, lambda r, s: (0, 0)),
            ],
            out_specs=(
                pl.BlockSpec((heads, hd, blk), lambda r, s: (r, 0, 0)),
                pl.BlockSpec((heads, 8, blk), lambda r, s: (r, 0, 0)),
            ),
        ),
        compiler_params=params(),
        name="near_attend",
    )(edges, query, around, first)


def rand_attend(slot, count, target, query, tiles, acc, stat, rows, heads, blk, hd, rand, peers, factor):
    items = rows * heads
    slots = items * rand
    share = slots // len(tiles)

    def kernel(slot_ref, count_ref, target_ref, q_ref, acc_ref, stat_ref, *refs):
        out_ref, buffer, done, in_sems, out_sems = refs[len(tiles) :]
        copies = [
            pltpu.make_async_copy(refs[n], buffer.at[pl.ds(n * share, share)], in_sems.at[n])
            for n in range(len(tiles))
        ]

        def deliver(i):
            return pltpu.make_async_copy(done.at[i], out_ref.at[target_ref[i]], out_sems.at[i])

        for copy in copies:
            copy.start()
        key = lax.broadcasted_iota(jnp.int32, (rand * blk, blk), 0)

        def step(r, carry):
            first = r * heads
            at = pl.ds(pl.multiple_of(r * blk, blk), blk)
            each = range(heads)
            places = [[slot_ref[(first + e) * rand + j] for j in range(rand)] for e in each]
            keys = [jnp.concatenate([buffer[p, :, :hd] for p in places[e]], axis=0) for e in each]
            scores = [dot_t(keys[e], q_ref[at, e * hd : (e + 1) * hd]) for e in each]
            scores = [
                jnp.where(key < count_ref[first + e] * blk, scores[e] * factor, NEG) for e in each
            ]
            top0 = [stat_ref[first + e, 0:1] for e in each]
            total0 = [stat_ref[first + e, 1:2] for e in each]
            top = [jnp.maximum(jnp.max(scores[e], axis=0, keepdims=True), top0[e]) for e in each]
            keep = [jnp.exp2(top0[e] - top[e]) for e in each]
            expo = [jnp.exp2(scores[e] - top[e]) for e in each]
            total = [total0[e] * keep[e] + jnp.sum(expo[e], axis=0, keepdims=True) for e in each]
            values = [jnp.concatenate([buffer[p, :, hd:] for p in places[e]], axis=1) for e in each]
            summed = [acc_ref[first + e] * keep[e] + dot(values[e], expo[e].astype(BF)) for e in each]
            for e in each:
                done[first + e] = (summed[e] / total[e]).T.astype(BF)
            for e in each:
                deliver(first + e).start()
            return carry

        for copy in copies:
            copy.wait()
        lax.fori_loop(0, rows, step, 0)
        for i in range(items):
            deliver(i).wait()

    vmem = pl.BlockSpec(memory_space=pltpu.VMEM)
    anywhere = pl.BlockSpec(memory_space=pl.ANY)
    return pl.pallas_call(
        kernel,
        out_shape=jax.ShapeDtypeStruct((peers, blk, hd), BF),
        grid_spec=pltpu.PrefetchScalarGridSpec(
            num_scalar_prefetch=3,
            grid=(1,),
            in_specs=[vmem, vmem, vmem, *[anywhere] * len(tiles)],
            out_specs=pl.BlockSpec(memory_space=pltpu.HBM),
            scratch_shapes=[
                pltpu.VMEM((slots, blk, 2 * hd), BF),
                pltpu.VMEM((items, blk, hd), BF),
                pltpu.SemaphoreType.DMA((len(tiles),)),
                pltpu.SemaphoreType.DMA((items,)),
            ],
        ),
        compiler_params=params(),
        name="rand_attend",
    )(slot, count, target, query, acc, stat, *tiles)


NX, NZ, NC = 4, 8, 2
def device(x, z, core):
    return (x % NX * NZ + z % NZ) * NC + core


def seq_pairs(goal):
    return [
        (device(x, z, c), device(*goal(x, z, c)))
        for x in range(NX)
        for z in range(NZ)
        for c in range(NC)
    ]


def local(tokens, w_qkv, item_at, rand_cols, rand_used):
    peers = lax.axis_size("seq")
    assert peers == NX * NZ * NC
    me = lax.axis_index("seq")
    my_x, my_z, my_core = me // (NZ * NC), me // NC % NZ, me % NC
    groups = lax.axis_size("head")
    mine_y = lax.axis_index("head")
    heads, nblocks, rand = rand_cols.shape
    rows = nblocks // peers
    count, depth = tokens.shape
    blk = count // rows
    hd = w_qkv.shape[1] // (3 * heads)
    width = heads * hd
    items = heads * rows
    factor = math.log2(math.e) / math.sqrt(hd)

    asked = rand_cols.reshape(heads, peers, rows, rand).transpose(1, 2, 0, 3)
    asked = asked.reshape(peers, items * rand)
    order = jnp.arange(items * rand, dtype=jnp.int32)
    code = order * items + (order // rand) % heads * rows + asked % rows

    def held_for(holder):
        held = asked // rows == holder
        low = jnp.min(jnp.where(held, code, jnp.int32(1 << 30)), axis=1) % items
        high = jnp.max(jnp.where(held, code, 0), axis=1) % items
        return jnp.stack([low, high], axis=1).reshape(-1)

    far_z = device(my_x, my_z + NZ // 2, my_core)
    tables = (held_for(me), held_for(far_z))
    spot = jnp.arange(NX * NC, dtype=jnp.int32)
    dests = jnp.concatenate(
        [device(spot // NC, my_z + step, spot % NC) for step in (0, 1, -1, 2 - 4 * my_core)]
    ).astype(jnp.int32)

    wanted = lax.dynamic_index_in_dim(asked, me, 0, keepdims=False)
    source = wanted // rows
    rank = jnp.sum(
        ((source[:, None] == source[None, :]) & (order[None, :] < order[:, None])).astype(jnp.int32),
        axis=1,
    )
    step = (my_z - source // NC) % NZ
    source_spot = source // (NZ * NC) * NC + source % NC
    source_two = (2 - 4 * (source % NC)) % NZ

    def route_kind(step):
        return jnp.where(
            step == 0, 0, jnp.where(step == 1, 1, jnp.where(step == NZ - 1, 2, jnp.where(step == source_two, 3, -1)))
        )

    near_kind = route_kind(step)
    other_kind = route_kind((step + NZ // 2) % NZ)
    half = (near_kind < 0).astype(jnp.int32)
    slot = source_spot * 4 + jnp.where(half == 1, other_kind, near_kind)
    slot = half * (items * rand // 2) + slot * 2 + rank

    my_used = lax.dynamic_slice_in_dim(rand_used, me * rows, rows, axis=1).T.reshape(-1)
    number = jnp.arange(items, dtype=jnp.int32)
    my_item = (number % heads) * nblocks + me * rows + number // heads
    place = jnp.arange(peers * items, dtype=jnp.int32)
    target = jnp.sum(
        jnp.where(item_at[0][None, :] == my_item[:, None], place[None, :] // items, 0), axis=1
    )
    home = (lax.dynamic_slice_in_dim(item_at[0], me * items, items) % nblocks) // rows
    edges = jnp.stack([me == 0, me == peers - 1]).astype(jnp.int32)

    def weight(shift, first, size):
        row = (mine_y + shift) % groups * depth
        return lax.dynamic_slice(w_qkv, (row, jnp.int32(first)), (depth, size))

    def w_pair(shift):
        return weight(shift, width, 2 * width)

    def w_query(shift):
        return weight(shift, 0, width)

    def spread(block, holders, stride):
        got = [lax.ppermute(block, "seq", [(h, h + k * stride) for h in holders]) for k in (1, 2, 3)]
        return block + got[0] + got[1] + got[2]

    onward = [(i, (i + 1) % groups) for i in range(groups)]
    backward = [(b, a) for a, b in onward]

    def ring(part):
        middle = part.shape[0] // 2
        low = lax.ppermute(part, "head", onward)
        high = lax.ppermute(part, "head", backward)
        top = lax.ppermute(low[:middle], "head", onward)
        bottom = lax.ppermute(high[middle:], "head", backward)
        return low, high, top, bottom

    def keys_values(part, low, high, top, bottom):
        middle = part.shape[0] // 2
        total = dot(part, w_pair(0)) + dot(low, w_pair(3)) + dot(high, w_pair(1))
        return jnp.concatenate(
            [
                (total[:middle] + dot(top, w_pair(2))).astype(BF),
                (total[middle:] + dot(bottom, w_pair(2))).astype(BF),
            ],
            axis=0,
        )

    from_low, from_high, far_top, far_bottom = ring(tokens)
    zero = tokens[:blk]
    zero = jnp.where(me == 0, zero, jnp.zeros_like(zero))
    zero = spread(spread(zero, [0], 4), range(0, 16, 4), 1)
    copied, zero = lax.optimization_barrier((tokens, zero))
    copied = lax.ppermute(copied, "seq", seq_pairs(lambda x, z, c: (x, z + NZ // 2, c)))
    zero = spread(zero, range(16), 16)

    pair = keys_values(tokens, from_low, from_high, far_top, far_bottom)
    up = [(i, i + 1) for i in range(peers - 1)]
    down = [(b, a) for a, b in up]
    before = lax.ppermute(pair[-blk:], "seq", up)
    after = lax.ppermute(pair[:blk], "seq", down)

    planes = [[device(x, z, c) for x in range(NX) for c in range(NC)] for z in range(NZ)]

    def pack(table, pair, name):
        return pack_tiles(table, dests, pair, [NX * NC] * 4, rows, heads, blk, hd, name)

    def shifted(parts):
        goals = [
            lambda x, z, c: (x, z + 1, c),
            lambda x, z, c: (x, z - 1, c),
            lambda x, z, c: (x, z + 2 - 4 * c, c),
        ]
        moved = [lax.ppermute(part, "seq", seq_pairs(goal)) for part, goal in zip(parts[1:], goals)]
        return [parts[0], *moved]

    places = [[(g, a) for g in range(NX * NC)] for a in range(4)]

    def in_plane(block):
        got = lax.all_to_all(
            block, "seq", split_axis=0, concat_axis=0, axis_index_groups=planes, tiled=True
        )
        return got.reshape(-1, blk, 2 * hd)

    own_parts = pack(tables[0], pair, "pack_own")
    own_parts, far_top, far_bottom = lax.optimization_barrier((own_parts, far_top, far_bottom))
    far = jnp.concatenate([far_top, far_bottom], axis=0)
    query = dot(far, w_query(2)) + dot(tokens, w_query(0))
    query = (query + dot(from_low, w_query(3)) + dot(from_high, w_query(1))).astype(BF)
    copied, zero, before, after, query = lax.optimization_barrier(
        (copied, zero, before, after, query)
    )
    own_parts = shifted(own_parts)
    copied = jnp.concatenate([copied, zero], axis=0)
    copied_ring = ring(copied)
    copied_pair = keys_values(copied, *copied_ring)
    copied_parts = pack(tables[1], copied_pair, "pack_copied")
    own_parts, _ = lax.optimization_barrier((own_parts, copied_parts))
    copied_parts = shifted(copied_parts)
    own_tiles = in_plane(merge_parts(own_parts, places, "merge_own"))

    around = jnp.concatenate([before, pair, after], axis=0)
    first = copied_pair[count:]
    acc, stat = near_attend(edges, query, around, first, rows, heads, blk, hd, factor)
    copied_parts, acc, stat = lax.optimization_barrier((copied_parts, acc, stat))
    copied_tiles = in_plane(merge_parts(copied_parts, places, "merge_copied"))
    done = rand_attend(
        slot, my_used, target, query, (own_tiles, copied_tiles), acc, stat,
        rows, heads, blk, hd, rand, peers, factor,
    )
    back = lax.all_to_all(done, "seq", split_axis=0, concat_axis=0, tiled=True)
    return take_tiles(home, back)[None]


def solution(mesh):
    return jax.shard_map(
        local,
        mesh=mesh,
        in_specs=(
            P("seq", "head"),
            P(None, "head"),
            P("head", None),
            P("head", None, None),
            P("head", None),
        ),
        out_specs=P("head", "seq", None, None),
        check_vma=False,
    )
```

```python
import math

import jax
import jax.numpy as jnp
from jax import lax
from jax.experimental import pallas as pl
from jax.experimental.pallas import tpu as pltpu
from jax.sharding import PartitionSpec as P

NEG = -1e30
BF = jnp.bfloat16
F32 = jnp.float32
VMEM_BYTES = 48 << 20


def dot(a, b):
    return jnp.dot(a, b, preferred_element_type=F32)


def dot_t(a, b):
    return lax.dot_general(a, b, (((1,), (1,)), ((), ())), preferred_element_type=F32)


def params():
    return pltpu.CompilerParams(vmem_limit_bytes=VMEM_BYTES)


def pack_tiles(table, dests, pair, shares, rows, heads, blk, hd, name):
    width = heads * hd
    ends = [(k, i) for k, share in enumerate(shares) for i in range(share)]

    def kernel(table_ref, dest_ref, pair_ref, *refs):
        outs = refs[: len(shares)]
        tiles, sems = refs[len(shares) :]

        def copy(n, t):
            k, i = ends[n]
            tile = table_ref[2 * dest_ref[n] + t]
            return pltpu.make_async_copy(tiles.at[tile], outs[k].at[i, t], sems.at[2 * n + t])

        for e in range(heads):
            for r in range(rows):
                at = slice(r * blk, (r + 1) * blk)
                tiles[e * rows + r, :, :hd] = pair_ref[at, e * hd : (e + 1) * hd]
                tiles[e * rows + r, :, hd:] = pair_ref[at, width + e * hd : width + (e + 1) * hd].T
        for n in range(len(ends)):
            for t in range(2):
                copy(n, t).start()
        for n in range(len(ends)):
            for t in range(2):
                copy(n, t).wait()

    anywhere = pl.BlockSpec(memory_space=pl.ANY)
    return pl.pallas_call(
        kernel,
        out_shape=[jax.ShapeDtypeStruct((share, 2, blk, 2 * hd), BF) for share in shares],
        grid_spec=pltpu.PrefetchScalarGridSpec(
            num_scalar_prefetch=2,
            grid=(1,),
            in_specs=[pl.BlockSpec(memory_space=pltpu.VMEM)],
            out_specs=[anywhere] * len(shares),
            scratch_shapes=[
                pltpu.VMEM((rows * heads, blk, 2 * hd), BF),
                pltpu.SemaphoreType.DMA((2 * len(ends),)),
            ],
        ),
        compiler_params=params(),
        name=name,
    )(table, dests, pair)


def take_tiles(index, tiles):
    count = index.shape[0]

    def kernel(index_ref, in_ref, out_ref, sems):
        def copy(i):
            return pltpu.make_async_copy(in_ref.at[index_ref[i]], out_ref.at[i], sems.at[i])

        for i in range(count):
            copy(i).start()
        for i in range(count):
            copy(i).wait()

    return pl.pallas_call(
        kernel,
        out_shape=jax.ShapeDtypeStruct((count, *tiles.shape[1:]), tiles.dtype),
        grid_spec=pltpu.PrefetchScalarGridSpec(
            num_scalar_prefetch=1,
            grid=(1,),
            in_specs=[pl.BlockSpec(memory_space=pltpu.VMEM)],
            out_specs=pl.BlockSpec(memory_space=pl.ANY),
            scratch_shapes=[pltpu.SemaphoreType.DMA((count,))],
        ),
        compiler_params=params(),
        name="take_tiles",
    )(index, tiles)


def near_attend(edges, query, around, first, rows, heads, blk, hd, factor):
    width = heads * hd

    def kernel(edge_ref, q_ref, kv_ref, first_ref, acc_ref, stat_ref):
        r = pl.program_id(0)
        window = pl.ds(pl.multiple_of(r * blk, blk), 3 * blk)
        key = lax.broadcasted_iota(jnp.int32, (3 * blk, blk), 0)
        low = jnp.where((r == 0) & (edge_ref[0] == 1), blk, 0)
        high = jnp.where((r == rows - 1) & (edge_ref[1] == 1), 2 * blk, 3 * blk)
        usable = (key >= low) & (key < high)
        row = lax.broadcasted_iota(jnp.int32, (8, blk), 0)
        for e in range(heads):
            keys = slice(e * hd, (e + 1) * hd)
            values = slice(width + e * hd, width + (e + 1) * hd)
            q = q_ref[:, keys]
            near = jnp.where(usable, dot_t(kv_ref[window, keys], q) * factor, NEG)
            glob = dot_t(first_ref[:, keys], q) * factor
            top = jnp.maximum(
                jnp.max(near, axis=0, keepdims=True), jnp.max(glob, axis=0, keepdims=True)
            )
            near = jnp.exp2(near - top)
            glob = jnp.exp2(glob - top)
            total = jnp.sum(near, axis=0, keepdims=True) + jnp.sum(glob, axis=0, keepdims=True)
            acc_ref[e] = dot(kv_ref[window, values].T, near.astype(BF)) + dot(
                first_ref[:, values].T, glob.astype(BF)
            )
            stat_ref[e] = jnp.where(row == 0, top, total)

    return pl.pallas_call(
        kernel,
        out_shape=(
            jax.ShapeDtypeStruct((rows * heads, hd, blk), F32),
            jax.ShapeDtypeStruct((rows * heads, 8, blk), F32),
        ),
        grid_spec=pltpu.PrefetchScalarGridSpec(
            num_scalar_prefetch=1,
            grid=(rows,),
            in_specs=[
                pl.BlockSpec((blk, width), lambda r, s: (r, 0)),
                pl.BlockSpec(around.shape, lambda r, s: (0, 0)),
                pl.BlockSpec(first.shape, lambda r, s: (0, 0)),
            ],
            out_specs=(
                pl.BlockSpec((heads, hd, blk), lambda r, s: (r, 0, 0)),
                pl.BlockSpec((heads, 8, blk), lambda r, s: (r, 0, 0)),
            ),
        ),
        compiler_params=params(),
        name="near_attend",
    )(edges, query, around, first)


def rand_attend(slot, count, target, query, tiles, acc, stat, rows, heads, blk, hd, rand, peers, factor):
    items = rows * heads
    slots = items * rand
    share = slots // len(tiles)
    spots = share // 2

    def kernel(slot_ref, count_ref, target_ref, q_ref, acc_ref, stat_ref, *refs):
        out_ref, buffer, done, in_sems, out_sems = refs[len(tiles) :]
        pairs = []
        for n in range(len(tiles)):
            if n % 4:
                pairs.append((refs[n], buffer.at[n]))
            else:
                pairs += [(refs[n].at[g, 0], buffer.at[n, pl.ds(2 * g, 2)]) for g in range(spots)]
        copies = [
            pltpu.make_async_copy(source, place, in_sems.at[n])
            for n, (source, place) in enumerate(pairs)
        ]

        def deliver(i):
            return pltpu.make_async_copy(done.at[i], out_ref.at[target_ref[i]], out_sems.at[i])

        for copy in copies:
            copy.start()
        key = lax.broadcasted_iota(jnp.int32, (rand * blk, blk), 0)

        def step(r, carry):
            first = r * heads
            at = pl.ds(pl.multiple_of(r * blk, blk), blk)
            each = range(heads)
            places = [[slot_ref[(first + e) * rand + j] for j in range(rand)] for e in each]
            places = [[(p // share, p % share) for p in at_e] for at_e in places]
            keys = [jnp.concatenate([buffer[n, i, :, :hd] for n, i in places[e]], axis=0) for e in each]
            scores = [dot_t(keys[e], q_ref[at, e * hd : (e + 1) * hd]) for e in each]
            scores = [
                jnp.where(key < count_ref[first + e] * blk, scores[e] * factor, NEG) for e in each
            ]
            top0 = [stat_ref[first + e, 0:1] for e in each]
            total0 = [stat_ref[first + e, 1:2] for e in each]
            top = [jnp.maximum(jnp.max(scores[e], axis=0, keepdims=True), top0[e]) for e in each]
            keep = [jnp.exp2(top0[e] - top[e]) for e in each]
            expo = [jnp.exp2(scores[e] - top[e]) for e in each]
            total = [total0[e] * keep[e] + jnp.sum(expo[e], axis=0, keepdims=True) for e in each]
            values = [jnp.concatenate([buffer[n, i, :, hd:] for n, i in places[e]], axis=1) for e in each]
            summed = [acc_ref[first + e] * keep[e] + dot(values[e], expo[e].astype(BF)) for e in each]
            for e in each:
                done[first + e] = (summed[e] / total[e]).T.astype(BF)
            for e in each:
                deliver(first + e).start()
            return carry

        for copy in copies:
            copy.wait()
        lax.fori_loop(0, rows, step, 0)
        for i in range(items):
            deliver(i).wait()

    vmem = pl.BlockSpec(memory_space=pltpu.VMEM)
    anywhere = pl.BlockSpec(memory_space=pl.ANY)
    return pl.pallas_call(
        kernel,
        out_shape=jax.ShapeDtypeStruct((peers, blk, hd), BF),
        grid_spec=pltpu.PrefetchScalarGridSpec(
            num_scalar_prefetch=3,
            grid=(1,),
            in_specs=[vmem, vmem, vmem, *[anywhere] * len(tiles)],
            out_specs=pl.BlockSpec(memory_space=pltpu.HBM),
            scratch_shapes=[
                pltpu.VMEM((len(tiles), share, blk, 2 * hd), BF),
                pltpu.VMEM((items, blk, hd), BF),
                pltpu.SemaphoreType.DMA((len(tiles) * 3 // 4 + 2 * spots,)),
                pltpu.SemaphoreType.DMA((items,)),
            ],
        ),
        compiler_params=params(),
        name="rand_attend",
    )(slot, count, target, query, acc, stat, *tiles)


NX, NZ, NC = 4, 8, 2
def device(x, z, core):
    return (x % NX * NZ + z % NZ) * NC + core


def seq_pairs(goal):
    return [
        (device(x, z, c), device(*goal(x, z, c)))
        for x in range(NX)
        for z in range(NZ)
        for c in range(NC)
    ]


def local(tokens, w_qkv, item_at, rand_cols, rand_used):
    peers = lax.axis_size("seq")
    assert peers == NX * NZ * NC
    me = lax.axis_index("seq")
    my_x, my_z, my_core = me // (NZ * NC), me // NC % NZ, me % NC
    groups = lax.axis_size("head")
    mine_y = lax.axis_index("head")
    heads, nblocks, rand = rand_cols.shape
    rows = nblocks // peers
    count, depth = tokens.shape
    blk = count // rows
    hd = w_qkv.shape[1] // (3 * heads)
    width = heads * hd
    items = heads * rows
    factor = math.log2(math.e) / math.sqrt(hd)

    asked = rand_cols.reshape(heads, peers, rows, rand).transpose(1, 2, 0, 3)
    asked = asked.reshape(peers, items * rand)
    order = jnp.arange(items * rand, dtype=jnp.int32)
    code = order * items + (order // rand) % heads * rows + asked % rows

    def held_for(holder):
        held = asked // rows == holder
        low = jnp.min(jnp.where(held, code, jnp.int32(1 << 30)), axis=1) % items
        high = jnp.max(jnp.where(held, code, 0), axis=1) % items
        return jnp.stack([low, high], axis=1).reshape(-1)

    far_z = device(my_x, my_z + NZ // 2, my_core)
    tables = (held_for(me), held_for(far_z))
    goal = jnp.arange(4 * NX * NC, dtype=jnp.int32)
    spot, kind = goal // 4, goal % 4
    two = 2 - 4 * (spot % NC)
    z_move = jnp.where(kind == 3, two, jnp.where(kind == 2, -1, kind))
    dests = device(spot // NC, my_z + z_move, spot % NC).astype(jnp.int32)

    wanted = lax.dynamic_index_in_dim(asked, me, 0, keepdims=False)
    source = wanted // rows
    rank = jnp.sum(
        ((source[:, None] == source[None, :]) & (order[None, :] < order[:, None])).astype(jnp.int32),
        axis=1,
    )
    step = (my_z - source // NC) % NZ
    source_spot = source // (NZ * NC) * NC + source % NC
    my_two = (2 - 4 * my_core) % NZ

    def route_kind(step):
        return jnp.where(
            step == 0, 0, jnp.where(step == 1, 1, jnp.where(step == NZ - 1, 2, jnp.where(step == my_two, 3, -1)))
        )

    near_kind = route_kind(step)
    other_kind = route_kind((step + NZ // 2) % NZ)
    half = (near_kind < 0).astype(jnp.int32)
    slot = jnp.where(half == 1, 4 + other_kind, near_kind) * (2 * NX * NC) + source_spot * 2 + rank

    my_used = lax.dynamic_slice_in_dim(rand_used, me * rows, rows, axis=1).T.reshape(-1)
    number = jnp.arange(items, dtype=jnp.int32)
    my_item = (number % heads) * nblocks + me * rows + number // heads
    place = jnp.arange(peers * items, dtype=jnp.int32)
    target = jnp.sum(
        jnp.where(item_at[0][None, :] == my_item[:, None], place[None, :] // items, 0), axis=1
    )
    home = (lax.dynamic_slice_in_dim(item_at[0], me * items, items) % nblocks) // rows
    edges = jnp.stack([me == 0, me == peers - 1]).astype(jnp.int32)

    def weight(shift, first, size):
        row = (mine_y + shift) % groups * depth
        return lax.dynamic_slice(w_qkv, (row, jnp.int32(first)), (depth, size))

    def w_pair(shift):
        return weight(shift, width, 2 * width)

    def w_query(shift):
        return weight(shift, 0, width)

    def spread(block, holders, stride):
        got = [lax.ppermute(block, "seq", [(h, h + k * stride) for h in holders]) for k in (1, 2, 3)]
        return block + got[0] + got[1] + got[2]

    onward = [(i, (i + 1) % groups) for i in range(groups)]
    backward = [(b, a) for a, b in onward]

    def ring(part):
        middle = part.shape[0] // 2
        low = lax.ppermute(part, "head", onward)
        high = lax.ppermute(part, "head", backward)
        top = lax.ppermute(low[:middle], "head", onward)
        bottom = lax.ppermute(high[middle:], "head", backward)
        return low, high, top, bottom

    def keys_values(part, low, high, top, bottom):
        middle = part.shape[0] // 2
        total = dot(part, w_pair(0)) + dot(low, w_pair(3)) + dot(high, w_pair(1))
        return jnp.concatenate(
            [
                (total[:middle] + dot(top, w_pair(2))).astype(BF),
                (total[middle:] + dot(bottom, w_pair(2))).astype(BF),
            ],
            axis=0,
        )

    from_low, from_high, far_top, far_bottom = ring(tokens)
    zero = tokens[:blk]
    zero = jnp.where(me == 0, zero, jnp.zeros_like(zero))
    zero = spread(spread(zero, [0], 4), range(0, 16, 4), 1)
    copied, zero = lax.optimization_barrier((tokens, zero))
    copied = lax.ppermute(copied, "seq", seq_pairs(lambda x, z, c: (x, z + NZ // 2, c)))
    zero = spread(zero, range(16), 16)

    pair = keys_values(tokens, from_low, from_high, far_top, far_bottom)
    up = [(i, i + 1) for i in range(peers - 1)]
    down = [(b, a) for a, b in up]
    before = lax.ppermute(pair[-blk:], "seq", up)
    after = lax.ppermute(pair[:blk], "seq", down)

    planes = [[device(x, z, c) for x in range(NX) for c in range(NC)] for z in range(NZ)]

    def pack(table, pair, name):
        (packed,) = pack_tiles(table, dests, pair, [4 * NX * NC], rows, heads, blk, hd, name)
        return packed.reshape(NX * NC, 4, 2, blk, 2 * hd)

    def in_plane(block):
        return lax.all_to_all(
            block, "seq", split_axis=0, concat_axis=0, axis_index_groups=planes, tiled=True
        )

    def along_z(got):
        goals = [
            lambda x, z, c: (x, z + 1, c),
            lambda x, z, c: (x, z - 1, c),
            lambda x, z, c: (x, z + 2 - 4 * c, c),
        ]
        moved = [
            lax.ppermute(got[:, k].reshape(-1, blk, 2 * hd), "seq", seq_pairs(goal))
            for k, goal in enumerate(goals, 1)
        ]
        return [got, *moved]

    own_block = pack(tables[0], pair, "pack_own")
    own_block, far_top, far_bottom = lax.optimization_barrier((own_block, far_top, far_bottom))
    far = jnp.concatenate([far_top, far_bottom], axis=0)
    query = dot(far, w_query(2)) + dot(tokens, w_query(0))
    query = (query + dot(from_low, w_query(3)) + dot(from_high, w_query(1))).astype(BF)
    copied, zero, before, after, query = lax.optimization_barrier(
        (copied, zero, before, after, query)
    )
    own_parts = along_z(in_plane(own_block))
    copied = jnp.concatenate([copied, zero], axis=0)
    copied_ring = ring(copied)
    copied_pair = keys_values(copied, *copied_ring)
    copied_block = pack(tables[1], copied_pair, "pack_copied")
    around = jnp.concatenate([before, pair, after], axis=0)
    first = copied_pair[count:]
    acc, stat = near_attend(edges, query, around, first, rows, heads, blk, hd, factor)
    copied_got, acc, stat = lax.optimization_barrier((in_plane(copied_block), acc, stat))
    copied_parts = along_z(copied_got)
    done = rand_attend(
        slot, my_used, target, query, (*own_parts, *copied_parts), acc, stat,
        rows, heads, blk, hd, rand, peers, factor,
    )
    back = lax.all_to_all(done, "seq", split_axis=0, concat_axis=0, tiled=True)
    return take_tiles(home, back)[None]


def solution(mesh):
    return jax.shard_map(
        local,
        mesh=mesh,
        in_specs=(
            P("seq", "head"),
            P(None, "head"),
            P("head", None),
            P("head", None, None),
            P("head", None),
        ),
        out_specs=P("head", "seq", None, None),
        check_vma=False,
    )
```

```python
import math

import jax
import jax.numpy as jnp
from jax import lax
from jax.experimental import pallas as pl
from jax.experimental.pallas import tpu as pltpu
from jax.sharding import PartitionSpec as P

NEG = -1e30
BF = jnp.bfloat16
F32 = jnp.float32
VMEM_BYTES = 48 << 20


def dot(a, b):
    return jnp.dot(a, b, preferred_element_type=F32)


def dot_t(a, b):
    return lax.dot_general(a, b, (((1,), (1,)), ((), ())), preferred_element_type=F32)


def params():
    return pltpu.CompilerParams(vmem_limit_bytes=VMEM_BYTES)


def pack_tiles(index, pair, slots, rows, heads, blk, hd):
    width = heads * hd

    def kernel(index_ref, pair_ref, out_ref, tiles, sems):
        def copy(s):
            return pltpu.make_async_copy(tiles.at[index_ref[s]], out_ref.at[s], sems.at[s])

        for e in range(heads):
            for r in range(rows):
                at = slice(r * blk, (r + 1) * blk)
                tiles[e * rows + r, :, :hd] = pair_ref[at, e * hd : (e + 1) * hd]
                tiles[e * rows + r, :, hd:] = pair_ref[at, width + e * hd : width + (e + 1) * hd].T
        for s in range(slots):
            copy(s).start()
        for s in range(slots):
            copy(s).wait()

    return pl.pallas_call(
        kernel,
        out_shape=jax.ShapeDtypeStruct((slots, blk, 2 * hd), BF),
        grid_spec=pltpu.PrefetchScalarGridSpec(
            num_scalar_prefetch=1,
            grid=(1,),
            in_specs=[pl.BlockSpec(memory_space=pltpu.VMEM)],
            out_specs=pl.BlockSpec(memory_space=pl.ANY),
            scratch_shapes=[
                pltpu.VMEM((rows * heads, blk, 2 * hd), BF),
                pltpu.SemaphoreType.DMA((slots,)),
            ],
        ),
        compiler_params=params(),
        name="pack_tiles",
    )(index, pair)


def take_tiles(index, tiles):
    count = index.shape[0]

    def kernel(index_ref, in_ref, out_ref, sems):
        def copy(i):
            return pltpu.make_async_copy(in_ref.at[index_ref[i]], out_ref.at[i], sems.at[i])

        for i in range(count):
            copy(i).start()
        for i in range(count):
            copy(i).wait()

    return pl.pallas_call(
        kernel,
        out_shape=jax.ShapeDtypeStruct((count, *tiles.shape[1:]), tiles.dtype),
        grid_spec=pltpu.PrefetchScalarGridSpec(
            num_scalar_prefetch=1,
            grid=(1,),
            in_specs=[pl.BlockSpec(memory_space=pltpu.VMEM)],
            out_specs=pl.BlockSpec(memory_space=pl.ANY),
            scratch_shapes=[pltpu.SemaphoreType.DMA((count,))],
        ),
        compiler_params=params(),
        name="take_tiles",
    )(index, tiles)


def near_attend(edges, query, around, first, rows, heads, blk, hd, factor):
    width = heads * hd

    def kernel(edge_ref, q_ref, kv_ref, first_ref, acc_ref, stat_ref):
        r = pl.program_id(0)
        window = pl.ds(pl.multiple_of(r * blk, blk), 3 * blk)
        key = lax.broadcasted_iota(jnp.int32, (3 * blk, blk), 0)
        low = jnp.where((r == 0) & (edge_ref[0] == 1), blk, 0)
        high = jnp.where((r == rows - 1) & (edge_ref[1] == 1), 2 * blk, 3 * blk)
        usable = (key >= low) & (key < high)
        row = lax.broadcasted_iota(jnp.int32, (8, blk), 0)
        for e in range(heads):
            keys = slice(e * hd, (e + 1) * hd)
            values = slice(width + e * hd, width + (e + 1) * hd)
            q = q_ref[:, keys]
            near = jnp.where(usable, dot_t(kv_ref[window, keys], q) * factor, NEG)
            glob = dot_t(first_ref[:, keys], q) * factor
            top = jnp.maximum(
                jnp.max(near, axis=0, keepdims=True), jnp.max(glob, axis=0, keepdims=True)
            )
            near = jnp.exp2(near - top)
            glob = jnp.exp2(glob - top)
            total = jnp.sum(near, axis=0, keepdims=True) + jnp.sum(glob, axis=0, keepdims=True)
            acc_ref[e] = dot(kv_ref[window, values].T, near.astype(BF)) + dot(
                first_ref[:, values].T, glob.astype(BF)
            )
            stat_ref[e] = jnp.where(row == 0, top, total)

    return pl.pallas_call(
        kernel,
        out_shape=(
            jax.ShapeDtypeStruct((rows * heads, hd, blk), F32),
            jax.ShapeDtypeStruct((rows * heads, 8, blk), F32),
        ),
        grid_spec=pltpu.PrefetchScalarGridSpec(
            num_scalar_prefetch=1,
            grid=(rows,),
            in_specs=[
                pl.BlockSpec((blk, width), lambda r, s: (r, 0)),
                pl.BlockSpec(around.shape, lambda r, s: (0, 0)),
                pl.BlockSpec(first.shape, lambda r, s: (0, 0)),
            ],
            out_specs=(
                pl.BlockSpec((heads, hd, blk), lambda r, s: (r, 0, 0)),
                pl.BlockSpec((heads, 8, blk), lambda r, s: (r, 0, 0)),
            ),
        ),
        compiler_params=params(),
        name="near_attend",
    )(edges, query, around, first)


def rand_attend(slot, count, target, query, tiles, acc, stat, rows, heads, blk, hd, rand, peers, factor):
    items = rows * heads
    slots = items * rand

    def kernel(
        slot_ref, count_ref, target_ref, q_ref, acc_ref, stat_ref, tiles_ref, out_ref,
        buffer, done, in_sems, out_sems,
    ):
        def fetch(n):
            return pltpu.make_async_copy(tiles_ref.at[slot_ref[n]], buffer.at[n], in_sems.at[n])

        def deliver(i):
            return pltpu.make_async_copy(done.at[i], out_ref.at[target_ref[i]], out_sems.at[i])

        for n in range(slots):
            fetch(n).start()
        key = lax.broadcasted_iota(jnp.int32, (rand * blk, blk), 0)

        def step(r, carry):
            first = r * heads
            for n in range(heads * rand):
                fetch(first * rand + n).wait()
            at = pl.ds(pl.multiple_of(r * blk, blk), blk)
            each = range(heads)
            keys = [
                buffer[pl.ds((first + e) * rand, rand), :, :hd].reshape(rand * blk, hd) for e in each
            ]
            scores = [dot_t(keys[e], q_ref[at, e * hd : (e + 1) * hd]) for e in each]
            scores = [
                jnp.where(key < count_ref[first + e] * blk, scores[e] * factor, NEG) for e in each
            ]
            top0 = [stat_ref[first + e, 0:1] for e in each]
            total0 = [stat_ref[first + e, 1:2] for e in each]
            top = [jnp.maximum(jnp.max(scores[e], axis=0, keepdims=True), top0[e]) for e in each]
            keep = [jnp.exp2(top0[e] - top[e]) for e in each]
            expo = [jnp.exp2(scores[e] - top[e]) for e in each]
            total = [total0[e] * keep[e] + jnp.sum(expo[e], axis=0, keepdims=True) for e in each]
            values = [
                jnp.concatenate([buffer[(first + e) * rand + j, :, hd:] for j in range(rand)], axis=1)
                for e in each
            ]
            summed = [acc_ref[first + e] * keep[e] + dot(values[e], expo[e].astype(BF)) for e in each]
            for e in each:
                done[first + e] = (summed[e] / total[e]).T.astype(BF)
            for e in each:
                deliver(first + e).start()
            return carry

        lax.fori_loop(0, rows, step, 0)
        for i in range(items):
            deliver(i).wait()

    vmem = pl.BlockSpec(memory_space=pltpu.VMEM)
    anywhere = pl.BlockSpec(memory_space=pl.ANY)
    return pl.pallas_call(
        kernel,
        out_shape=jax.ShapeDtypeStruct((peers, blk, hd), BF),
        grid_spec=pltpu.PrefetchScalarGridSpec(
            num_scalar_prefetch=3,
            grid=(1,),
            in_specs=[vmem, vmem, vmem, anywhere],
            out_specs=anywhere,
            scratch_shapes=[
                pltpu.VMEM((slots, blk, 2 * hd), BF),
                pltpu.VMEM((items, blk, hd), BF),
                pltpu.SemaphoreType.DMA((slots,)),
                pltpu.SemaphoreType.DMA((items,)),
            ],
        ),
        compiler_params=params(),
        name="rand_attend",
    )(slot, count, target, query, acc, stat, tiles)


def local(tokens, w_qkv, item_at, rand_cols, rand_used):
    peers = lax.axis_size("seq")
    me = lax.axis_index("seq")
    groups = lax.axis_size("head")
    mine_y = lax.axis_index("head")
    heads, nblocks, rand = rand_cols.shape
    rows = nblocks // peers
    count, depth = tokens.shape
    blk = count // rows
    hd = w_qkv.shape[1] // (3 * heads)
    width = heads * hd
    items = heads * rows
    factor = math.log2(math.e) / math.sqrt(hd)

    asked = rand_cols.reshape(heads, peers, rows, rand).transpose(1, 2, 0, 3)
    asked = asked.reshape(peers, items * rand)
    order = jnp.arange(items * rand, dtype=jnp.int32)
    head_of = (order // rand) % heads
    code = order * items + head_of * rows + asked % rows
    mine = asked // rows == me
    low = jnp.min(jnp.where(mine, code, jnp.int32(1 << 30)), axis=1) % items
    high = jnp.max(jnp.where(mine, code, 0), axis=1) % items
    send_tile = jnp.stack([low, high], axis=1).reshape(-1)
    wanted = lax.dynamic_index_in_dim(asked, me, 0, keepdims=False)
    source = wanted // rows
    again = jnp.sum(
        ((source[:, None] == source[None, :]) & (order[None, :] < order[:, None])).astype(jnp.int32),
        axis=1,
    )
    slot = source * 2 + again
    my_used = lax.dynamic_slice_in_dim(rand_used, me * rows, rows, axis=1).T.reshape(-1)
    number = jnp.arange(items, dtype=jnp.int32)
    my_item = (number % heads) * nblocks + me * rows + number // heads
    place = jnp.arange(peers * items, dtype=jnp.int32)
    target = jnp.sum(
        jnp.where(item_at[0][None, :] == my_item[:, None], place[None, :] // items, 0), axis=1
    )
    home = (lax.dynamic_slice_in_dim(item_at[0], me * items, items) % nblocks) // rows
    edges = jnp.stack([me == 0, me == peers - 1]).astype(jnp.int32)

    def weight(shift, first, size):
        row = (mine_y + shift) % groups * depth
        return lax.dynamic_slice(w_qkv, (row, jnp.int32(first)), (depth, size))

    def w_pair(shift):
        return weight(shift, width, 2 * width)

    def w_query(shift):
        return weight(shift, 0, width)

    def spread(block, stride):
        holders = range(0, peers, 4 * stride)
        got = [
            lax.ppermute(block, "seq", [(h, h + k * stride) for h in holders]) for k in (1, 2, 3)
        ]
        return block + got[0] + got[1] + got[2]

    onward = [(i, (i + 1) % groups) for i in range(groups)]
    backward = [(b, a) for a, b in onward]
    across = [(i, (i + 2) % groups) for i in range(groups)]
    middle = count // 2
    from_low = lax.ppermute(tokens, "head", onward)
    from_high = lax.ppermute(tokens, "head", backward)
    zero = tokens[:blk]
    zero = jnp.where(me == 0, zero, jnp.zeros_like(zero))
    zero = spread(spread(spread(zero, peers // 4), peers // 16), peers // 64)
    far_top = lax.ppermute(from_low[:middle], "head", onward)
    far_bottom = lax.ppermute(from_high[middle:], "head", backward)
    own, zero = lax.optimization_barrier((tokens, zero))
    total = dot(own, w_pair(0)) + dot(from_low, w_pair(3)) + dot(from_high, w_pair(1))
    far_top, far_bottom, zero = lax.optimization_barrier((far_top, far_bottom, zero))
    pair = jnp.concatenate(
        [
            (total[:middle] + dot(far_top, w_pair(2))).astype(BF),
            (total[middle:] + dot(far_bottom, w_pair(2))).astype(BF),
        ],
        axis=0,
    )
    up = [(i, i + 1) for i in range(peers - 1)]
    down = [(b, a) for a, b in up]
    before = lax.ppermute(pair[-blk:], "seq", up)
    after = lax.ppermute(pair[:blk], "seq", down)
    sent = pack_tiles(send_tile, pair, 2 * peers, rows, heads, blk, hd)
    sent, before, after, far_top, far_bottom, zero = lax.optimization_barrier(
        (sent, before, after, far_top, far_bottom, zero)
    )
    tiles = lax.all_to_all(sent, "seq", split_axis=0, concat_axis=0, tiled=True)

    zero_low = lax.ppermute(zero, "head", onward)
    zero_high = lax.ppermute(zero, "head", backward)
    zero_far = lax.ppermute(zero, "head", across)
    around = jnp.concatenate([before, pair, after], axis=0)
    far = jnp.concatenate([far_top, far_bottom], axis=0)
    query = dot(far, w_query(2)) + dot(tokens, w_query(0))
    query = (query + dot(from_low, w_query(3)) + dot(from_high, w_query(1))).astype(BF)
    first = dot(zero, w_pair(0)) + dot(zero_low, w_pair(3))
    first = (first + dot(zero_high, w_pair(1)) + dot(zero_far, w_pair(2))).astype(BF)
    acc, stat = near_attend(edges, query, around, first, rows, heads, blk, hd, factor)
    done = rand_attend(
        slot, my_used, target, query, tiles, acc, stat, rows, heads, blk, hd, rand, peers, factor
    )
    back = lax.all_to_all(done, "seq", split_axis=0, concat_axis=0, tiled=True)
    return take_tiles(home, back)[None]


def solution(mesh):
    return jax.shard_map(
        local,
        mesh=mesh,
        in_specs=(
            P("seq", "head"),
            P(None, "head"),
            P("head", None),
            P("head", None, None),
            P("head", None),
        ),
        out_specs=P("head", "seq", None, None),
        check_vma=False,
    )
```

```python
import math

import jax
import jax.numpy as jnp
from jax import lax
from jax.experimental import pallas as pl
from jax.experimental.pallas import tpu as pltpu
from jax.sharding import PartitionSpec as P

NEG = -1e30
BF = jnp.bfloat16
F32 = jnp.float32
VMEM_BYTES = 48 << 20


def dot(a, b):
    return jnp.dot(a, b, preferred_element_type=F32)


def dot_t(a, b):
    return lax.dot_general(a, b, (((1,), (1,)), ((), ())), preferred_element_type=F32)


def params():
    return pltpu.CompilerParams(vmem_limit_bytes=VMEM_BYTES)


def pack_tiles(index, halves, slots, rows, heads, blk, hd):
    width = heads * hd

    def kernel(index_ref, top_ref, bottom_ref, out_ref, tiles, sems):
        def copy(s):
            return pltpu.make_async_copy(tiles.at[index_ref[s]], out_ref.at[s], sems.at[s])

        for e in range(heads):
            for r in range(rows):
                pair_ref, place = (top_ref, r) if r < rows // 2 else (bottom_ref, r - rows // 2)
                at = slice(place * blk, (place + 1) * blk)
                tiles[e * rows + r, :, :hd] = pair_ref[at, e * hd : (e + 1) * hd]
                tiles[e * rows + r, :, hd:] = pair_ref[at, width + e * hd : width + (e + 1) * hd].T
        for s in range(slots):
            copy(s).start()
        for s in range(slots):
            copy(s).wait()

    return pl.pallas_call(
        kernel,
        out_shape=jax.ShapeDtypeStruct((slots, blk, 2 * hd), BF),
        grid_spec=pltpu.PrefetchScalarGridSpec(
            num_scalar_prefetch=1,
            grid=(1,),
            in_specs=[pl.BlockSpec(memory_space=pltpu.VMEM)] * 2,
            out_specs=pl.BlockSpec(memory_space=pl.ANY),
            scratch_shapes=[
                pltpu.VMEM((rows * heads, blk, 2 * hd), BF),
                pltpu.SemaphoreType.DMA((slots,)),
            ],
        ),
        compiler_params=params(),
        name="pack_tiles",
    )(index, *halves)


def take_tiles(index, tiles):
    count = index.shape[0]

    def kernel(index_ref, in_ref, out_ref, sems):
        def copy(i):
            return pltpu.make_async_copy(in_ref.at[index_ref[i]], out_ref.at[i], sems.at[i])

        for i in range(count):
            copy(i).start()
        for i in range(count):
            copy(i).wait()

    return pl.pallas_call(
        kernel,
        out_shape=jax.ShapeDtypeStruct((count, *tiles.shape[1:]), tiles.dtype),
        grid_spec=pltpu.PrefetchScalarGridSpec(
            num_scalar_prefetch=1,
            grid=(1,),
            in_specs=[pl.BlockSpec(memory_space=pltpu.VMEM)],
            out_specs=pl.BlockSpec(memory_space=pl.ANY),
            scratch_shapes=[pltpu.SemaphoreType.DMA((count,))],
        ),
        compiler_params=params(),
        name="take_tiles",
    )(index, tiles)


def near_attend(edges, query, around, first, rows, heads, blk, hd, factor):
    width = heads * hd

    def kernel(edge_ref, q_ref, kv_ref, first_ref, acc_ref, stat_ref):
        r = pl.program_id(0)
        window = pl.ds(pl.multiple_of(r * blk, blk), 3 * blk)
        key = lax.broadcasted_iota(jnp.int32, (3 * blk, blk), 0)
        low = jnp.where((r == 0) & (edge_ref[0] == 1), blk, 0)
        high = jnp.where((r == rows - 1) & (edge_ref[1] == 1), 2 * blk, 3 * blk)
        usable = (key >= low) & (key < high)
        row = lax.broadcasted_iota(jnp.int32, (8, blk), 0)
        for e in range(heads):
            keys = slice(e * hd, (e + 1) * hd)
            values = slice(width + e * hd, width + (e + 1) * hd)
            q = q_ref[:, keys]
            near = jnp.where(usable, dot_t(kv_ref[window, keys], q) * factor, NEG)
            glob = dot_t(first_ref[:, keys], q) * factor
            top = jnp.maximum(
                jnp.max(near, axis=0, keepdims=True), jnp.max(glob, axis=0, keepdims=True)
            )
            near = jnp.exp2(near - top)
            glob = jnp.exp2(glob - top)
            total = jnp.sum(near, axis=0, keepdims=True) + jnp.sum(glob, axis=0, keepdims=True)
            acc_ref[e] = dot(kv_ref[window, values].T, near.astype(BF)) + dot(
                first_ref[:, values].T, glob.astype(BF)
            )
            stat_ref[e] = jnp.where(row == 0, top, total)

    return pl.pallas_call(
        kernel,
        out_shape=(
            jax.ShapeDtypeStruct((rows * heads, hd, blk), F32),
            jax.ShapeDtypeStruct((rows * heads, 8, blk), F32),
        ),
        grid_spec=pltpu.PrefetchScalarGridSpec(
            num_scalar_prefetch=1,
            grid=(rows,),
            in_specs=[
                pl.BlockSpec((blk, width), lambda r, s: (r, 0)),
                pl.BlockSpec(around.shape, lambda r, s: (0, 0)),
                pl.BlockSpec(first.shape, lambda r, s: (0, 0)),
            ],
            out_specs=(
                pl.BlockSpec((heads, hd, blk), lambda r, s: (r, 0, 0)),
                pl.BlockSpec((heads, 8, blk), lambda r, s: (r, 0, 0)),
            ),
        ),
        compiler_params=params(),
        name="near_attend",
    )(edges, query, around, first)


def rand_attend(slot, count, target, query, tiles, acc, stat, rows, heads, blk, hd, rand, peers, factor):
    items = rows * heads
    slots = items * rand

    def kernel(
        slot_ref, count_ref, target_ref, q_ref, acc_ref, stat_ref, tiles_ref, out_ref,
        buffer, done, in_sems, out_sems,
    ):
        def fetch(n):
            return pltpu.make_async_copy(tiles_ref.at[slot_ref[n]], buffer.at[n], in_sems.at[n])

        def deliver(i):
            return pltpu.make_async_copy(done.at[i], out_ref.at[target_ref[i]], out_sems.at[i])

        for n in range(slots):
            fetch(n).start()
        key = lax.broadcasted_iota(jnp.int32, (rand * blk, blk), 0)

        def step(r, carry):
            first = r * heads
            for n in range(heads * rand):
                fetch(first * rand + n).wait()
            at = pl.ds(pl.multiple_of(r * blk, blk), blk)
            each = range(heads)
            keys = [
                buffer[pl.ds((first + e) * rand, rand), :, :hd].reshape(rand * blk, hd) for e in each
            ]
            scores = [dot_t(keys[e], q_ref[at, e * hd : (e + 1) * hd]) for e in each]
            scores = [
                jnp.where(key < count_ref[first + e] * blk, scores[e] * factor, NEG) for e in each
            ]
            top0 = [stat_ref[first + e, 0:1] for e in each]
            total0 = [stat_ref[first + e, 1:2] for e in each]
            top = [jnp.maximum(jnp.max(scores[e], axis=0, keepdims=True), top0[e]) for e in each]
            keep = [jnp.exp2(top0[e] - top[e]) for e in each]
            expo = [jnp.exp2(scores[e] - top[e]) for e in each]
            total = [total0[e] * keep[e] + jnp.sum(expo[e], axis=0, keepdims=True) for e in each]
            values = [
                jnp.concatenate([buffer[(first + e) * rand + j, :, hd:] for j in range(rand)], axis=1)
                for e in each
            ]
            summed = [acc_ref[first + e] * keep[e] + dot(values[e], expo[e].astype(BF)) for e in each]
            for e in each:
                done[first + e] = (summed[e] / total[e]).T.astype(BF)
            for e in each:
                deliver(first + e).start()
            return carry

        lax.fori_loop(0, rows, step, 0)
        for i in range(items):
            deliver(i).wait()

    vmem = pl.BlockSpec(memory_space=pltpu.VMEM)
    anywhere = pl.BlockSpec(memory_space=pl.ANY)
    return pl.pallas_call(
        kernel,
        out_shape=pltpu.HBM((peers, blk, hd), BF),
        grid_spec=pltpu.PrefetchScalarGridSpec(
            num_scalar_prefetch=3,
            grid=(1,),
            in_specs=[vmem, vmem, vmem, anywhere],
            out_specs=pl.BlockSpec(memory_space=pltpu.HBM),
            scratch_shapes=[
                pltpu.VMEM((slots, blk, 2 * hd), BF),
                pltpu.VMEM((items, blk, hd), BF),
                pltpu.SemaphoreType.DMA((slots,)),
                pltpu.SemaphoreType.DMA((items,)),
            ],
        ),
        compiler_params=params(),
        name="rand_attend",
    )(slot, count, target, query, acc, stat, tiles)


def local(tokens, w_qkv, item_at, rand_cols, rand_used):
    peers = lax.axis_size("seq")
    me = lax.axis_index("seq")
    groups = lax.axis_size("head")
    mine_y = lax.axis_index("head")
    heads, nblocks, rand = rand_cols.shape
    rows = nblocks // peers
    count, depth = tokens.shape
    blk = count // rows
    hd = w_qkv.shape[1] // (3 * heads)
    width = heads * hd
    items = heads * rows
    factor = math.log2(math.e) / math.sqrt(hd)

    asked = rand_cols.reshape(heads, peers, rows, rand).transpose(1, 2, 0, 3)
    asked = asked.reshape(peers, items * rand)
    order = jnp.arange(items * rand, dtype=jnp.int32)
    head_of = (order // rand) % heads
    code = order * items + head_of * rows + asked % rows
    mine = asked // rows == me
    low = jnp.min(jnp.where(mine, code, jnp.int32(1 << 30)), axis=1) % items
    high = jnp.max(jnp.where(mine, code, 0), axis=1) % items
    send_tile = jnp.stack([low, high], axis=1).reshape(-1)
    wanted = lax.dynamic_index_in_dim(asked, me, 0, keepdims=False)
    source = wanted // rows
    again = jnp.sum(
        ((source[:, None] == source[None, :]) & (order[None, :] < order[:, None])).astype(jnp.int32),
        axis=1,
    )
    slot = source * 2 + again
    my_used = lax.dynamic_slice_in_dim(rand_used, me * rows, rows, axis=1).T.reshape(-1)
    number = jnp.arange(items, dtype=jnp.int32)
    my_item = (number % heads) * nblocks + me * rows + number // heads
    place = jnp.arange(peers * items, dtype=jnp.int32)
    target = jnp.sum(
        jnp.where(item_at[0][None, :] == my_item[:, None], place[None, :] // items, 0), axis=1
    )
    home = (lax.dynamic_slice_in_dim(item_at[0], me * items, items) % nblocks) // rows
    edges = jnp.stack([me == 0, me == peers - 1]).astype(jnp.int32)

    def weight(shift, first, size):
        row = (mine_y + shift) % groups * depth
        return lax.dynamic_slice(w_qkv, (row, jnp.int32(first)), (depth, size))

    def w_pair(shift):
        return weight(shift, width, 2 * width)

    def w_query(shift):
        return weight(shift, 0, width)

    def spread(block, stride):
        holders = range(0, peers, 4 * stride)
        got = [
            lax.ppermute(block, "seq", [(h, h + k * stride) for h in holders]) for k in (1, 2, 3)
        ]
        return block + got[0] + got[1] + got[2]

    onward = [(i, (i + 1) % groups) for i in range(groups)]
    backward = [(b, a) for a, b in onward]
    across = [(i, (i + 2) % groups) for i in range(groups)]
    middle = count // 2
    from_low = lax.ppermute(tokens, "head", onward)
    from_high = lax.ppermute(tokens, "head", backward)
    zero = tokens[:blk]
    zero = jnp.where(me == 0, zero, jnp.zeros_like(zero))
    zero = spread(spread(spread(zero, peers // 4), peers // 16), peers // 64)
    far_top = lax.ppermute(from_low[:middle], "head", onward)
    far_bottom = lax.ppermute(from_high[middle:], "head", backward)
    own, from_low = lax.optimization_barrier((tokens, from_low))
    total = dot(own, w_pair(0)) + dot(from_low, w_pair(3)) + dot(from_high, w_pair(1))
    top = (total[:middle] + dot(far_top, w_pair(2))).astype(BF)
    bottom = (total[middle:] + dot(far_bottom, w_pair(2))).astype(BF)
    up = [(i, i + 1) for i in range(peers - 1)]
    down = [(b, a) for a, b in up]
    before = lax.ppermute(bottom[-blk:], "seq", up)
    after = lax.ppermute(top[:blk], "seq", down)
    sent = pack_tiles(send_tile, (top, bottom), 2 * peers, rows, heads, blk, hd)
    sent, before, after, far_top, far_bottom, zero = lax.optimization_barrier(
        (sent, before, after, far_top, far_bottom, zero)
    )
    tiles = lax.all_to_all(sent, "seq", split_axis=0, concat_axis=0, tiled=True)

    zero_low = lax.ppermute(zero, "head", onward)
    zero_high = lax.ppermute(zero, "head", backward)
    zero_far = lax.ppermute(zero, "head", across)
    around = jnp.concatenate([before, top, bottom, after], axis=0)
    far = jnp.concatenate([far_top, far_bottom], axis=0)
    query = dot(far, w_query(2)) + dot(tokens, w_query(0))
    query = (query + dot(from_low, w_query(3)) + dot(from_high, w_query(1))).astype(BF)
    first = dot(zero, w_pair(0)) + dot(zero_low, w_pair(3))
    first = (first + dot(zero_high, w_pair(1)) + dot(zero_far, w_pair(2))).astype(BF)
    acc, stat = near_attend(edges, query, around, first, rows, heads, blk, hd, factor)
    done = rand_attend(
        slot, my_used, target, query, tiles, acc, stat, rows, heads, blk, hd, rand, peers, factor
    )
    back = lax.all_to_all(done, "seq", split_axis=0, concat_axis=0, tiled=True)
    return take_tiles(home, back)[None]


def solution(mesh):
    return jax.shard_map(
        local,
        mesh=mesh,
        in_specs=(
            P("seq", "head"),
            P(None, "head"),
            P("head", None),
            P("head", None, None),
            P("head", None),
        ),
        out_specs=P("head", "seq", None, None),
        check_vma=False,
    )
```

```python
import math

import jax
import jax.numpy as jnp
from jax import lax
from jax.experimental import pallas as pl
from jax.experimental.pallas import tpu as pltpu
from jax.sharding import PartitionSpec as P

NEG = -1e30
BF = jnp.bfloat16
F32 = jnp.float32
VMEM_BYTES = 48 << 20


def dot(a, b):
    return jnp.dot(a, b, preferred_element_type=F32)


def dot_t(a, b):
    return lax.dot_general(a, b, (((1,), (1,)), ((), ())), preferred_element_type=F32)


def params():
    return pltpu.CompilerParams(vmem_limit_bytes=VMEM_BYTES)


def pack_tiles(index, halves, slots, rows, heads, blk, hd):
    width = heads * hd

    def kernel(index_ref, top_ref, bottom_ref, out_ref, tiles, sems):
        def copy(s):
            return pltpu.make_async_copy(tiles.at[index_ref[s]], out_ref.at[s], sems.at[s])

        for e in range(heads):
            for r in range(rows):
                pair_ref, place = (top_ref, r) if r < rows // 2 else (bottom_ref, r - rows // 2)
                at = slice(place * blk, (place + 1) * blk)
                tiles[e * rows + r, :, :hd] = pair_ref[at, e * hd : (e + 1) * hd]
                tiles[e * rows + r, :, hd:] = pair_ref[at, width + e * hd : width + (e + 1) * hd].T
        for s in range(slots):
            copy(s).start()
        for s in range(slots):
            copy(s).wait()

    return pl.pallas_call(
        kernel,
        out_shape=jax.ShapeDtypeStruct((slots, blk, 2 * hd), BF),
        grid_spec=pltpu.PrefetchScalarGridSpec(
            num_scalar_prefetch=1,
            grid=(1,),
            in_specs=[pl.BlockSpec(memory_space=pltpu.VMEM)] * 2,
            out_specs=pl.BlockSpec(memory_space=pl.ANY),
            scratch_shapes=[
                pltpu.VMEM((rows * heads, blk, 2 * hd), BF),
                pltpu.SemaphoreType.DMA((slots,)),
            ],
        ),
        compiler_params=params(),
        name="pack_tiles",
    )(index, *halves)


def take_tiles(index, tiles):
    count = index.shape[0]

    def kernel(index_ref, in_ref, out_ref, sems):
        def copy(i):
            return pltpu.make_async_copy(in_ref.at[index_ref[i]], out_ref.at[i], sems.at[i])

        for i in range(count):
            copy(i).start()
        for i in range(count):
            copy(i).wait()

    return pl.pallas_call(
        kernel,
        out_shape=jax.ShapeDtypeStruct((count, *tiles.shape[1:]), tiles.dtype),
        grid_spec=pltpu.PrefetchScalarGridSpec(
            num_scalar_prefetch=1,
            grid=(1,),
            in_specs=[pl.BlockSpec(memory_space=pltpu.VMEM)],
            out_specs=pl.BlockSpec(memory_space=pl.ANY),
            scratch_shapes=[pltpu.SemaphoreType.DMA((count,))],
        ),
        compiler_params=params(),
        name="take_tiles",
    )(index, tiles)


def near_attend(edges, query, around, first, rows, heads, blk, hd, factor):
    width = heads * hd

    def kernel(edge_ref, q_ref, kv_ref, first_ref, acc_ref, stat_ref):
        r = pl.program_id(0)
        window = pl.ds(pl.multiple_of(r * blk, blk), 3 * blk)
        key = lax.broadcasted_iota(jnp.int32, (3 * blk, blk), 0)
        low = jnp.where((r == 0) & (edge_ref[0] == 1), blk, 0)
        high = jnp.where((r == rows - 1) & (edge_ref[1] == 1), 2 * blk, 3 * blk)
        usable = (key >= low) & (key < high)
        row = lax.broadcasted_iota(jnp.int32, (8, blk), 0)
        for e in range(heads):
            keys = slice(e * hd, (e + 1) * hd)
            values = slice(width + e * hd, width + (e + 1) * hd)
            q = q_ref[:, keys]
            near = jnp.where(usable, dot_t(kv_ref[window, keys], q) * factor, NEG)
            glob = dot_t(first_ref[:, keys], q) * factor
            top = jnp.maximum(
                jnp.max(near, axis=0, keepdims=True), jnp.max(glob, axis=0, keepdims=True)
            )
            near = jnp.exp2(near - top)
            glob = jnp.exp2(glob - top)
            total = jnp.sum(near, axis=0, keepdims=True) + jnp.sum(glob, axis=0, keepdims=True)
            acc_ref[e] = dot(kv_ref[window, values].T, near.astype(BF)) + dot(
                first_ref[:, values].T, glob.astype(BF)
            )
            stat_ref[e] = jnp.where(row == 0, top, total)

    return pl.pallas_call(
        kernel,
        out_shape=(
            jax.ShapeDtypeStruct((rows * heads, hd, blk), F32),
            jax.ShapeDtypeStruct((rows * heads, 8, blk), F32),
        ),
        grid_spec=pltpu.PrefetchScalarGridSpec(
            num_scalar_prefetch=1,
            grid=(rows,),
            in_specs=[
                pl.BlockSpec((blk, width), lambda r, s: (r, 0)),
                pl.BlockSpec(around.shape, lambda r, s: (0, 0)),
                pl.BlockSpec(first.shape, lambda r, s: (0, 0)),
            ],
            out_specs=(
                pl.BlockSpec((heads, hd, blk), lambda r, s: (r, 0, 0)),
                pl.BlockSpec((heads, 8, blk), lambda r, s: (r, 0, 0)),
            ),
        ),
        compiler_params=params(),
        name="near_attend",
    )(edges, query, around, first)


def rand_attend(slot, count, target, query, tiles, acc, stat, rows, heads, blk, hd, rand, peers, factor):
    items = rows * heads
    slots = items * rand

    def kernel(
        slot_ref, count_ref, target_ref, q_ref, acc_ref, stat_ref, tiles_ref, out_ref,
        buffer, done, in_sems, out_sems,
    ):
        def fetch(n):
            return pltpu.make_async_copy(tiles_ref.at[slot_ref[n]], buffer.at[n], in_sems.at[n])

        def deliver(i):
            return pltpu.make_async_copy(done.at[i], out_ref.at[target_ref[i]], out_sems.at[i])

        for n in range(slots):
            fetch(n).start()
        key = lax.broadcasted_iota(jnp.int32, (rand * blk, blk), 0)

        def step(r, carry):
            first = r * heads
            for n in range(heads * rand):
                fetch(first * rand + n).wait()
            at = pl.ds(pl.multiple_of(r * blk, blk), blk)
            each = range(heads)
            keys = [
                buffer[pl.ds((first + e) * rand, rand), :, :hd].reshape(rand * blk, hd) for e in each
            ]
            scores = [dot_t(keys[e], q_ref[at, e * hd : (e + 1) * hd]) for e in each]
            scores = [
                jnp.where(key < count_ref[first + e] * blk, scores[e] * factor, NEG) for e in each
            ]
            top0 = [stat_ref[first + e, 0:1] for e in each]
            total0 = [stat_ref[first + e, 1:2] for e in each]
            top = [jnp.maximum(jnp.max(scores[e], axis=0, keepdims=True), top0[e]) for e in each]
            keep = [jnp.exp2(top0[e] - top[e]) for e in each]
            expo = [jnp.exp2(scores[e] - top[e]) for e in each]
            total = [total0[e] * keep[e] + jnp.sum(expo[e], axis=0, keepdims=True) for e in each]
            values = [
                jnp.concatenate([buffer[(first + e) * rand + j, :, hd:] for j in range(rand)], axis=1)
                for e in each
            ]
            summed = [acc_ref[first + e] * keep[e] + dot(values[e], expo[e].astype(BF)) for e in each]
            for e in each:
                done[first + e] = (summed[e] * (1.0 / total[e])).T.astype(BF)
            for e in each:
                deliver(first + e).start()
            return carry

        lax.fori_loop(0, rows, step, 0)
        for i in range(items):
            deliver(i).wait()

    vmem = pl.BlockSpec(memory_space=pltpu.VMEM)
    anywhere = pl.BlockSpec(memory_space=pl.ANY)
    return pl.pallas_call(
        kernel,
        out_shape=pltpu.HBM((peers, blk, hd), BF),
        grid_spec=pltpu.PrefetchScalarGridSpec(
            num_scalar_prefetch=3,
            grid=(1,),
            in_specs=[vmem, vmem, vmem, anywhere],
            out_specs=pl.BlockSpec(memory_space=pltpu.HBM),
            scratch_shapes=[
                pltpu.VMEM((slots, blk, 2 * hd), BF),
                pltpu.VMEM((items, blk, hd), BF),
                pltpu.SemaphoreType.DMA((slots,)),
                pltpu.SemaphoreType.DMA((items,)),
            ],
        ),
        compiler_params=params(),
        name="rand_attend",
    )(slot, count, target, query, acc, stat, tiles)


def local(tokens, w_qkv, item_at, rand_cols, rand_used):
    peers = lax.axis_size("seq")
    me = lax.axis_index("seq")
    groups = lax.axis_size("head")
    mine_y = lax.axis_index("head")
    heads, nblocks, rand = rand_cols.shape
    rows = nblocks // peers
    count, depth = tokens.shape
    blk = count // rows
    hd = w_qkv.shape[1] // (3 * heads)
    width = heads * hd
    items = heads * rows
    factor = math.log2(math.e) / math.sqrt(hd)

    asked = rand_cols.reshape(heads, peers, rows, rand).transpose(1, 2, 0, 3)
    asked = asked.reshape(peers, items * rand)
    order = jnp.arange(items * rand, dtype=jnp.int32)
    head_of = (order // rand) % heads
    code = order * items + head_of * rows + asked % rows
    mine = asked // rows == me
    low = jnp.min(jnp.where(mine, code, jnp.int32(1 << 30)), axis=1) % items
    high = jnp.max(jnp.where(mine, code, 0), axis=1) % items
    send_tile = jnp.stack([low, high], axis=1).reshape(-1)
    wanted = lax.dynamic_index_in_dim(asked, me, 0, keepdims=False)
    source = wanted // rows
    again = jnp.sum(
        ((source[:, None] == source[None, :]) & (order[None, :] < order[:, None])).astype(jnp.int32),
        axis=1,
    )
    slot = source * 2 + again
    my_used = lax.dynamic_slice_in_dim(rand_used, me * rows, rows, axis=1).T.reshape(-1)
    number = jnp.arange(items, dtype=jnp.int32)
    my_item = (number % heads) * nblocks + me * rows + number // heads
    place = jnp.arange(peers * items, dtype=jnp.int32)
    target = jnp.sum(
        jnp.where(item_at[0][None, :] == my_item[:, None], place[None, :] // items, 0), axis=1
    )
    home = (lax.dynamic_slice_in_dim(item_at[0], me * items, items) % nblocks) // rows
    edges = jnp.stack([me == 0, me == peers - 1]).astype(jnp.int32)

    def weight(shift, first, size):
        row = (mine_y + shift) % groups * depth
        return lax.dynamic_slice(w_qkv, (row, jnp.int32(first)), (depth, size))

    def w_pair(shift):
        return weight(shift, width, 2 * width)

    def w_query(shift):
        return weight(shift, 0, width)

    def spread_parts(block, stride):
        holders = range(0, peers, 4 * stride)
        return [
            lax.ppermute(block, "seq", [(h, h + k * stride) for h in holders]) for k in (1, 2, 3)
        ]

    def spread(block, stride):
        return sum(spread_parts(block, stride), block)

    onward = [(i, (i + 1) % groups) for i in range(groups)]
    backward = [(b, a) for a, b in onward]
    across = [(i, (i + 2) % groups) for i in range(groups)]
    middle = count // 2
    from_low = lax.ppermute(tokens, "head", onward)
    from_high = lax.ppermute(tokens, "head", backward)
    zero = tokens[:blk]
    zero = jnp.where(me == 0, zero, jnp.zeros_like(zero))
    zero = spread(spread(zero, peers // 4), peers // 16)
    zero = [zero, *spread_parts(zero, peers // 64)]
    far_top = lax.ppermute(from_low[:middle], "head", onward)
    far_bottom = lax.ppermute(from_high[middle:], "head", backward)
    own, from_low = lax.optimization_barrier((tokens, from_low))
    total = dot(own, w_pair(0)) + dot(from_low, w_pair(3)) + dot(from_high, w_pair(1))
    top = (total[:middle] + dot(far_top, w_pair(2))).astype(BF)
    bottom = (total[middle:] + dot(far_bottom, w_pair(2))).astype(BF)
    up = [(i, i + 1) for i in range(peers - 1)]
    down = [(b, a) for a, b in up]
    before = lax.ppermute(bottom[-blk:], "seq", up)
    after = lax.ppermute(top[:blk], "seq", down)
    sent = pack_tiles(send_tile, (top, bottom), 2 * peers, rows, heads, blk, hd)
    sent, before, after, far_top, far_bottom, zero = lax.optimization_barrier(
        (sent, before, after, far_top, far_bottom, zero)
    )
    tiles = lax.all_to_all(sent, "seq", split_axis=0, concat_axis=0, tiled=True)

    zero = sum(zero[1:], zero[0])
    zero_low = lax.ppermute(zero, "head", onward)
    zero_high = lax.ppermute(zero, "head", backward)
    zero_far = lax.ppermute(zero, "head", across)
    around = jnp.concatenate([before, top, bottom, after], axis=0)
    far = jnp.concatenate([far_top, far_bottom], axis=0)
    query = dot(far, w_query(2)) + dot(tokens, w_query(0))
    query = (query + dot(from_low, w_query(3)) + dot(from_high, w_query(1))).astype(BF)
    first = dot(zero, w_pair(0)) + dot(zero_low, w_pair(3))
    first = (first + dot(zero_high, w_pair(1)) + dot(zero_far, w_pair(2))).astype(BF)
    acc, stat = near_attend(edges, query, around, first, rows, heads, blk, hd, factor)
    done = rand_attend(
        slot, my_used, target, query, tiles, acc, stat, rows, heads, blk, hd, rand, peers, factor
    )
    back = lax.all_to_all(done, "seq", split_axis=0, concat_axis=0, tiled=True)
    return take_tiles(home, back)[None]


def solution(mesh):
    return jax.shard_map(
        local,
        mesh=mesh,
        in_specs=(
            P("seq", "head"),
            P(None, "head"),
            P("head", None),
            P("head", None, None),
            P("head", None),
        ),
        out_specs=P("head", "seq", None, None),
        check_vma=False,
    )
```
